128 devices in a mesh: shard: 32 (over y, z, core), rep: 4 (over x).
Axes of the slice: x: 4, y: 4, z: 4, core: 2. Of those that a mesh axis runs over, the one named last changes fastest.
Arguments:
- feats: bfloat16 [32768, 768], P('shard'), may hold values from -6 to 6
- bases: bfloat16 [4, 768, 1024], P(None, None, 'rep'), may hold values from -0.21875 to 0.21875
- coef: bfloat16 [5, 4], replicated, may hold values from -2 to 2
- root_weight: bfloat16 [768, 1024], P(None, 'rep'), may hold values from -0.21875 to 0.21875
- slot_block: int32 [32, 32, 2], P('shard'), may hold values from 0 to 7
- recv_rel: int32 [32, 32, 2], P('shard'), may hold values from 0 to 4
- tile_slot: int32 [32, 256], P('shard'), may hold values from 0 to 63, as said below
- tile_dst: int32 [32, 256], P('shard'), may hold values from 0 to 7
- tile_adj: bfloat16 [32, 256, 128, 128], P('shard'), may hold values from 0 to 0.049804688
- d_out: bfloat16 [32768, 1024], P('shard', 'rep'), may hold values from -6 to 6
Outputs:
- output: bfloat16 [32768, 1024], P('shard', 'rep')
- grad_feats: bfloat16 [32768, 768], P(('shard', 'rep'))
- grad_bases: float32 [4, 768, 1024], P(None, 'shard', 'rep')
- grad_root: float32 [768, 1024], P('shard', 'rep')
- grad_coef: float32 [5, 4], replicated
The draws below stay inside these ranges and needn't reach their ends.
Inputs may be any that keep to these rules, and one draw needn't show every extreme that they name: `tile_slot`: in each row (one destination device) every one of the 64 slots is named by at least one tile.
All inputs are finite; a program needn't handle non-finite values.
Results may differ from the reference program's by a relative error of at most 0.0062.
Values may be sent and summed in bfloat16 or wider, within the bound.
No kernel may reach another device: no remote copies, remote signals or barrier semaphores. Data moves between devices by JAX's collectives and lax.ppermute only.
A program may use at most 192 MiB of HBM per device.

```python
import jax
import jax.numpy as jnp
from jax import lax

DIN = 768
DOUT = 1024
NREL = 5
NBASE = 4
BLK = 128
CAP = 2
NBLK_DEV = 8
TILES = 256
NODES = 32768
N_SHARD = 32
N_REP = 4


def draw_tile_slot(key, part):
    slots = N_SHARD * CAP
    first_key, second_key = jax.random.split(key)
    extra = jax.random.randint(first_key, (N_SHARD, TILES), 0, slots)
    position = jnp.broadcast_to(jnp.arange(TILES, dtype=jnp.int32)[None, :], (N_SHARD, TILES))
    listed = jnp.where(position < slots, position, extra).astype(jnp.int32)
    scores = jax.random.randint(second_key, (N_SHARD, TILES), 0, 1048576) * TILES + position
    order = jnp.argsort(scores, axis=1, stable=True)
    return jnp.take_along_axis(listed, order, 1).astype(jnp.int32)


def set_ends(entries, rng, least, high):
    dims = entries.shape
    index_at = [jax.random.randint(jax.random.fold_in(rng, axis), (), 0, dims[axis]) for axis in range(len(dims))]
    entries = entries.at[tuple(index_at)].set(least)
    longest = dims.index(max(dims))
    index_at[longest] = (index_at[longest] + 1) % dims[longest]
    return entries.at[tuple(index_at)].set(high)


def steps_of(rng, shape, pieces, least, top_value):
    level = 1.0
    for dim, shards_of in pieces:
        heights = jax.random.uniform(jax.random.fold_in(jax.random.fold_in(rng, 6), dim), (shards_of,), jnp.float32, least / len(pieces), top_value / len(pieces))
        level = level * jnp.repeat(jnp.exp(heights), shape[dim] // shards_of).reshape((-1,) + (1,) * (len(shape) - 1 - dim))
    return level


def bell_draw(rng, shape, scale, reach, pieces=(), kind=jnp.bfloat16):
    values = scale * jax.random.normal(rng, shape, jnp.float32)
    if pieces:
        values = values * steps_of(rng, shape, pieces, -0.22, 0.18)
    return jnp.clip(values, -reach, reach).astype(kind)


def setup_inputs(seed: int = 0) -> dict:
    arg_keys = jax.random.split(jax.random.key(seed), 11)
    feats = bell_draw(arg_keys[0], (NODES, DIN), 1.0, 6.0, ((0, 32),))
    bases = bell_draw(arg_keys[1], (NBASE, DIN, DOUT), DIN ** -0.5, 0.21875, ((2, 4),))
    coef = bell_draw(arg_keys[2], (NREL, NBASE), 0.5, 2.0)
    root_weight = bell_draw(arg_keys[3], (DIN, DOUT), DIN ** -0.5, 0.21875, ((1, 4),))
    slot_block = set_ends(jax.random.randint(arg_keys[4], (N_SHARD, N_SHARD, CAP), 0, NBLK_DEV), jax.random.fold_in(arg_keys[4], 1), 0, NBLK_DEV - 1).astype(jnp.int32)
    recv_rel = set_ends(jax.random.randint(arg_keys[5], (N_SHARD, N_SHARD, CAP), 0, NREL), jax.random.fold_in(arg_keys[5], 1), 0, NREL - 1).astype(jnp.int32)
    tile_slot = draw_tile_slot(jax.random.fold_in(arg_keys[10], 71), 0)
    tile_dst = set_ends(jax.random.randint(arg_keys[7], (N_SHARD, TILES), 0, NBLK_DEV), jax.random.fold_in(arg_keys[7], 1), 0, NBLK_DEV - 1).astype(jnp.int32)
    tile_adj = jnp.clip(0.049804688 * jax.random.uniform(arg_keys[8], (N_SHARD, TILES, BLK, BLK), jnp.float32) ** steps_of(arg_keys[8], (N_SHARD, TILES, BLK, BLK), ((0, 32),), -0.2, 0.2), 0.0, 0.049804688).astype(jnp.bfloat16)
    d_out = bell_draw(arg_keys[9], (NODES, DOUT), 1.0, 6.0, ((0, 32), (1, 4)))
    return dict(feats=feats, bases=bases, coef=coef, root_weight=root_weight, slot_block=slot_block, recv_rel=recv_rel, tile_slot=tile_slot, tile_dst=tile_dst, tile_adj=tile_adj, d_out=d_out)


def reference(feats, bases, coef, root_weight, slot_block, recv_rel, tile_slot, tile_dst, tile_adj, d_out):
    highest = lax.Precision.HIGHEST
    wide = jnp.float32
    narrow = jnp.bfloat16
    blocks_all = N_SHARD * NBLK_DEV
    rows_all = blocks_all * BLK
    slot_count = N_SHARD * CAP
    width = DOUT // N_REP
    rel_weights = jnp.dot(coef, bases.reshape(NBASE, -1), preferred_element_type=wide).astype(narrow).reshape(NREL, DIN, DOUT)
    slot_owner = (jnp.arange(slot_count, dtype=jnp.int32) // CAP).astype(jnp.int32)
    slot_src = (slot_owner[None, :] * NBLK_DEV + jnp.transpose(slot_block, (1, 0, 2)).reshape(N_SHARD, slot_count)).astype(jnp.int32)
    slot_rel = recv_rel.reshape(N_SHARD, slot_count).astype(jnp.int32)
    group_key = (slot_rel * blocks_all + slot_src).reshape(-1).astype(jnp.int32)
    feats_wide = feats.astype(wide)
    dest_range = jnp.arange(N_SHARD, dtype=jnp.int32)
    outs_list = []
    feat_grad = jnp.zeros((rows_all, DIN), wide)
    rel_grads = []
    root_grads = []
    for group in range(N_REP):
        weights = rel_weights[:, :, group * width:(group + 1) * width].astype(wide)
        root_part = root_weight[:, group * width:(group + 1) * width]
        grad_part = d_out[:, group * width:(group + 1) * width]
        projected = jnp.einsum("nc,rco->rno", feats_wide, weights, precision=highest)
        projected = lax.optimization_barrier(projected.astype(narrow))
        projected = projected.reshape(NREL, blocks_all, BLK, width)
        grad_blocks = grad_part.reshape(blocks_all, BLK, width)

        def one_dest(dest):
            adj_here = tile_adj[dest].astype(wide)
            slots_here = tile_slot[dest]
            targets = tile_dst[dest]
            slot_msgs = projected[slot_rel[dest], slot_src[dest]]
            tile_msgs = slot_msgs[slots_here].astype(wide)
            weighted = jnp.einsum("tij,tjo->tio", adj_here, tile_msgs, precision=highest)
            dst_onehot = (targets[:, None] == jnp.arange(NBLK_DEV, dtype=jnp.int32)[None, :]).astype(wide)
            agg = jnp.einsum("tb,tio->bio", dst_onehot, weighted, precision=highest)
            local_grads = lax.dynamic_slice_in_dim(grad_blocks, dest * NBLK_DEV, NBLK_DEV, 0)
            tile_grads = jnp.einsum("tji,tjo->tio", adj_here, local_grads[targets].astype(wide), precision=highest)
            slot_onehot = (slots_here[:, None] == jnp.arange(slot_count, dtype=jnp.int32)[None, :]).astype(wide)
            gslot = jnp.einsum("ts,tio->sio", slot_onehot, tile_grads, precision=highest)
            return agg, gslot.astype(narrow)

        agg_all, gslot_all = lax.map(one_dest, dest_range)
        gslot_wide = lax.optimization_barrier(gslot_all).astype(wide).reshape(-1, BLK, width)
        gsrc = jax.ops.segment_sum(gslot_wide, group_key, num_segments=NREL * blocks_all)
        gsrc = lax.optimization_barrier(gsrc.astype(narrow)).astype(wide).reshape(NREL, rows_all, width)
        out_part = agg_all.reshape(rows_all, width) + jnp.dot(feats, root_part, preferred_element_type=wide)
        outs_list.append(out_part)
        feat_grad = feat_grad + jnp.einsum("rno,rco->nc", gsrc, weights, precision=highest)
        feat_grad = feat_grad + jnp.dot(grad_part, root_part.T, preferred_element_type=wide)
        rel_grads.append(jnp.einsum("nc,rno->rco", feats_wide, gsrc, precision=highest))
        root_grads.append(jnp.dot(feats.T, grad_part, preferred_element_type=wide))
    output = jnp.concatenate(outs_list, axis=1).astype(narrow)
    grad_feats = feat_grad.astype(narrow)
    grad_rel = jnp.concatenate(rel_grads, axis=2)
    grad_root = jnp.concatenate(root_grads, axis=1)
    grad_bases = jnp.einsum("rb,rio->bio", coef.astype(wide), grad_rel, precision=highest)
    grad_coef = jnp.einsum("rio,bio->rb", grad_rel, bases.astype(wide), precision=highest)
    return (output, grad_feats, grad_bases, grad_root, grad_coef)
```

```python
import jax
import jax.numpy as jnp
from jax import lax
from jax.experimental import pallas as pl
from jax.experimental.pallas import tpu as pltpu
from jax.sharding import PartitionSpec as P

BLK = 128
F32 = jnp.float32
BF16 = jnp.bfloat16
VMEM_LIMIT = 48 * 1024 * 1024


def params():
    return pltpu.CompilerParams(vmem_limit_bytes=VMEM_LIMIT)


def whole(shape):
    return pl.BlockSpec(shape, lambda *_: (0,) * len(shape))


def tile_grads(tile_ids, dest_ids, adjacency, grads, slots, chunk=16):
    tiles = adjacency.shape[0]
    nblocks, _, width = grads.shape

    def kernel(slot_ref, dst_ref, adj_ref, grad_ref, out_ref, acc_ref):
        step = pl.program_id(0)

        @pl.when(step == 0)
        def _():
            acc_ref[...] = jnp.zeros_like(acc_ref)

        for u in range(chunk):
            t = step * chunk + u
            part = lax.dot_general(
                adj_ref[u],
                grad_ref[dst_ref[t]],
                (((0,), (0,)), ((), ())),
                preferred_element_type=F32,
            )
            acc_ref[slot_ref[t]] += part

        @pl.when(step == pl.num_programs(0) - 1)
        def _():
            out_ref[...] = acc_ref[...].astype(BF16)

    return pl.pallas_call(
        kernel,
        name="tile_grads",
        out_shape=jax.ShapeDtypeStruct((slots, BLK, width), BF16),
        grid_spec=pltpu.PrefetchScalarGridSpec(
            num_scalar_prefetch=2,
            grid=(tiles // chunk,),
            in_specs=[
                pl.BlockSpec((chunk, BLK, BLK), lambda i, *_: (i, 0, 0)),
                whole(grads.shape),
            ],
            out_specs=whole((slots, BLK, width)),
            scratch_shapes=[pltpu.VMEM((slots, BLK, width), F32)],
        ),
        compiler_params=params(),
    )(tile_ids, dest_ids, adjacency, grads)


def tile_sums(tile_ids, dest_ids, adjacency, msgs, root_term, chunk=16):
    tiles = adjacency.shape[0]
    nblocks, _, width = root_term.shape

    def kernel(slot_ref, dst_ref, adj_ref, msg_ref, root_ref, out_ref, acc_ref):
        step = pl.program_id(0)

        @pl.when(step == 0)
        def _():
            acc_ref[...] = root_ref[...]

        for u in range(chunk):
            t = step * chunk + u
            acc_ref[dst_ref[t]] += jnp.dot(
                adj_ref[u], msg_ref[slot_ref[t]], preferred_element_type=F32
            )

        @pl.when(step == pl.num_programs(0) - 1)
        def _():
            out_ref[...] = acc_ref[...].astype(BF16)

    return pl.pallas_call(
        kernel,
        name="tile_sums",
        out_shape=jax.ShapeDtypeStruct(root_term.shape, BF16),
        grid_spec=pltpu.PrefetchScalarGridSpec(
            num_scalar_prefetch=2,
            grid=(tiles // chunk,),
            in_specs=[
                pl.BlockSpec((chunk, BLK, BLK), lambda i, *_: (i, 0, 0)),
                whole(msgs.shape),
                whole(root_term.shape),
            ],
            out_specs=whole(root_term.shape),
            scratch_shapes=[pltpu.VMEM(root_term.shape, F32)],
        ),
        compiler_params=params(),
    )(tile_ids, dest_ids, adjacency, msgs, root_term)


def project_select(keys, feats, rel_weights, nblocks):
    relations, _, width = rel_weights.shape
    slots = keys.shape[0]

    def kernel(key_ref, feat_ref, w_ref, out_ref, msg_ref):
        for r in range(relations):
            for b in range(nblocks):
                msg_ref[r * nblocks + b] = jnp.dot(
                    feat_ref[pl.ds(b * BLK, BLK), :], w_ref[r], preferred_element_type=F32
                ).astype(BF16)

        def copy(s, carry):
            out_ref[s] = msg_ref[key_ref[s]]
            return carry

        lax.fori_loop(0, slots, copy, 0)

    return pl.pallas_call(
        kernel,
        name="project_select",
        out_shape=jax.ShapeDtypeStruct((slots, BLK, width), BF16),
        grid_spec=pltpu.PrefetchScalarGridSpec(
            num_scalar_prefetch=1,
            grid=(1,),
            in_specs=[whole(feats.shape), whole(rel_weights.shape)],
            out_specs=whole((slots, BLK, width)),
            scratch_shapes=[pltpu.VMEM((relations * nblocks, BLK, width), BF16)],
        ),
        compiler_params=params(),
    )(keys, feats, rel_weights)


def sum_by_key(keys, returned, bins, chunk=8):
    slots, _, width = returned.shape

    def kernel(key_ref, ret_ref, out_ref, acc_ref):
        step = pl.program_id(0)

        @pl.when(step == 0)
        def _():
            acc_ref[...] = jnp.zeros_like(acc_ref)

        for u in range(chunk):
            acc_ref[key_ref[step * chunk + u]] += ret_ref[u].astype(F32)

        @pl.when(step == pl.num_programs(0) - 1)
        def _():
            out_ref[...] = acc_ref[...].astype(BF16)

    return pl.pallas_call(
        kernel,
        name="sum_by_key",
        out_shape=jax.ShapeDtypeStruct((bins, BLK, width), BF16),
        grid_spec=pltpu.PrefetchScalarGridSpec(
            num_scalar_prefetch=1,
            grid=(slots // chunk,),
            in_specs=[pl.BlockSpec((chunk, BLK, width), lambda i, *_: (i, 0, 0))],
            out_specs=whole((bins, BLK, width)),
            scratch_shapes=[pltpu.VMEM((bins, BLK, width), F32)],
        ),
        compiler_params=params(),
    )(keys, returned)


def exchange(x, axis, mask):
    return lax.ppermute(x, axis, [(i, i ^ mask) for i in range(lax.axis_size(axis))])


def scatter_sum(x, axis, shift, size, me):
    at = (me >> shift) & (size - 1)
    total = lax.dynamic_index_in_dim(x, at, 0, keepdims=False)
    for k in range(1, size):
        part = lax.dynamic_index_in_dim(x, at ^ k, 0, keepdims=False).astype(BF16)
        total = total + exchange(part, axis, k << shift).astype(F32)
    return total


def body(
    feats, bases, coef, root_weight, slot_block, recv_rel, tile_slot, tile_dst, tile_adj, d_out
):
    shards = lax.axis_size("shard")
    reps = lax.axis_size("rep")
    me = lax.axis_index("shard")
    my_rep = lax.axis_index("rep")
    nblocks = feats.shape[0] // BLK
    width_in = feats.shape[1]
    width = root_weight.shape[1]
    relations, nbase = coef.shape
    capacity = slot_block.shape[2]
    slots = shards * capacity

    slot_grads = tile_grads(
        tile_slot[0], tile_dst[0], tile_adj[0], d_out.reshape(nblocks, BLK, width), slots
    )
    returned = lax.all_to_all(
        slot_grads.reshape(shards, capacity * BLK, width), "shard", 0, 0, tiled=True
    )

    table = recv_rel.reshape(1, slots)
    step = 1
    while step < shards:
        table = jnp.concatenate([table, exchange(table, "shard", step)], axis=0)
        step *= 2
    mine = jnp.sum(
        jnp.where(
            jnp.arange(slots)[None, :, None]
            == (me * capacity + jnp.arange(capacity))[None, None, :],
            table[:, :, None],
            0,
        ),
        axis=1,
    )
    order = jnp.arange(shards)
    owner_rel = jnp.sum(
        jnp.where((order[:, None] ^ me) == order[None, :], 1, 0)[:, :, None] * mine[None], axis=1
    )
    keys = (owner_rel * nblocks + slot_block[0]).reshape(-1).astype(jnp.int32)

    rel_weights = (
        jnp.dot(coef, bases.reshape(nbase, -1), preferred_element_type=F32)
        .astype(BF16)
        .reshape(relations, width_in, width)
    )
    outgoing = project_select(keys, feats, rel_weights, nblocks)
    root_term = jnp.dot(feats, root_weight, preferred_element_type=F32)
    incoming = lax.all_to_all(
        outgoing.reshape(shards, capacity * BLK, width), "shard", 0, 0, tiled=True
    )

    source_grads = sum_by_key(keys, returned.reshape(slots, BLK, width), relations * nblocks)
    source_grads = source_grads.reshape(relations, nblocks * BLK, width)
    relation_grads = jnp.einsum("nc,rno->rco", feats, source_grads, preferred_element_type=F32)
    root_grad = jnp.dot(feats.T, d_out, preferred_element_type=F32)

    wide_coef = coef.astype(F32)
    partial_bases = [
        sum(wide_coef[r, b] * relation_grads[r] for r in range(relations)) for b in range(nbase)
    ]
    rows = width_in // shards
    stacked = jnp.concatenate(
        [g.reshape(shards, rows, width) for g in (*partial_bases, root_grad)], axis=1
    )
    part = scatter_sum(
        jnp.swapaxes(stacked.reshape(shards // 2, 2, -1, width), 0, 1), "shard", 0, 2, me
    )
    part = scatter_sum(part.reshape(4, shards // 8, -1, width), "shard", 3, 4, me)
    part = scatter_sum(part, "shard", 1, 4, me)
    reduced = part.reshape(nbase + 1, rows, width)
    grad_bases = reduced[:nbase]
    grad_root = reduced[nbase]

    grad_coef = jnp.sum(
        relation_grads[:, None] * bases.astype(F32)[None], axis=(2, 3)
    )
    for axis in ("shard", "rep"):
        step = 1
        while step < lax.axis_size(axis):
            grad_coef = grad_coef + exchange(grad_coef, axis, step)
            step *= 2

    through = jnp.einsum("rno,rco->nc", source_grads, rel_weights, preferred_element_type=F32)
    through = through + jnp.dot(d_out, root_weight.T, preferred_element_type=F32)
    grad_feats = scatter_sum(
        through.reshape(reps, -1, width_in), "rep", 0, reps, my_rep
    ).astype(BF16)

    output = tile_sums(
        tile_slot[0],
        tile_dst[0],
        tile_adj[0],
        incoming.reshape(slots, BLK, width),
        root_term.reshape(nblocks, BLK, width),
    ).reshape(nblocks * BLK, width)
    return (output, grad_feats, grad_bases, grad_root, grad_coef)


def solution(mesh):
    placed = (
        P("shard", None),
        P(None, None, "rep"),
        P(),
        P(None, "rep"),
        P("shard", None, None),
        P("shard", None, None),
        P("shard", None),
        P("shard", None),
        P("shard", None, None, None),
        P("shard", "rep"),
    )
    return jax.shard_map(
        body,
        mesh=mesh,
        in_specs=placed,
        out_specs=(
            P("shard", "rep"),
            P(("shard", "rep"), None),
            P(None, "shard", "rep"),
            P("shard", "rep"),
            P(),
        ),
        check_vma=False,
    )
```

```python
import jax
import jax.numpy as jnp
from jax import lax
from jax.experimental import pallas as pl
from jax.experimental.pallas import tpu as pltpu
from jax.sharding import PartitionSpec as P

BLK = 128
F32 = jnp.float32
BF16 = jnp.bfloat16
VMEM_LIMIT = 48 * 1024 * 1024


def params():
    return pltpu.CompilerParams(vmem_limit_bytes=VMEM_LIMIT)


def whole(shape):
    return pl.BlockSpec(shape, lambda *_: (0,) * len(shape))


def tile_grads(tile_ids, dest_ids, rels, adjacency, grads, shards, chunk=16):
    tiles = adjacency.shape[0]
    nblocks, _, width = grads.shape
    slots = rels.shape[0]
    capacity = slots // shards
    rows = capacity * BLK + 8

    def kernel(slot_ref, dst_ref, rel_ref, adj_ref, grad_ref, out_ref, acc_ref):
        step = pl.program_id(0)

        @pl.when(step == 0)
        def _():
            acc_ref[...] = jnp.zeros_like(acc_ref)

        for u in range(chunk):
            t = step * chunk + u
            part = lax.dot_general(
                adj_ref[u],
                grad_ref[dst_ref[t]],
                (((0,), (0,)), ((), ())),
                preferred_element_type=F32,
            )
            acc_ref[slot_ref[t]] += part

        @pl.when(step == pl.num_programs(0) - 1)
        def _():
            row = lax.broadcasted_iota(jnp.int32, (8, width), 0)
            for o in range(shards):
                tail = jnp.zeros((8, width), F32)
                for c in range(capacity):
                    s = o * capacity + c
                    out_ref[o, pl.ds(c * BLK, BLK), :] = acc_ref[s].astype(BF16)
                    tail = jnp.where(row == c, rel_ref[s].astype(F32), tail)
                out_ref[o, pl.ds(capacity * BLK, 8), :] = tail.astype(BF16)

    return pl.pallas_call(
        kernel,
        name="tile_grads",
        out_shape=jax.ShapeDtypeStruct((shards, rows, width), BF16),
        grid_spec=pltpu.PrefetchScalarGridSpec(
            num_scalar_prefetch=3,
            grid=(tiles // chunk,),
            in_specs=[
                pl.BlockSpec((chunk, BLK, BLK), lambda i, *_: (i, 0, 0)),
                whole(grads.shape),
            ],
            out_specs=whole((shards, rows, width)),
            scratch_shapes=[pltpu.VMEM((slots, BLK, width), F32)],
        ),
        compiler_params=params(),
    )(tile_ids, dest_ids, rels, adjacency, grads)


def dense_tiles(tile_ids, dest_ids, adjacency, slots, nblocks, chunk=16, halves=2):
    tiles = adjacency.shape[0]
    per = nblocks // halves

    def kernel(slot_ref, dst_ref, adj_ref, out_ref, acc_ref):
        half = pl.program_id(0)
        step = pl.program_id(1)

        @pl.when(step == 0)
        def _():
            acc_ref[...] = jnp.zeros_like(acc_ref)

        for u in range(chunk):
            t = step * chunk + u
            local = dst_ref[t] - half * per

            @pl.when((local >= 0) & (local < per))
            def _():
                acc_ref[local, slot_ref[t]] += adj_ref[u].astype(F32)

        @pl.when(step == pl.num_programs(1) - 1)
        def _():
            def store(s, carry):
                for b in range(per):
                    out_ref[pl.ds(b * BLK, BLK), pl.ds(pl.multiple_of(s * BLK, BLK), BLK)] = (
                        acc_ref[b, s].astype(BF16)
                    )
                return carry

            lax.fori_loop(0, slots, store, 0)

    return pl.pallas_call(
        kernel,
        name="dense_tiles",
        out_shape=jax.ShapeDtypeStruct((nblocks * BLK, slots * BLK), BF16),
        grid_spec=pltpu.PrefetchScalarGridSpec(
            num_scalar_prefetch=2,
            grid=(halves, tiles // chunk),
            in_specs=[pl.BlockSpec((chunk, BLK, BLK), lambda h, i, *_: (i, 0, 0))],
            out_specs=pl.BlockSpec((per * BLK, slots * BLK), lambda h, i, *_: (h, 0)),
            scratch_shapes=[pltpu.VMEM((per, slots, BLK, BLK), F32)],
        ),
        compiler_params=params(),
    )(tile_ids, dest_ids, adjacency)


def project(feats, rel_weights, nblocks):
    relations, _, width = rel_weights.shape

    def kernel(feat_ref, w_ref, out_ref):
        for b in range(nblocks):
            out_ref[b] = jnp.dot(
                feat_ref[pl.ds(b * BLK, BLK), :], w_ref[0], preferred_element_type=F32
            ).astype(BF16)

    return pl.pallas_call(
        kernel,
        name="project",
        out_shape=jax.ShapeDtypeStruct((relations * nblocks, BLK, width), BF16),
        grid=(relations,),
        in_specs=[
            whole(feats.shape),
            pl.BlockSpec((1,) + rel_weights.shape[1:], lambda r: (r, 0, 0)),
        ],
        out_specs=pl.BlockSpec((nblocks, BLK, width), lambda r: (r, 0, 0)),
        compiler_params=params(),
    )(feats, rel_weights)


def select_blocks(keys, blocks, chunk=16):
    slots = keys.shape[0]
    _, rows, width = blocks.shape

    def kernel(key_ref, in_ref, out_ref):
        step = pl.program_id(0)
        for u in range(chunk):
            out_ref[u] = in_ref[key_ref[step * chunk + u]]

    return pl.pallas_call(
        kernel,
        name="select_blocks",
        out_shape=jax.ShapeDtypeStruct((slots, rows, width), BF16),
        grid_spec=pltpu.PrefetchScalarGridSpec(
            num_scalar_prefetch=1,
            grid=(slots // chunk,),
            in_specs=[whole(blocks.shape)],
            out_specs=pl.BlockSpec((chunk, rows, width), lambda i, *_: (i, 0, 0)),
        ),
        compiler_params=params(),
    )(keys, blocks)


def sum_by_key(keys, returned, bins, capacity, chunk=4):
    shards, rows, width = returned.shape

    def kernel(key_ref, ret_ref, out_ref, acc_ref):
        step = pl.program_id(0)

        @pl.when(step == 0)
        def _():
            acc_ref[...] = jnp.zeros_like(acc_ref)

        for u in range(chunk):
            for c in range(capacity):
                key = key_ref[(step * chunk + u) * capacity + c]
                acc_ref[key] += ret_ref[u, pl.ds(c * BLK, BLK), :].astype(F32)

        @pl.when(step == pl.num_programs(0) - 1)
        def _():
            out_ref[...] = acc_ref[...].astype(BF16)

    return pl.pallas_call(
        kernel,
        name="sum_by_key",
        out_shape=jax.ShapeDtypeStruct((bins, BLK, width), BF16),
        grid_spec=pltpu.PrefetchScalarGridSpec(
            num_scalar_prefetch=1,
            grid=(shards // chunk,),
            in_specs=[pl.BlockSpec((chunk, rows, width), lambda i, *_: (i, 0, 0))],
            out_specs=whole((bins, BLK, width)),
            scratch_shapes=[pltpu.VMEM((bins, BLK, width), F32)],
        ),
        compiler_params=params(),
    )(keys, returned)


def weight_grads(coef, feats, source_grads, d_out, bases, chunk=128):
    relations, nodes, width = source_grads.shape
    nbase, width_in, _ = bases.shape

    def kernel(coef_ref, feat_ref, src_ref, grad_ref, base_ref, out_ref, dots_ref):
        @pl.when(pl.program_id(0) == 0)
        def _():
            dots_ref[...] = jnp.zeros_like(dots_ref)

        cols = feat_ref[...].T
        for r in range(relations):
            g = jnp.dot(cols, src_ref[r], preferred_element_type=F32)
            for b in range(nbase):
                scaled = coef_ref[r * nbase + b] * g
                if r == 0:
                    out_ref[b] = scaled
                else:
                    out_ref[b] += scaled
                prod = g * base_ref[b].astype(F32)
                dots_ref[r * nbase + b] += jnp.sum(prod.reshape(-1, 8, width), axis=0)
        out_ref[nbase] = jnp.dot(cols, grad_ref[...], preferred_element_type=F32)

    return pl.pallas_call(
        kernel,
        name="weight_grads",
        out_shape=(
            jax.ShapeDtypeStruct((nbase + 1, width_in, width), F32),
            jax.ShapeDtypeStruct((relations * nbase, 8, width), F32),
        ),
        grid_spec=pltpu.PrefetchScalarGridSpec(
            num_scalar_prefetch=1,
            grid=(width_in // chunk,),
            in_specs=[
                pl.BlockSpec((nodes, chunk), lambda i, *_: (0, i)),
                whole(source_grads.shape),
                whole(d_out.shape),
                pl.BlockSpec((nbase, chunk, width), lambda i, *_: (0, i, 0)),
            ],
            out_specs=(
                pl.BlockSpec((nbase + 1, chunk, width), lambda i, *_: (0, i, 0)),
                whole((relations * nbase, 8, width)),
            ),
        ),
        compiler_params=params(),
    )(coef, feats, source_grads, d_out, bases)


def exchange(x, axis, mask):
    return lax.ppermute(x, axis, [(i, i ^ mask) for i in range(lax.axis_size(axis))])


def chunk_of(x, at, dim):
    return lax.dynamic_index_in_dim(x, at, dim, keepdims=False)


def scatter_sum(x, axis, shift, size, me, dim=0):
    at = (me >> shift) & (size - 1)
    total = chunk_of(x, at, dim)
    for k in range(1, size):
        part = chunk_of(x, at ^ k, dim).astype(BF16)
        total = total + exchange(part, axis, k << shift).astype(F32)
    return total


def scatter_sum_with(x, extra, axis, shift, size, me, dim):
    at = (me >> shift) & (size - 1)
    total = chunk_of(x, at, dim)
    width = x.shape[-1]
    count = extra.shape[0]
    high = lax.reduce_precision(extra, 8, 7)
    low = lax.reduce_precision(extra - high, 8, 7)
    line = jnp.concatenate([high, low, jnp.zeros((width - 2 * count,), F32)])
    lines = jnp.where(jnp.arange(8)[:, None] == 0, line[None], 0.0).astype(BF16)
    sums = [high + low]
    for k in range(1, size):
        part = chunk_of(x, at ^ k, dim).astype(BF16)
        sent = jnp.concatenate([part.reshape(-1, width), lines], axis=0)
        got = exchange(sent, axis, k << shift)
        total = total + got[:-8].reshape(part.shape).astype(F32)
        last = got[-8].astype(F32)
        sums.append(last[:count] + last[count : 2 * count])
    while len(sums) > 1:
        sums = [sums[i] + sums[i + 1] for i in range(0, len(sums), 2)]
    return total, sums[0]


def body(
    feats, bases, coef, root_weight, slot_block, recv_rel, tile_slot, tile_dst, tile_adj, d_out
):
    shards = lax.axis_size("shard")
    reps = lax.axis_size("rep")
    me = lax.axis_index("shard")
    my_rep = lax.axis_index("rep")
    nblocks = feats.shape[0] // BLK
    width_in = feats.shape[1]
    width = root_weight.shape[1]
    relations, nbase = coef.shape
    capacity = slot_block.shape[2]
    slots = shards * capacity

    slot_grads = tile_grads(
        tile_slot[0],
        tile_dst[0],
        recv_rel.reshape(slots),
        tile_adj[0],
        d_out.reshape(nblocks, BLK, width),
        shards,
    )
    returned = lax.all_to_all(slot_grads, "shard", 0, 0, tiled=True)

    rel_weights = (
        jnp.dot(coef, bases.reshape(nbase, -1), preferred_element_type=F32)
        .astype(BF16)
        .reshape(relations, width_in, width)
    )
    projected = project(feats, rel_weights, nblocks)
    root_term = jnp.dot(feats, root_weight, preferred_element_type=F32)
    dense = dense_tiles(tile_slot[0], tile_dst[0], tile_adj[0], slots, nblocks)

    owner_rel = returned[:, capacity * BLK : capacity * BLK + capacity, 0].astype(jnp.int32)
    keys = (owner_rel * nblocks + slot_block[0]).reshape(-1)
    outgoing = select_blocks(keys, projected)
    incoming = lax.all_to_all(
        outgoing.reshape(shards, capacity * BLK, width), "shard", 0, 0, tiled=True
    )

    source_grads = sum_by_key(keys, returned, relations * nblocks, capacity)
    source_grads = source_grads.reshape(relations, nblocks * BLK, width)
    stacked, dots = weight_grads(
        coef.astype(F32).reshape(-1), feats, source_grads, d_out, bases
    )
    dots = jnp.sum(dots, axis=(1, 2))
    dots = dots + exchange(dots, "shard", 1)
    for step in (1, 2):
        dots = dots + exchange(dots, "rep", step)

    rows = width_in // shards
    part = scatter_sum(
        stacked.reshape(nbase + 1, shards // 2, 2, rows, width), "shard", 0, 2, me, dim=2
    )
    part = part.reshape(nbase + 1, 4, shards // 8, rows, width)
    part, dots = scatter_sum_with(part, dots, "shard", 3, 4, me, dim=1)
    reduced, dots = scatter_sum_with(part, dots, "shard", 1, 4, me, dim=1)
    grad_bases = reduced[:nbase]
    grad_root = reduced[nbase]
    grad_coef = dots.reshape(relations, nbase)

    through = jnp.einsum("rno,rco->nc", source_grads, rel_weights, preferred_element_type=F32)
    through = through + jnp.dot(d_out, root_weight.T, preferred_element_type=F32)
    grad_feats = scatter_sum(
        through.reshape(reps, -1, width_in), "rep", 0, reps, my_rep
    ).astype(BF16)

    output = (
        jnp.dot(dense, incoming.reshape(slots * BLK, width), preferred_element_type=F32)
        + root_term
    ).astype(BF16)
    return (output, grad_feats, grad_bases, grad_root, grad_coef)


def solution(mesh):
    placed = (
        P("shard", None),
        P(None, None, "rep"),
        P(),
        P(None, "rep"),
        P("shard", None, None),
        P("shard", None, None),
        P("shard", None),
        P("shard", None),
        P("shard", None, None, None),
        P("shard", "rep"),
    )
    return jax.shard_map(
        body,
        mesh=mesh,
        in_specs=placed,
        out_specs=(
            P("shard", "rep"),
            P(("shard", "rep"), None),
            P(None, "shard", "rep"),
            P("shard", "rep"),
            P(),
        ),
        check_vma=False,
    )
```

```python
import jax
import jax.numpy as jnp
from jax import lax
from jax.experimental import pallas as pl
from jax.experimental.pallas import tpu as pltpu
from jax.sharding import PartitionSpec as P

BLK = 128
F32 = jnp.float32
BF16 = jnp.bfloat16
VMEM_LIMIT = 48 * 1024 * 1024


def params():
    return pltpu.CompilerParams(vmem_limit_bytes=VMEM_LIMIT)


def whole(shape):
    return pl.BlockSpec(shape, lambda *_: (0,) * len(shape))


def tile_grads(tile_ids, dest_ids, rels, adjacency, grads, shards, chunk=16):
    tiles = adjacency.shape[0]
    nblocks, _, width = grads.shape
    slots = rels.shape[0]
    capacity = slots // shards
    rows = capacity * BLK + 8

    def kernel(slot_ref, dst_ref, rel_ref, adj_ref, grad_ref, out_ref, acc_ref):
        step = pl.program_id(0)

        @pl.when(step == 0)
        def _():
            acc_ref[...] = jnp.zeros_like(acc_ref)

        for u in range(chunk):
            t = step * chunk + u
            part = lax.dot_general(
                adj_ref[u],
                grad_ref[dst_ref[t]],
                (((0,), (0,)), ((), ())),
                preferred_element_type=F32,
            )
            acc_ref[slot_ref[t]] += part

        @pl.when(step == pl.num_programs(0) - 1)
        def _():
            lane = lax.broadcasted_iota(jnp.int32, (8, width), 1)
            for o in range(shards):
                tail = jnp.zeros((8, width), F32)
                for c in range(capacity):
                    s = o * capacity + c
                    out_ref[o, pl.ds(c * BLK, BLK), :] = acc_ref[s].astype(BF16)
                    tail = jnp.where(lane // BLK == c, rel_ref[s].astype(F32), tail)
                out_ref[o, pl.ds(capacity * BLK, 8), :] = tail.astype(BF16)

    return pl.pallas_call(
        kernel,
        name="tile_grads",
        out_shape=pltpu.HBM((shards, rows, width), BF16),
        grid_spec=pltpu.PrefetchScalarGridSpec(
            num_scalar_prefetch=3,
            grid=(tiles // chunk,),
            in_specs=[
                pl.BlockSpec((chunk, BLK, BLK), lambda i, *_: (i, 0, 0)),
                whole(grads.shape),
            ],
            out_specs=whole((shards, rows, width)),
            scratch_shapes=[pltpu.VMEM((slots, BLK, width), F32)],
        ),
        compiler_params=params(),
    )(tile_ids, dest_ids, rels, adjacency, grads)


def dense_tiles(tile_ids, dest_ids, adjacency, slots, nblocks, chunk=16, halves=2):
    tiles = adjacency.shape[0]
    per = nblocks // halves

    def kernel(slot_ref, dst_ref, adj_ref, out_ref, acc_ref):
        half = pl.program_id(0)
        step = pl.program_id(1)

        @pl.when(step == 0)
        def _():
            acc_ref[...] = jnp.zeros_like(acc_ref)

        for u in range(chunk):
            t = step * chunk + u
            local = dst_ref[t] - half * per

            @pl.when((local >= 0) & (local < per))
            def _():
                acc_ref[local, slot_ref[t]] += adj_ref[u].astype(F32)

        @pl.when(step == pl.num_programs(1) - 1)
        def _():
            def store(s, carry):
                for b in range(per):
                    out_ref[pl.ds(b * BLK, BLK), pl.ds(pl.multiple_of(s * BLK, BLK), BLK)] = (
                        acc_ref[b, s].astype(BF16)
                    )
                return carry

            lax.fori_loop(0, slots, store, 0)

    return pl.pallas_call(
        kernel,
        name="dense_tiles",
        out_shape=jax.ShapeDtypeStruct((nblocks * BLK, slots * BLK), BF16),
        grid_spec=pltpu.PrefetchScalarGridSpec(
            num_scalar_prefetch=2,
            grid=(halves, tiles // chunk),
            in_specs=[pl.BlockSpec((chunk, BLK, BLK), lambda h, i, *_: (i, 0, 0))],
            out_specs=pl.BlockSpec((per * BLK, slots * BLK), lambda h, i, *_: (h, 0)),
            scratch_shapes=[pltpu.VMEM((per, slots, BLK, BLK), F32)],
        ),
        compiler_params=params(),
    )(tile_ids, dest_ids, adjacency)


def project(feats, rel_weights, nblocks):
    relations, _, width = rel_weights.shape

    def kernel(feat_ref, w_ref, out_ref):
        for b in range(nblocks):
            out_ref[b] = jnp.dot(
                feat_ref[pl.ds(b * BLK, BLK), :], w_ref[0], preferred_element_type=F32
            ).astype(BF16)

    return pl.pallas_call(
        kernel,
        name="project",
        out_shape=jax.ShapeDtypeStruct((relations * nblocks, BLK, width), BF16),
        grid=(relations,),
        in_specs=[
            whole(feats.shape),
            pl.BlockSpec((1,) + rel_weights.shape[1:], lambda r: (r, 0, 0)),
        ],
        out_specs=pl.BlockSpec((nblocks, BLK, width), lambda r: (r, 0, 0)),
        compiler_params=params(),
    )(feats, rel_weights)


def select_blocks(slot_block, returned, blocks, nblocks, capacity, chunk=4):
    shards, rows, width = returned.shape
    relations = blocks.shape[0] // nblocks

    def kernel(block_ref, rel_ref, in_ref, out_ref):
        step = pl.program_id(0)
        for u in range(chunk):
            for c in range(capacity):
                block = block_ref[(step * chunk + u) * capacity + c]
                rel = rel_ref[u, pl.ds(0, 1), pl.ds(c * BLK, BLK)].astype(F32)
                rel = jnp.broadcast_to(rel, (BLK, BLK))
                for j in range(width // BLK):
                    cols = pl.ds(j * BLK, BLK)
                    value = in_ref[block, :, cols].astype(F32)
                    for r in range(1, relations):
                        value = jnp.where(
                            rel == r, in_ref[r * nblocks + block, :, cols].astype(F32), value
                        )
                    out_ref[u, pl.ds(c * BLK, BLK), cols] = value.astype(BF16)

    return pl.pallas_call(
        kernel,
        name="select_blocks",
        out_shape=jax.ShapeDtypeStruct((shards, capacity * BLK, width), BF16),
        grid_spec=pltpu.PrefetchScalarGridSpec(
            num_scalar_prefetch=1,
            grid=(shards // chunk,),
            in_specs=[
                pl.BlockSpec((chunk, 8, width), lambda i, *_: (i, capacity * BLK // 8, 0)),
                whole(blocks.shape),
            ],
            out_specs=pl.BlockSpec((chunk, capacity * BLK, width), lambda i, *_: (i, 0, 0)),
        ),
        compiler_params=params(),
    )(slot_block, returned, blocks)


def add_product(base, left, right, first, steps, out_type, depth=1024):
    nodes, width = base.shape
    rows = right.shape[1]
    per = depth // rows

    def kernel(base_ref, left_ref, right_ref, out_ref, acc_ref):
        step = pl.program_id(0)

        @pl.when(step == 0)
        def _():
            acc_ref[...] = base_ref[...]

        acc_ref[...] += jnp.dot(
            left_ref[...], right_ref[...].reshape(depth, width), preferred_element_type=F32
        )

        @pl.when(step == steps - 1)
        def _():
            out_ref[...] = acc_ref[...].astype(out_type)

    return pl.pallas_call(
        kernel,
        name="add_product",
        out_shape=jax.ShapeDtypeStruct((nodes, width), out_type),
        grid=(steps,),
        in_specs=[
            whole(base.shape),
            pl.BlockSpec((nodes, depth), lambda i: (0, first + i)),
            pl.BlockSpec((per, rows, width), lambda i: (first + i, 0, 0)),
        ],
        out_specs=whole((nodes, width)),
        scratch_shapes=[pltpu.VMEM((nodes, width), F32)],
        compiler_params=params(),
    )(base, left, right)


def sum_by_key(keys, returned, bins, capacity, chunk=4):
    shards, rows, width = returned.shape

    def kernel(key_ref, ret_ref, out_ref, acc_ref):
        step = pl.program_id(0)

        @pl.when(step == 0)
        def _():
            acc_ref[...] = jnp.zeros_like(acc_ref)

        for u in range(chunk):
            for c in range(capacity):
                key = key_ref[(step * chunk + u) * capacity + c]
                acc_ref[key] += ret_ref[u, pl.ds(c * BLK, BLK), :].astype(F32)

        @pl.when(step == pl.num_programs(0) - 1)
        def _():
            out_ref[...] = acc_ref[...].astype(BF16)

    return pl.pallas_call(
        kernel,
        name="sum_by_key",
        out_shape=jax.ShapeDtypeStruct((bins, BLK, width), BF16),
        grid_spec=pltpu.PrefetchScalarGridSpec(
            num_scalar_prefetch=1,
            grid=(shards // chunk,),
            in_specs=[pl.BlockSpec((chunk, rows, width), lambda i, *_: (i, 0, 0))],
            out_specs=whole((bins, BLK, width)),
            scratch_shapes=[pltpu.VMEM((bins, BLK, width), F32)],
        ),
        compiler_params=params(),
    )(keys, returned)


def weight_grads(coef, feats, source_grads, d_out, bases, chunk=128):
    relations, nodes, width = source_grads.shape
    nbase, width_in, _ = bases.shape

    def kernel(coef_ref, feat_ref, src_ref, grad_ref, base_ref, out_ref, dots_ref, acc_ref):
        @pl.when(pl.program_id(0) == 0)
        def _():
            acc_ref[...] = jnp.zeros_like(acc_ref)

        cols = feat_ref[...].T
        for r in range(relations):
            g = jnp.dot(cols, src_ref[r], preferred_element_type=F32)
            for b in range(nbase):
                scaled = coef_ref[r * nbase + b] * g
                if r == 0:
                    out_ref[b] = scaled
                else:
                    out_ref[b] += scaled
                prod = g * base_ref[b].astype(F32)
                acc_ref[r * nbase + b] += jnp.sum(prod.reshape(-1, 8, width), axis=0)
        out_ref[nbase] = jnp.dot(cols, grad_ref[...], preferred_element_type=F32)

        @pl.when(pl.program_id(0) == pl.num_programs(0) - 1)
        def _():
            row = lax.broadcasted_iota(jnp.int32, (8, BLK), 0)
            lane = lax.broadcasted_iota(jnp.int32, (8, BLK), 1)
            tile = jnp.zeros((8, BLK), F32)
            for r in range(relations):
                for b in range(nbase):
                    total = jnp.sum(acc_ref[r * nbase + b])
                    tile = jnp.where((row == r) & (lane == b), total, tile)
            dots_ref[...] = tile

    return pl.pallas_call(
        kernel,
        name="weight_grads",
        out_shape=(
            jax.ShapeDtypeStruct((nbase + 1, width_in, width), F32),
            jax.ShapeDtypeStruct((8, BLK), F32),
        ),
        grid_spec=pltpu.PrefetchScalarGridSpec(
            num_scalar_prefetch=1,
            grid=(width_in // chunk,),
            in_specs=[
                pl.BlockSpec((nodes, chunk), lambda i, *_: (0, i)),
                whole(source_grads.shape),
                whole(d_out.shape),
                pl.BlockSpec((nbase, chunk, width), lambda i, *_: (0, i, 0)),
            ],
            out_specs=(
                pl.BlockSpec((nbase + 1, chunk, width), lambda i, *_: (0, i, 0)),
                whole((8, BLK)),
            ),
            scratch_shapes=[pltpu.VMEM((relations * nbase, 8, width), F32)],
        ),
        compiler_params=params(),
    )(coef, feats, source_grads, d_out, bases)


def exchange(x, axis, mask):
    return lax.ppermute(x, axis, [(i, i ^ mask) for i in range(lax.axis_size(axis))])


def chunk_of(x, at, dim):
    return lax.dynamic_index_in_dim(x, at, dim, keepdims=False)


def scatter_sum(x, axis, shift, size, me, dim=0):
    at = (me >> shift) & (size - 1)
    total = chunk_of(x, at, dim)
    for k in range(1, size):
        part = chunk_of(x, at ^ k, dim).astype(BF16)
        total = total + exchange(part, axis, k << shift).astype(F32)
    return total


def two_terms(x):
    high = x.astype(BF16)
    low = (x - high.astype(F32)).astype(BF16)
    return high, low


def sum_terms(x):
    return x[:, :BLK].astype(F32) + x[:, BLK:].astype(F32)


def first_stage(place, stacked, got, dots, size):
    parts, _, rest, _, rows, width = stacked.shape
    length = parts * rest * rows

    def kernel(place_ref, own_ref, got_ref, dots_ref, keep_ref, *send_refs):
        core = place_ref[0]
        at = place_ref[1]
        high, low = two_terms(dots_ref[...])
        for k in range(size):
            for p in range(parts):
                for q in range(rest):
                    value = own_ref[p, at ^ k, q, core] + got_ref[p, at ^ k, q].astype(F32)
                    if k == 0:
                        keep_ref[p, q] = value
                    else:
                        send_refs[k - 1][pl.ds((p * rest + q) * rows, rows), :] = value.astype(BF16)
            if k:
                send_refs[k - 1][pl.ds(length, 8), pl.ds(0, BLK)] = high
                send_refs[k - 1][pl.ds(length, 8), pl.ds(BLK, BLK)] = low

    sent = (length + 8, width)
    return pl.pallas_call(
        kernel,
        name="first_stage",
        out_shape=(jax.ShapeDtypeStruct((parts, rest, rows, width), F32),)
        + (jax.ShapeDtypeStruct(sent, BF16),) * (size - 1),
        grid_spec=pltpu.PrefetchScalarGridSpec(
            num_scalar_prefetch=1,
            grid=(1,),
            in_specs=[whole(stacked.shape), whole(got.shape), whole(dots.shape)],
            out_specs=(whole((parts, rest, rows, width)),) + (whole(sent),) * (size - 1),
        ),
        compiler_params=params(),
    )(place, stacked, got, dots)


def second_stage(place, kept, dots, got, size):
    parts, _, rows, width = kept.shape
    length = parts * rows

    def kernel(place_ref, own_ref, dots_ref, *refs):
        gots = refs[: len(got)]
        keep_ref, all_ref = refs[len(got) : len(got) + 2]
        send_refs = refs[len(got) + 2 :]
        at = place_ref[2]
        high, low = two_terms(dots_ref[...])
        sums = [high.astype(F32) + low.astype(F32)]
        sums += [sum_terms(g[pl.ds(length * size, 8), :]) for g in gots]
        while len(sums) > 1:
            sums = [sums[i] + sums[i + 1] for i in range(0, len(sums), 2)]
        all_ref[...] = sums[0]
        high, low = two_terms(sums[0])
        for k in range(size):
            for p in range(parts):
                value = own_ref[p, at ^ k]
                start = pl.multiple_of((p * size + (at ^ k)) * rows, 8)
                for g in gots:
                    value = value + g[pl.ds(start, rows), :].astype(F32)
                if k == 0:
                    keep_ref[p] = value
                else:
                    send_refs[k - 1][pl.ds(p * rows, rows), :] = value.astype(BF16)
            if k:
                send_refs[k - 1][pl.ds(length, 8), pl.ds(0, BLK)] = high
                send_refs[k - 1][pl.ds(length, 8), pl.ds(BLK, BLK)] = low

    sent = (length + 8, width)
    return pl.pallas_call(
        kernel,
        name="second_stage",
        out_shape=(
            jax.ShapeDtypeStruct((parts, rows, width), F32),
            jax.ShapeDtypeStruct((8, BLK), F32),
        )
        + (jax.ShapeDtypeStruct(sent, BF16),) * (size - 1),
        grid_spec=pltpu.PrefetchScalarGridSpec(
            num_scalar_prefetch=1,
            grid=(1,),
            in_specs=[whole(kept.shape), whole(dots.shape)] + [whole(g.shape) for g in got],
            out_specs=(whole((parts, rows, width)), whole((8, BLK))) + (whole(sent),) * (size - 1),
        ),
        compiler_params=params(),
    )(place, kept, dots, *got)


def last_stage(kept, dots, got, relations):
    parts, rows, width = kept.shape
    length = parts * rows
    nbase = parts - 1

    def kernel(own_ref, dots_ref, *refs):
        gots = refs[: len(got)]
        bases_ref, root_ref, coef_ref = refs[len(got) :]
        high, low = two_terms(dots_ref[...])
        sums = [high.astype(F32) + low.astype(F32)]
        sums += [sum_terms(g[pl.ds(length, 8), :]) for g in gots]
        while len(sums) > 1:
            sums = [sums[i] + sums[i + 1] for i in range(0, len(sums), 2)]
        coef_ref[...] = sums[0][:relations, :nbase]
        for p in range(parts):
            value = own_ref[p]
            for g in gots:
                value = value + g[pl.ds(p * rows, rows), :].astype(F32)
            if p < nbase:
                bases_ref[p] = value
            else:
                root_ref[...] = value

    shapes = ((nbase, rows, width), (rows, width), (relations, nbase))
    return pl.pallas_call(
        kernel,
        name="last_stage",
        out_shape=tuple(jax.ShapeDtypeStruct(x, F32) for x in shapes),
        grid=(1,),
        in_specs=[whole(kept.shape), whole(dots.shape)] + [whole(g.shape) for g in got],
        out_specs=tuple(whole(x) for x in shapes),
        compiler_params=params(),
    )(kept, dots, *got)


def body(
    feats, bases, coef, root_weight, slot_block, recv_rel, tile_slot, tile_dst, tile_adj, d_out
):
    shards = lax.axis_size("shard")
    reps = lax.axis_size("rep")
    me = lax.axis_index("shard")
    my_rep = lax.axis_index("rep")
    nblocks = feats.shape[0] // BLK
    width_in = feats.shape[1]
    width = root_weight.shape[1]
    relations, nbase = coef.shape
    capacity = slot_block.shape[2]
    slots = shards * capacity

    slot_grads = tile_grads(
        tile_slot[0],
        tile_dst[0],
        recv_rel.reshape(slots),
        tile_adj[0],
        d_out.reshape(nblocks, BLK, width),
        shards,
    )
    returned = lax.all_to_all(slot_grads, "shard", 0, 0, tiled=True)

    rel_weights = (
        jnp.dot(coef, bases.reshape(nbase, -1), preferred_element_type=F32)
        .astype(BF16)
        .reshape(relations, width_in, width)
    )
    projected = project(feats, rel_weights, nblocks)
    root_term = jnp.dot(feats, root_weight, preferred_element_type=F32)
    dense = dense_tiles(tile_slot[0], tile_dst[0], tile_adj[0], slots, nblocks)

    returned, dense = lax.optimization_barrier((returned, dense))
    outgoing = select_blocks(slot_block.reshape(slots), returned, projected, nblocks, capacity)
    outgoing, returned = lax.optimization_barrier((outgoing, returned))
    incoming = lax.all_to_all(outgoing, "shard", 0, 0, tiled=True)

    owner_rel = returned[:, capacity * BLK, :: BLK][:, :capacity].astype(jnp.int32)
    keys = (owner_rel * nblocks + slot_block[0]).reshape(-1)
    source_grads = sum_by_key(keys, returned, relations * nblocks, capacity)
    source_grads = source_grads.reshape(relations, nblocks * BLK, width)
    stacked, dots = weight_grads(
        coef.astype(F32).reshape(-1), feats, source_grads, d_out, bases
    )
    dots = dots + exchange(dots, "shard", 1)
    for step in (1, 2):
        dots = dots + exchange(dots, "rep", step)

    through = jnp.einsum("rno,rco->nc", source_grads, rel_weights, preferred_element_type=F32)
    through = through + jnp.dot(d_out, root_weight.T, preferred_element_type=F32)
    grad_feats = scatter_sum(
        through.reshape(reps, -1, width_in), "rep", 0, reps, my_rep
    ).astype(BF16)

    rows = width_in // shards
    stacked = stacked.reshape(nbase + 1, 4, 4, 2, rows, width)
    place = jnp.stack([me & 1, (me >> 3) & 3, (me >> 1) & 3]).astype(jnp.int32)
    got = exchange(chunk_of(stacked, (me & 1) ^ 1, 3).astype(BF16), "shard", 1)
    kept, *sends = first_stage(place, stacked, got, dots, 4)
    grad_feats, *sends = lax.optimization_barrier((grad_feats, *sends))
    got = [exchange(x, "shard", k << 3) for k, x in zip((1, 2, 3), sends)]
    total_steps = slots * BLK // 1024
    early = total_steps // 2
    partial = add_product(root_term, dense, incoming, 0, early, F32)
    partial, kept = lax.optimization_barrier((partial, kept))
    kept, dots, *sends = second_stage(place, kept, dots, got, 4)
    got = [exchange(x, "shard", k << 1) for k, x in zip((1, 2, 3), sends)]
    partial, kept = lax.optimization_barrier((partial, kept))
    output = add_product(partial, dense, incoming, early, total_steps - early, BF16)
    grad_bases, grad_root, grad_coef = last_stage(kept, dots, got, relations)
    return (output, grad_feats, grad_bases, grad_root, grad_coef)


def solution(mesh):
    placed = (
        P("shard", None),
        P(None, None, "rep"),
        P(),
        P(None, "rep"),
        P("shard", None, None),
        P("shard", None, None),
        P("shard", None),
        P("shard", None),
        P("shard", None, None, None),
        P("shard", "rep"),
    )
    return jax.shard_map(
        body,
        mesh=mesh,
        in_specs=placed,
        out_specs=(
            P("shard", "rep"),
            P(("shard", "rep"), None),
            P(None, "shard", "rep"),
            P("shard", "rep"),
            P(),
        ),
        check_vma=False,
    )
```

```python
import jax
import jax.numpy as jnp
from jax import lax
from jax.experimental import pallas as pl
from jax.experimental.pallas import tpu as pltpu
from jax.sharding import PartitionSpec as P

BLK = 128
F32 = jnp.float32
BF16 = jnp.bfloat16
VMEM_LIMIT = 48 * 1024 * 1024


def params():
    return pltpu.CompilerParams(vmem_limit_bytes=VMEM_LIMIT)


def whole(shape):
    return pl.BlockSpec(shape, lambda *_: (0,) * len(shape))


def tile_grads(tile_ids, dest_ids, rels, adjacency, grads, shards, chunk=64):
    tiles = adjacency.shape[0]
    nblocks, _, width = grads.shape
    capacity = rels.shape[0]
    slots = shards * capacity
    rows = capacity * BLK + 8

    def kernel(slot_ref, dst_ref, rel_ref, adj_ref, grad_ref, out_ref, acc_ref):
        step = pl.program_id(0)

        @pl.when(step == 0)
        def _():
            acc_ref[...] = jnp.zeros_like(acc_ref)

        for u in range(chunk):
            t = step * chunk + u
            part = lax.dot_general(
                adj_ref[u],
                grad_ref[dst_ref[t]],
                (((0,), (0,)), ((), ())),
                preferred_element_type=F32,
            )
            acc_ref[slot_ref[t]] += part

        @pl.when(step == pl.num_programs(0) - 1)
        def _():
            lane = lax.broadcasted_iota(jnp.int32, (8, width), 1)
            for o in range(shards):
                tail = jnp.zeros((8, width), F32)
                for c in range(capacity):
                    s = o * capacity + c
                    out_ref[o, pl.ds(c * BLK, BLK), :] = acc_ref[s].astype(BF16)
                    tail = jnp.where(lane // BLK == c, rel_ref[c, o].astype(F32), tail)
                out_ref[o, pl.ds(capacity * BLK, 8), :] = tail.astype(BF16)

    return pl.pallas_call(
        kernel,
        name="tile_grads",
        out_shape=pltpu.HBM((shards, rows, width), BF16),
        grid_spec=pltpu.PrefetchScalarGridSpec(
            num_scalar_prefetch=3,
            grid=(tiles // chunk,),
            in_specs=[
                pl.BlockSpec((chunk, BLK, BLK), lambda i, *_: (i, 0, 0)),
                whole(grads.shape),
            ],
            out_specs=whole((shards, rows, width)),
            scratch_shapes=[pltpu.VMEM((slots, BLK, width), F32)],
        ),
        compiler_params=params(),
    )(tile_ids, dest_ids, rels, adjacency, grads)


def project(feats, rel_weights, nblocks):
    relations, _, width = rel_weights.shape

    def kernel(feat_ref, w_ref, out_ref):
        for b in range(nblocks):
            out_ref[b] = jnp.dot(
                feat_ref[pl.ds(b * BLK, BLK), :], w_ref[0], preferred_element_type=F32
            ).astype(BF16)

    return pl.pallas_call(
        kernel,
        name="project",
        out_shape=jax.ShapeDtypeStruct((relations * nblocks, BLK, width), BF16),
        grid=(relations,),
        in_specs=[
            whole(feats.shape),
            pl.BlockSpec((1,) + rel_weights.shape[1:], lambda r: (r, 0, 0)),
        ],
        out_specs=pl.BlockSpec((nblocks, BLK, width), lambda r: (r, 0, 0)),
        compiler_params=params(),
    )(feats, rel_weights)


def tile_sums(tile_ids, dest_ids, adjacency, msgs, root_term, chunk=64):
    tiles = adjacency.shape[0]

    def kernel(slot_ref, dst_ref, adj_ref, msg_ref, root_ref, out_ref, acc_ref):
        step = pl.program_id(0)

        @pl.when(step == 0)
        def _():
            acc_ref[...] = root_ref[...]

        for u in range(chunk):
            t = step * chunk + u
            acc_ref[dst_ref[t]] += jnp.dot(
                adj_ref[u], msg_ref[slot_ref[t]], preferred_element_type=F32
            )

        @pl.when(step == pl.num_programs(0) - 1)
        def _():
            out_ref[...] = acc_ref[...].astype(BF16)

    return pl.pallas_call(
        kernel,
        name="tile_sums",
        out_shape=jax.ShapeDtypeStruct(root_term.shape, BF16),
        grid_spec=pltpu.PrefetchScalarGridSpec(
            num_scalar_prefetch=2,
            grid=(tiles // chunk,),
            in_specs=[
                pl.BlockSpec((chunk, BLK, BLK), lambda i, *_: (i, 0, 0)),
                whole(msgs.shape),
                whole(root_term.shape),
            ],
            out_specs=whole(root_term.shape),
            scratch_shapes=[pltpu.VMEM(root_term.shape, F32)],
        ),
        compiler_params=params(),
    )(tile_ids, dest_ids, adjacency, msgs, root_term)


def relation_of(ref, c):
    return jnp.max(ref[:, c * BLK : (c + 1) * BLK].astype(F32)).astype(jnp.int32)


def select_blocks(slot_block, returned, blocks, nblocks, capacity):
    shards, _, width = returned.shape

    def kernel(block_ref, rel_ref, in_ref, out_ref, sem_ref):
        copies = []
        for o in range(shards):
            for c in range(capacity):
                key = relation_of(rel_ref[o], c) * nblocks + block_ref[c, o]
                copy = pltpu.make_async_copy(
                    in_ref.at[key], out_ref.at[o, pl.ds(c * BLK, BLK)], sem_ref.at[o, c]
                )
                copy.start()
                copies.append(copy)
        for copy in copies:
            copy.wait()

    return pl.pallas_call(
        kernel,
        name="select_blocks",
        out_shape=pltpu.HBM((shards, capacity * BLK, width), BF16),
        grid_spec=pltpu.PrefetchScalarGridSpec(
            num_scalar_prefetch=1,
            grid=(1,),
            in_specs=[
                pl.BlockSpec((shards, 8, width), lambda i, *_: (0, capacity * BLK // 8, 0)),
                whole(blocks.shape),
            ],
            out_specs=pl.BlockSpec(memory_space=pl.ANY),
            scratch_shapes=[pltpu.SemaphoreType.DMA((shards, capacity))],
        ),
        compiler_params=params(),
    )(slot_block, returned, blocks)


def sum_by_key(slot_block, returned, relations, nblocks, chunk=8):
    shards, rows, width = returned.shape
    capacity = slot_block.shape[0]
    bins = relations * nblocks

    def kernel(block_ref, ret_ref, out_ref, acc_ref):
        step = pl.program_id(0)

        @pl.when(step == 0)
        def _():
            acc_ref[...] = jnp.zeros_like(acc_ref)

        for u in range(chunk):
            for c in range(capacity):
                rel = relation_of(ret_ref[u, pl.ds(capacity * BLK, 8), :], c)
                key = rel * nblocks + block_ref[c, step * chunk + u]
                acc_ref[key] += ret_ref[u, pl.ds(c * BLK, BLK), :].astype(F32)

        @pl.when(step == pl.num_programs(0) - 1)
        def _():
            out_ref[...] = acc_ref[...].astype(BF16)

    return pl.pallas_call(
        kernel,
        name="sum_by_key",
        out_shape=pltpu.HBM((bins, BLK, width), BF16),
        grid_spec=pltpu.PrefetchScalarGridSpec(
            num_scalar_prefetch=1,
            grid=(shards // chunk,),
            in_specs=[pl.BlockSpec((chunk, rows, width), lambda i, *_: (i, 0, 0))],
            out_specs=whole((bins, BLK, width)),
            scratch_shapes=[pltpu.VMEM((bins, BLK, width), F32)],
        ),
        compiler_params=params(),
    )(slot_block, returned)


def weight_grads(coef, feats, source_grads, d_out, bases, chunk=128):
    relations, nodes, width = source_grads.shape
    nbase, width_in, _ = bases.shape

    def kernel(coef_ref, feat_ref, src_ref, grad_ref, base_ref, out_ref, dots_ref, acc_ref):
        @pl.when(pl.program_id(0) == 0)
        def _():
            acc_ref[...] = jnp.zeros_like(acc_ref)

        cols = feat_ref[...].T
        for r in range(relations):
            g = jnp.dot(cols, src_ref[r], preferred_element_type=F32)
            for b in range(nbase):
                scaled = coef_ref[r * nbase + b] * g
                if r == 0:
                    out_ref[b] = scaled
                else:
                    out_ref[b] += scaled
                prod = g * base_ref[b].astype(F32)
                acc_ref[r * nbase + b] += jnp.sum(prod.reshape(-1, 8, width), axis=0)
        out_ref[nbase] = jnp.dot(cols, grad_ref[...], preferred_element_type=F32)

        @pl.when(pl.program_id(0) == pl.num_programs(0) - 1)
        def _():
            row = lax.broadcasted_iota(jnp.int32, (8, BLK), 0)
            lane = lax.broadcasted_iota(jnp.int32, (8, BLK), 1)
            tile = jnp.zeros((8, BLK), F32)
            for r in range(relations):
                for b in range(nbase):
                    total = jnp.sum(acc_ref[r * nbase + b])
                    tile = jnp.where((row == r) & (lane == b), total, tile)
            dots_ref[...] = tile

    return pl.pallas_call(
        kernel,
        name="weight_grads",
        out_shape=(
            jax.ShapeDtypeStruct((nbase + 1, width_in, width), F32),
            jax.ShapeDtypeStruct((8, BLK), F32),
        ),
        grid_spec=pltpu.PrefetchScalarGridSpec(
            num_scalar_prefetch=1,
            grid=(width_in // chunk,),
            in_specs=[
                pl.BlockSpec((nodes, chunk), lambda i, *_: (0, i)),
                whole(source_grads.shape),
                whole(d_out.shape),
                pl.BlockSpec((nbase, chunk, width), lambda i, *_: (0, i, 0)),
            ],
            out_specs=(
                pl.BlockSpec((nbase + 1, chunk, width), lambda i, *_: (0, i, 0)),
                whole((8, BLK)),
            ),
            scratch_shapes=[pltpu.VMEM((relations * nbase, 8, width), F32)],
        ),
        compiler_params=params(),
    )(coef, feats, source_grads, d_out, bases)


def exchange(x, axis, mask):
    return lax.ppermute(x, axis, [(i, i ^ mask) for i in range(lax.axis_size(axis))])


def chunk_of(x, at, dim):
    return lax.dynamic_index_in_dim(x, at, dim, keepdims=False)


def scatter_sum(x, axis, shift, size, me, dim=0):
    at = (me >> shift) & (size - 1)
    total = chunk_of(x, at, dim)
    for k in range(1, size):
        part = chunk_of(x, at ^ k, dim).astype(BF16)
        total = total + exchange(part, axis, k << shift).astype(F32)
    return total


def two_terms(x):
    high = x.astype(BF16)
    low = (x - high.astype(F32)).astype(BF16)
    return high, low


def sum_terms(x):
    return x[:, :BLK].astype(F32) + x[:, BLK:].astype(F32)


def first_stage(place, stacked, got, dots, size):
    parts, _, rest, _, rows, width = stacked.shape
    length = parts * rest * rows

    def kernel(place_ref, own_ref, got_ref, dots_ref, keep_ref, *send_refs):
        core = place_ref[0]
        at = place_ref[1]
        high, low = two_terms(dots_ref[...])
        for k in range(size):
            for p in range(parts):
                for q in range(rest):
                    value = own_ref[p, at ^ k, q, core] + got_ref[p, at ^ k, q].astype(F32)
                    if k == 0:
                        keep_ref[p, q] = value
                    else:
                        send_refs[k - 1][pl.ds((p * rest + q) * rows, rows), :] = value.astype(BF16)
            if k:
                send_refs[k - 1][pl.ds(length, 8), pl.ds(0, BLK)] = high
                send_refs[k - 1][pl.ds(length, 8), pl.ds(BLK, BLK)] = low

    sent = (length + 8, width)
    return pl.pallas_call(
        kernel,
        name="first_stage",
        out_shape=(jax.ShapeDtypeStruct((parts, rest, rows, width), F32),)
        + (jax.ShapeDtypeStruct(sent, BF16),) * (size - 1),
        grid_spec=pltpu.PrefetchScalarGridSpec(
            num_scalar_prefetch=1,
            grid=(1,),
            in_specs=[whole(stacked.shape), whole(got.shape), whole(dots.shape)],
            out_specs=(whole((parts, rest, rows, width)),) + (whole(sent),) * (size - 1),
        ),
        compiler_params=params(),
    )(place, stacked, got, dots)


def second_stage(place, kept, dots, got, size):
    parts, _, rows, width = kept.shape
    length = parts * rows

    def kernel(place_ref, own_ref, dots_ref, *refs):
        gots = refs[: len(got)]
        keep_ref, all_ref = refs[len(got) : len(got) + 2]
        send_refs = refs[len(got) + 2 :]
        at = place_ref[2]
        high, low = two_terms(dots_ref[...])
        sums = [high.astype(F32) + low.astype(F32)]
        sums += [sum_terms(g[pl.ds(length * size, 8), :]) for g in gots]
        while len(sums) > 1:
            sums = [sums[i] + sums[i + 1] for i in range(0, len(sums), 2)]
        all_ref[...] = sums[0]
        high, low = two_terms(sums[0])
        for k in range(size):
            for p in range(parts):
                value = own_ref[p, at ^ k]
                start = pl.multiple_of((p * size + (at ^ k)) * rows, 8)
                for g in gots:
                    value = value + g[pl.ds(start, rows), :].astype(F32)
                if k == 0:
                    keep_ref[p] = value
                else:
                    send_refs[k - 1][pl.ds(p * rows, rows), :] = value.astype(BF16)
            if k:
                send_refs[k - 1][pl.ds(length, 8), pl.ds(0, BLK)] = high
                send_refs[k - 1][pl.ds(length, 8), pl.ds(BLK, BLK)] = low

    sent = (length + 8, width)
    return pl.pallas_call(
        kernel,
        name="second_stage",
        out_shape=(
            jax.ShapeDtypeStruct((parts, rows, width), F32),
            jax.ShapeDtypeStruct((8, BLK), F32),
        )
        + (jax.ShapeDtypeStruct(sent, BF16),) * (size - 1),
        grid_spec=pltpu.PrefetchScalarGridSpec(
            num_scalar_prefetch=1,
            grid=(1,),
            in_specs=[whole(kept.shape), whole(dots.shape)] + [whole(g.shape) for g in got],
            out_specs=(whole((parts, rows, width)), whole((8, BLK))) + (whole(sent),) * (size - 1),
        ),
        compiler_params=params(),
    )(place, kept, dots, *got)


def last_stage(kept, dots, got, relations):
    parts, rows, width = kept.shape
    length = parts * rows
    nbase = parts - 1

    def kernel(own_ref, dots_ref, *refs):
        gots = refs[: len(got)]
        bases_ref, root_ref, coef_ref = refs[len(got) :]
        high, low = two_terms(dots_ref[...])
        sums = [high.astype(F32) + low.astype(F32)]
        sums += [sum_terms(g[pl.ds(length, 8), :]) for g in gots]
        while len(sums) > 1:
            sums = [sums[i] + sums[i + 1] for i in range(0, len(sums), 2)]
        coef_ref[...] = sums[0][:relations, :nbase]
        for p in range(parts):
            value = own_ref[p]
            for g in gots:
                value = value + g[pl.ds(p * rows, rows), :].astype(F32)
            if p < nbase:
                bases_ref[p] = value
            else:
                root_ref[...] = value

    shapes = ((nbase, rows, width), (rows, width), (relations, nbase))
    return pl.pallas_call(
        kernel,
        name="last_stage",
        out_shape=tuple(jax.ShapeDtypeStruct(x, F32) for x in shapes),
        grid=(1,),
        in_specs=[whole(kept.shape), whole(dots.shape)] + [whole(g.shape) for g in got],
        out_specs=tuple(whole(x) for x in shapes),
        compiler_params=params(),
    )(kept, dots, *got)


def body(
    feats, bases, coef, root_weight, slot_block, recv_rel, tile_slot, tile_dst, tile_adj, d_out
):
    shards = lax.axis_size("shard")
    reps = lax.axis_size("rep")
    me = lax.axis_index("shard")
    my_rep = lax.axis_index("rep")
    nblocks = feats.shape[0] // BLK
    width_in = feats.shape[1]
    width = root_weight.shape[1]
    relations, nbase = coef.shape
    capacity = slot_block.shape[2]
    slots = shards * capacity

    slot_grads = tile_grads(
        tile_slot[0],
        tile_dst[0],
        recv_rel[0].T,
        tile_adj[0],
        d_out.reshape(nblocks, BLK, width),
        shards,
    )
    returned = lax.all_to_all(slot_grads, "shard", 0, 0, tiled=True)

    rel_weights = (
        jnp.dot(coef, bases.reshape(nbase, -1), preferred_element_type=F32)
        .astype(BF16)
        .reshape(relations, width_in, width)
    )
    projected = project(feats, rel_weights, nblocks)
    root_term = jnp.dot(feats, root_weight, preferred_element_type=F32)

    requested = slot_block[0].T
    outgoing = select_blocks(requested, returned, projected, nblocks, capacity)
    outgoing, returned = lax.optimization_barrier((outgoing, returned))
    incoming = lax.all_to_all(outgoing, "shard", 0, 0, tiled=True)

    source_grads = sum_by_key(requested, returned, relations, nblocks)
    source_grads = source_grads.reshape(relations, nblocks * BLK, width)
    stacked, dots = weight_grads(
        coef.astype(F32).reshape(-1), feats, source_grads, d_out, bases
    )
    dots = dots + exchange(dots, "shard", 1)
    for step in (1, 2):
        dots = dots + exchange(dots, "rep", step)

    through = jnp.einsum("rno,rco->nc", source_grads, rel_weights, preferred_element_type=F32)
    through = through + jnp.dot(d_out, root_weight.T, preferred_element_type=F32)
    through, dots = lax.optimization_barrier((through, dots))
    grad_feats = scatter_sum(
        through.reshape(reps, -1, width_in), "rep", 0, reps, my_rep
    ).astype(BF16)

    rows = width_in // shards
    stacked = stacked.reshape(nbase + 1, 4, 4, 2, rows, width)
    place = jnp.stack([me & 1, (me >> 3) & 3, (me >> 1) & 3]).astype(jnp.int32)
    got = exchange(chunk_of(stacked, (me & 1) ^ 1, 3).astype(BF16), "shard", 1)
    kept, *sends = first_stage(place, stacked, got, dots, 4)
    grad_feats, sends[-1] = lax.optimization_barrier((grad_feats, sends[-1]))
    got = [exchange(x, "shard", k << 3) for k, x in zip((1, 2, 3), sends)]
    kept, dots, *sends = second_stage(place, kept, dots, got, 4)
    root_term, *sends = lax.optimization_barrier((root_term, *sends))
    got = [exchange(x, "shard", k << 1) for k, x in zip((1, 2, 3), sends)]
    output = tile_sums(
        tile_slot[0],
        tile_dst[0],
        tile_adj[0],
        incoming.reshape(slots, BLK, width),
        root_term.reshape(nblocks, BLK, width),
    ).reshape(nblocks * BLK, width)
    output, kept = lax.optimization_barrier((output, kept))
    grad_bases, grad_root, grad_coef = last_stage(kept, dots, got, relations)
    return (output, grad_feats, grad_bases, grad_root, grad_coef)


def solution(mesh):
    placed = (
        P("shard", None),
        P(None, None, "rep"),
        P(),
        P(None, "rep"),
        P("shard", None, None),
        P("shard", None, None),
        P("shard", None),
        P("shard", None),
        P("shard", None, None, None),
        P("shard", "rep"),
    )
    return jax.shard_map(
        body,
        mesh=mesh,
        in_specs=placed,
        out_specs=(
            P("shard", "rep"),
            P(("shard", "rep"), None),
            P(None, "shard", "rep"),
            P("shard", "rep"),
            P(),
        ),
        check_vma=False,
    )
```

```python
import jax
import jax.numpy as jnp
from jax import lax
from jax.experimental import pallas as pl
from jax.experimental.pallas import tpu as pltpu
from jax.sharding import PartitionSpec as P

BLK = 128
F32 = jnp.float32
BF16 = jnp.bfloat16
VMEM_LIMIT = 48 * 1024 * 1024


def params():
    return pltpu.CompilerParams(vmem_limit_bytes=VMEM_LIMIT)


def in_hbm(x):
    return pltpu.with_memory_space_constraint(x, pltpu.HBM)


def whole(shape):
    return pl.BlockSpec(shape, lambda *_: (0,) * len(shape))


def tile_grads(tile_ids, dest_ids, rels, adjacency, grads, shards, chunk=64):
    tiles = adjacency.shape[0]
    nblocks, _, width = grads.shape
    capacity = rels.shape[0]
    slots = shards * capacity
    rows = capacity * BLK + 8

    def kernel(slot_ref, dst_ref, rel_ref, adj_ref, grad_ref, out_ref, acc_ref):
        step = pl.program_id(0)

        @pl.when(step == 0)
        def _():
            acc_ref[...] = jnp.zeros_like(acc_ref)

        for u in range(chunk):
            t = step * chunk + u
            part = lax.dot_general(
                adj_ref[u],
                grad_ref[dst_ref[t]],
                (((0,), (0,)), ((), ())),
                preferred_element_type=F32,
            )
            acc_ref[slot_ref[t]] += part

        @pl.when(step == pl.num_programs(0) - 1)
        def _():
            lane = lax.broadcasted_iota(jnp.int32, (8, width), 1)
            for o in range(shards):
                tail = jnp.zeros((8, width), F32)
                for c in range(capacity):
                    s = o * capacity + c
                    out_ref[o, pl.ds(c * BLK, BLK), :] = acc_ref[s].astype(BF16)
                    tail = jnp.where(lane // BLK == c, rel_ref[c, o].astype(F32), tail)
                out_ref[o, pl.ds(capacity * BLK, 8), :] = tail.astype(BF16)

    return pl.pallas_call(
        kernel,
        name="tile_grads",
        out_shape=pltpu.HBM((shards, rows, width), BF16),
        grid_spec=pltpu.PrefetchScalarGridSpec(
            num_scalar_prefetch=3,
            grid=(tiles // chunk,),
            in_specs=[
                pl.BlockSpec((chunk, BLK, BLK), lambda i, *_: (i, 0, 0)),
                whole(grads.shape),
            ],
            out_specs=whole((shards, rows, width)),
            scratch_shapes=[pltpu.VMEM((slots, BLK, width), F32)],
        ),
        compiler_params=params(),
    )(in_hbm(tile_ids), in_hbm(dest_ids), in_hbm(rels), adjacency, in_hbm(grads))


def project(feats, rel_weights, nblocks):
    relations, _, width = rel_weights.shape

    def kernel(feat_ref, w_ref, out_ref):
        for b in range(nblocks):
            out_ref[b] = jnp.dot(
                feat_ref[pl.ds(b * BLK, BLK), :], w_ref[0], preferred_element_type=F32
            ).astype(BF16)

    return pl.pallas_call(
        kernel,
        name="project",
        out_shape=pltpu.HBM((relations * nblocks, BLK, width), BF16),
        grid=(relations,),
        in_specs=[
            whole(feats.shape),
            pl.BlockSpec((1,) + rel_weights.shape[1:], lambda r: (r, 0, 0)),
        ],
        out_specs=pl.BlockSpec((nblocks, BLK, width), lambda r: (r, 0, 0)),
        compiler_params=params(),
    )(feats, rel_weights)


def tile_sums(tile_ids, dest_ids, adjacency, msgs, root_term, chunk=64):
    tiles = adjacency.shape[0]

    def kernel(slot_ref, dst_ref, adj_ref, msg_ref, root_ref, out_ref, acc_ref):
        step = pl.program_id(0)

        @pl.when(step == 0)
        def _():
            acc_ref[...] = root_ref[...]

        for u in range(chunk):
            t = step * chunk + u
            acc_ref[dst_ref[t]] += jnp.dot(
                adj_ref[u], msg_ref[slot_ref[t]], preferred_element_type=F32
            )

        @pl.when(step == pl.num_programs(0) - 1)
        def _():
            out_ref[...] = acc_ref[...].astype(BF16)

    return pl.pallas_call(
        kernel,
        name="tile_sums",
        out_shape=jax.ShapeDtypeStruct(root_term.shape, BF16),
        grid_spec=pltpu.PrefetchScalarGridSpec(
            num_scalar_prefetch=2,
            grid=(tiles // chunk,),
            in_specs=[
                pl.BlockSpec((chunk, BLK, BLK), lambda i, *_: (i, 0, 0)),
                whole(msgs.shape),
                whole(root_term.shape),
            ],
            out_specs=whole(root_term.shape),
            scratch_shapes=[pltpu.VMEM(root_term.shape, F32)],
        ),
        compiler_params=params(),
    )(in_hbm(tile_ids), in_hbm(dest_ids), adjacency, msgs, root_term)


def relation_of(ref, c):
    return jnp.max(ref[:, c * BLK : (c + 1) * BLK].astype(F32)).astype(jnp.int32)


def select_blocks(slot_block, returned, blocks, nblocks, capacity):
    shards, _, width = returned.shape

    def kernel(block_ref, rel_ref, in_ref, out_ref, sem_ref):
        copies = []
        for o in range(shards):
            for c in range(capacity):
                key = relation_of(rel_ref[o], c) * nblocks + block_ref[c, o]
                copy = pltpu.make_async_copy(
                    in_ref.at[key], out_ref.at[o, pl.ds(c * BLK, BLK)], sem_ref.at[o, c]
                )
                copy.start()
                copies.append(copy)
        for copy in copies:
            copy.wait()

    return pl.pallas_call(
        kernel,
        name="select_blocks",
        out_shape=pltpu.HBM((shards, capacity * BLK, width), BF16),
        grid_spec=pltpu.PrefetchScalarGridSpec(
            num_scalar_prefetch=1,
            grid=(1,),
            in_specs=[
                pl.BlockSpec((shards, 8, width), lambda i, *_: (0, capacity * BLK // 8, 0)),
                pl.BlockSpec(memory_space=pl.ANY),
            ],
            out_specs=pl.BlockSpec(memory_space=pl.ANY),
            scratch_shapes=[pltpu.SemaphoreType.DMA((shards, capacity))],
        ),
        compiler_params=params(),
    )(in_hbm(slot_block), returned, in_hbm(blocks))


def sum_by_key(slot_block, returned, relations, nblocks, chunk=8):
    shards, rows, width = returned.shape
    capacity = slot_block.shape[0]
    bins = relations * nblocks

    def kernel(block_ref, ret_ref, out_ref, acc_ref):
        step = pl.program_id(0)

        @pl.when(step == 0)
        def _():
            acc_ref[...] = jnp.zeros_like(acc_ref)

        for u in range(chunk):
            for c in range(capacity):
                rel = relation_of(ret_ref[u, pl.ds(capacity * BLK, 8), :], c)
                key = rel * nblocks + block_ref[c, step * chunk + u]
                acc_ref[key] += ret_ref[u, pl.ds(c * BLK, BLK), :].astype(F32)

        @pl.when(step == pl.num_programs(0) - 1)
        def _():
            out_ref[...] = acc_ref[...].astype(BF16)

    return pl.pallas_call(
        kernel,
        name="sum_by_key",
        out_shape=pltpu.HBM((bins, BLK, width), BF16),
        grid_spec=pltpu.PrefetchScalarGridSpec(
            num_scalar_prefetch=1,
            grid=(shards // chunk,),
            in_specs=[pl.BlockSpec((chunk, rows, width), lambda i, *_: (i, 0, 0))],
            out_specs=whole((bins, BLK, width)),
            scratch_shapes=[pltpu.VMEM((bins, BLK, width), F32)],
        ),
        compiler_params=params(),
    )(slot_block, returned)


def weight_grads(coef, feats, source_grads, d_out, bases, chunk=128):
    relations, nodes, width = source_grads.shape
    nbase, width_in, _ = bases.shape

    def kernel(coef_ref, feat_ref, src_ref, grad_ref, base_ref, out_ref, dots_ref, acc_ref):
        @pl.when(pl.program_id(0) == 0)
        def _():
            acc_ref[...] = jnp.zeros_like(acc_ref)

        cols = feat_ref[...].T
        for r in range(relations):
            g = jnp.dot(cols, src_ref[r], preferred_element_type=F32)
            for b in range(nbase):
                scaled = coef_ref[r * nbase + b] * g
                if r == 0:
                    out_ref[b] = scaled
                else:
                    out_ref[b] += scaled
                prod = g * base_ref[b].astype(F32)
                acc_ref[r * nbase + b] += jnp.sum(prod.reshape(-1, 8, width), axis=0)
        out_ref[nbase] = jnp.dot(cols, grad_ref[...], preferred_element_type=F32)

        @pl.when(pl.program_id(0) == pl.num_programs(0) - 1)
        def _():
            row = lax.broadcasted_iota(jnp.int32, (8, BLK), 0)
            lane = lax.broadcasted_iota(jnp.int32, (8, BLK), 1)
            tile = jnp.zeros((8, BLK), F32)
            for r in range(relations):
                for b in range(nbase):
                    total = jnp.sum(acc_ref[r * nbase + b])
                    tile = jnp.where((row == b) & (lane == r), total, tile)
            dots_ref[...] = tile

    return pl.pallas_call(
        kernel,
        name="weight_grads",
        out_shape=(
            jax.ShapeDtypeStruct((nbase + 1, width_in, width), F32),
            jax.ShapeDtypeStruct((8, BLK), F32),
        ),
        grid_spec=pltpu.PrefetchScalarGridSpec(
            num_scalar_prefetch=1,
            grid=(width_in // chunk,),
            in_specs=[
                pl.BlockSpec((nodes, chunk), lambda i, *_: (0, i)),
                whole(source_grads.shape),
                whole(d_out.shape),
                pl.BlockSpec((nbase, chunk, width), lambda i, *_: (0, i, 0)),
            ],
            out_specs=(
                pl.BlockSpec((nbase + 1, chunk, width), lambda i, *_: (0, i, 0)),
                whole((8, BLK)),
            ),
            scratch_shapes=[pltpu.VMEM((relations * nbase, 8, width), F32)],
        ),
        compiler_params=params(),
    )(coef, feats, source_grads, d_out, bases)


def exchange(x, axis, mask):
    return lax.ppermute(x, axis, [(i, i ^ mask) for i in range(lax.axis_size(axis))])


def chunk_of(x, at, dim):
    return lax.dynamic_index_in_dim(x, at, dim, keepdims=False)


def scatter_sum(x, axis, shift, size, me, dim=0):
    at = (me >> shift) & (size - 1)
    total = chunk_of(x, at, dim)
    for k in range(1, size):
        part = chunk_of(x, at ^ k, dim).astype(BF16)
        total = total + exchange(part, axis, k << shift).astype(F32)
    return total


def two_terms(x):
    high = x.astype(BF16)
    low = (x - high.astype(F32)).astype(BF16)
    return high, low


def sum_terms(x):
    return x[:, :BLK].astype(F32) + x[:, BLK:].astype(F32)


def first_stage(place, stacked, got, dots, size):
    parts, _, rest, _, rows, width = stacked.shape
    length = parts * rest * rows

    def kernel(place_ref, own_ref, got_ref, dots_ref, keep_ref, *send_refs):
        core = place_ref[0]
        at = place_ref[1]
        high, low = two_terms(dots_ref[...])
        for k in range(size):
            for p in range(parts):
                for q in range(rest):
                    value = own_ref[p, at ^ k, q, core] + got_ref[p, at ^ k, q].astype(F32)
                    if k == 0:
                        keep_ref[p, q] = value
                    else:
                        send_refs[k - 1][pl.ds((p * rest + q) * rows, rows), :] = value.astype(BF16)
            if k:
                send_refs[k - 1][pl.ds(length, 8), pl.ds(0, BLK)] = high
                send_refs[k - 1][pl.ds(length, 8), pl.ds(BLK, BLK)] = low

    sent = (length + 8, width)
    return pl.pallas_call(
        kernel,
        name="first_stage",
        out_shape=(jax.ShapeDtypeStruct((parts, rest, rows, width), F32),)
        + (jax.ShapeDtypeStruct(sent, BF16),) * (size - 1),
        grid_spec=pltpu.PrefetchScalarGridSpec(
            num_scalar_prefetch=1,
            grid=(1,),
            in_specs=[whole(stacked.shape), whole(got.shape), whole(dots.shape)],
            out_specs=(whole((parts, rest, rows, width)),) + (whole(sent),) * (size - 1),
        ),
        compiler_params=params(),
    )(place, stacked, got, dots)


def second_stage(place, kept, dots, got, size):
    parts, _, rows, width = kept.shape
    length = parts * rows

    def kernel(place_ref, own_ref, dots_ref, *refs):
        gots = refs[: len(got)]
        keep_ref, all_ref = refs[len(got) : len(got) + 2]
        send_refs = refs[len(got) + 2 :]
        at = place_ref[2]
        high, low = two_terms(dots_ref[...])
        sums = [high.astype(F32) + low.astype(F32)]
        sums += [sum_terms(g[pl.ds(length * size, 8), :]) for g in gots]
        while len(sums) > 1:
            sums = [sums[i] + sums[i + 1] for i in range(0, len(sums), 2)]
        all_ref[...] = sums[0]
        high, low = two_terms(sums[0])
        for k in range(size):
            for p in range(parts):
                value = own_ref[p, at ^ k]
                start = pl.multiple_of((p * size + (at ^ k)) * rows, 8)
                for g in gots:
                    value = value + g[pl.ds(start, rows), :].astype(F32)
                if k == 0:
                    keep_ref[p] = value
                else:
                    send_refs[k - 1][pl.ds(p * rows, rows), :] = value.astype(BF16)
            if k:
                send_refs[k - 1][pl.ds(length, 8), pl.ds(0, BLK)] = high
                send_refs[k - 1][pl.ds(length, 8), pl.ds(BLK, BLK)] = low

    sent = (length + 8, width)
    return pl.pallas_call(
        kernel,
        name="second_stage",
        out_shape=(
            jax.ShapeDtypeStruct((parts, rows, width), F32),
            jax.ShapeDtypeStruct((8, BLK), F32),
        )
        + (jax.ShapeDtypeStruct(sent, BF16),) * (size - 1),
        grid_spec=pltpu.PrefetchScalarGridSpec(
            num_scalar_prefetch=1,
            grid=(1,),
            in_specs=[whole(kept.shape), whole(dots.shape)] + [whole(g.shape) for g in got],
            out_specs=(whole((parts, rows, width)), whole((8, BLK))) + (whole(sent),) * (size - 1),
        ),
        compiler_params=params(),
    )(place, kept, dots, *got)


def last_stage(kept, dots, got, relations):
    parts, rows, width = kept.shape
    length = parts * rows
    nbase = parts - 1

    def kernel(own_ref, dots_ref, *refs):
        gots = refs[: len(got)]
        bases_ref, root_ref, coef_ref = refs[len(got) :]
        high, low = two_terms(dots_ref[...])
        sums = [high.astype(F32) + low.astype(F32)]
        sums += [sum_terms(g[pl.ds(length, 8), :]) for g in gots]
        while len(sums) > 1:
            sums = [sums[i] + sums[i + 1] for i in range(0, len(sums), 2)]
        coef_ref[...] = sums[0][:nbase, :relations]
        for p in range(parts):
            value = own_ref[p]
            for g in gots:
                value = value + g[pl.ds(p * rows, rows), :].astype(F32)
            if p < nbase:
                bases_ref[p] = value
            else:
                root_ref[...] = value

    shapes = ((nbase, rows, width), (rows, width), (nbase, relations))
    return pl.pallas_call(
        kernel,
        name="last_stage",
        out_shape=tuple(jax.ShapeDtypeStruct(x, F32) for x in shapes),
        grid=(1,),
        in_specs=[whole(kept.shape), whole(dots.shape)] + [whole(g.shape) for g in got],
        out_specs=tuple(whole(x) for x in shapes),
        compiler_params=params(),
    )(kept, dots, *got)


def body(
    feats, bases, coef, root_weight, slot_block, recv_rel, tile_slot, tile_dst, tile_adj, d_out
):
    shards = lax.axis_size("shard")
    reps = lax.axis_size("rep")
    me = lax.axis_index("shard")
    my_rep = lax.axis_index("rep")
    nblocks = feats.shape[0] // BLK
    width_in = feats.shape[1]
    width = root_weight.shape[1]
    relations, nbase = coef.shape
    capacity = slot_block.shape[2]
    slots = shards * capacity

    slot_grads = tile_grads(
        tile_slot[0],
        tile_dst[0],
        recv_rel[0].T,
        tile_adj[0],
        d_out.reshape(nblocks, BLK, width),
        shards,
    )
    returned = lax.all_to_all(slot_grads, "shard", 0, 0, tiled=True)

    rel_weights = (
        jnp.dot(coef, bases.reshape(nbase, -1), preferred_element_type=F32)
        .astype(BF16)
        .reshape(relations, width_in, width)
    )
    projected = project(feats, rel_weights, nblocks)
    root_term = jnp.dot(feats, root_weight, preferred_element_type=F32)

    requested = slot_block[0].T
    outgoing = select_blocks(requested, returned, projected, nblocks, capacity)
    outgoing, returned = lax.optimization_barrier((outgoing, returned))
    incoming = lax.all_to_all(outgoing, "shard", 0, 0, tiled=True)

    source_grads = sum_by_key(requested, returned, relations, nblocks)
    source_grads = source_grads.reshape(relations, nblocks * BLK, width)
    stacked, dots = weight_grads(
        coef.astype(F32).reshape(-1), feats, source_grads, d_out, bases
    )
    dots = dots + exchange(dots, "shard", 1)
    for step in (1, 2):
        dots = dots + exchange(dots, "rep", step)

    through = jnp.einsum("rno,rco->nc", source_grads, rel_weights, preferred_element_type=F32)
    through = through + jnp.dot(d_out, root_weight.T, preferred_element_type=F32)
    rows = width_in // shards
    stacked = stacked.reshape(nbase + 1, 4, 4, 2, rows, width)
    place = jnp.stack([me & 1, (me >> 3) & 3, (me >> 1) & 3]).astype(jnp.int32)
    got = exchange(chunk_of(stacked, (me & 1) ^ 1, 3).astype(BF16), "shard", 1)
    kept, *sends = first_stage(place, stacked, got, dots, 4)
    through, *sends = lax.optimization_barrier((through, *sends))
    got = [exchange(x, "shard", k << 3) for k, x in zip((1, 2, 3), sends)]
    grad_feats = scatter_sum(
        through.reshape(reps, -1, width_in), "rep", 0, reps, my_rep
    ).astype(BF16)
    output = tile_sums(
        tile_slot[0],
        tile_dst[0],
        tile_adj[0],
        incoming.reshape(slots, BLK, width),
        root_term.reshape(nblocks, BLK, width),
    ).reshape(nblocks * BLK, width)
    output, grad_feats, kept = lax.optimization_barrier((output, grad_feats, kept))
    kept, dots, *sends = second_stage(place, kept, dots, got, 4)
    got = [exchange(x, "shard", k << 1) for k, x in zip((1, 2, 3), sends)]
    grad_bases, grad_root, grad_coef = last_stage(kept, dots, got, relations)
    return (output, grad_feats, grad_bases, grad_root, grad_coef.T)


def solution(mesh):
    placed = (
        P("shard", None),
        P(None, None, "rep"),
        P(),
        P(None, "rep"),
        P("shard", None, None),
        P("shard", None, None),
        P("shard", None),
        P("shard", None),
        P("shard", None, None, None),
        P("shard", "rep"),
    )
    return jax.shard_map(
        body,
        mesh=mesh,
        in_specs=placed,
        out_specs=(
            P("shard", "rep"),
            P(("shard", "rep"), None),
            P(None, "shard", "rep"),
            P("shard", "rep"),
            P(),
        ),
        check_vma=False,
    )
```

```python
import jax
import jax.numpy as jnp
from jax import lax
from jax.experimental import pallas as pl
from jax.experimental.pallas import tpu as pltpu
from jax.sharding import PartitionSpec as P

BLK = 128
F32 = jnp.float32
BF16 = jnp.bfloat16
VMEM_LIMIT = 48 * 1024 * 1024


def params():
    return pltpu.CompilerParams(vmem_limit_bytes=VMEM_LIMIT)


def in_hbm(x):
    return pltpu.with_memory_space_constraint(x, pltpu.HBM)


def whole(shape):
    return pl.BlockSpec(shape, lambda *_: (0,) * len(shape))


def tile_grads(tile_ids, dest_ids, rels, adjacency, grads, shards, chunk=64):
    tiles = adjacency.shape[0]
    nblocks, _, width = grads.shape
    capacity = rels.shape[0]
    slots = shards * capacity
    rows = capacity * BLK + 8

    def kernel(slot_ref, dst_ref, rel_ref, adj_ref, grad_ref, out_ref, acc_ref):
        step = pl.program_id(0)

        @pl.when(step == 0)
        def _():
            acc_ref[...] = jnp.zeros_like(acc_ref)

        for u in range(chunk):
            t = step * chunk + u
            part = lax.dot_general(
                adj_ref[u],
                grad_ref[dst_ref[t]],
                (((0,), (0,)), ((), ())),
                preferred_element_type=F32,
            )
            acc_ref[slot_ref[t]] += part

        @pl.when(step == pl.num_programs(0) - 1)
        def _():
            lane = lax.broadcasted_iota(jnp.int32, (8, width), 1)
            for o in range(shards):
                tail = jnp.zeros((8, width), F32)
                for c in range(capacity):
                    s = o * capacity + c
                    out_ref[o, pl.ds(c * BLK, BLK), :] = acc_ref[s].astype(BF16)
                    tail = jnp.where(lane // BLK == c, rel_ref[c, o].astype(F32), tail)
                out_ref[o, pl.ds(capacity * BLK, 8), :] = tail.astype(BF16)

    return pl.pallas_call(
        kernel,
        name="tile_grads",
        out_shape=pltpu.HBM((shards, rows, width), BF16),
        grid_spec=pltpu.PrefetchScalarGridSpec(
            num_scalar_prefetch=3,
            grid=(tiles // chunk,),
            in_specs=[
                pl.BlockSpec((chunk, BLK, BLK), lambda i, *_: (i, 0, 0)),
                whole(grads.shape),
            ],
            out_specs=whole((shards, rows, width)),
            scratch_shapes=[pltpu.VMEM((slots, BLK, width), F32)],
        ),
        compiler_params=params(),
    )(in_hbm(tile_ids), in_hbm(dest_ids), in_hbm(rels), adjacency, in_hbm(grads))


def project(feats, rel_weights, nblocks):
    relations, _, width = rel_weights.shape

    def kernel(feat_ref, w_ref, out_ref):
        for b in range(nblocks):
            out_ref[b] = jnp.dot(
                feat_ref[pl.ds(b * BLK, BLK), :], w_ref[0], preferred_element_type=F32
            ).astype(BF16)

    return pl.pallas_call(
        kernel,
        name="project",
        out_shape=pltpu.HBM((relations * nblocks, BLK, width), BF16),
        grid=(relations,),
        in_specs=[
            whole(feats.shape),
            pl.BlockSpec((1,) + rel_weights.shape[1:], lambda r: (r, 0, 0)),
        ],
        out_specs=pl.BlockSpec((nblocks, BLK, width), lambda r: (r, 0, 0)),
        compiler_params=params(),
    )(feats, rel_weights)


def tile_sums(tile_ids, dest_ids, adjacency, msgs, root_term, chunk=64):
    tiles = adjacency.shape[0]

    def kernel(slot_ref, dst_ref, adj_ref, msg_ref, root_ref, out_ref, acc_ref):
        step = pl.program_id(0)

        @pl.when(step == 0)
        def _():
            acc_ref[...] = root_ref[...]

        for u in range(chunk):
            t = step * chunk + u
            acc_ref[dst_ref[t]] += jnp.dot(
                adj_ref[u], msg_ref[slot_ref[t]], preferred_element_type=F32
            )

        @pl.when(step == pl.num_programs(0) - 1)
        def _():
            out_ref[...] = acc_ref[...].astype(BF16)

    return pl.pallas_call(
        kernel,
        name="tile_sums",
        out_shape=jax.ShapeDtypeStruct(root_term.shape, BF16),
        grid_spec=pltpu.PrefetchScalarGridSpec(
            num_scalar_prefetch=2,
            grid=(tiles // chunk,),
            in_specs=[
                pl.BlockSpec((chunk, BLK, BLK), lambda i, *_: (i, 0, 0)),
                whole(msgs.shape),
                whole(root_term.shape),
            ],
            out_specs=whole(root_term.shape),
            scratch_shapes=[pltpu.VMEM(root_term.shape, F32)],
        ),
        compiler_params=params(),
    )(in_hbm(tile_ids), in_hbm(dest_ids), adjacency, msgs, root_term)


def relation_of(ref, c):
    return jnp.max(ref[:, c * BLK : (c + 1) * BLK].astype(F32)).astype(jnp.int32)


def select_blocks(slot_block, returned, blocks, nblocks, capacity):
    shards, _, width = returned.shape

    def kernel(block_ref, rel_ref, in_hbm_ref, out_ref, in_ref, load_ref, sem_ref):
        load = pltpu.make_async_copy(in_hbm_ref, in_ref, load_ref)
        load.start()
        rels = [[relation_of(rel_ref[o], c) for c in range(capacity)] for o in range(shards)]
        load.wait()
        copies = []
        for o in range(shards):
            for c in range(capacity):
                key = rels[o][c] * nblocks + block_ref[c, o]
                copy = pltpu.make_async_copy(
                    in_ref.at[key], out_ref.at[o, pl.ds(c * BLK, BLK)], sem_ref.at[o, c]
                )
                copy.start()
                copies.append(copy)
        for copy in copies:
            copy.wait()

    return pl.pallas_call(
        kernel,
        name="select_blocks",
        out_shape=pltpu.HBM((shards, capacity * BLK, width), BF16),
        grid_spec=pltpu.PrefetchScalarGridSpec(
            num_scalar_prefetch=1,
            grid=(1,),
            in_specs=[
                pl.BlockSpec((shards, 8, width), lambda i, *_: (0, capacity * BLK // 8, 0)),
                pl.BlockSpec(memory_space=pl.ANY),
            ],
            out_specs=pl.BlockSpec(memory_space=pl.ANY),
            scratch_shapes=[
                pltpu.VMEM(blocks.shape, BF16),
                pltpu.SemaphoreType.DMA,
                pltpu.SemaphoreType.DMA((shards, capacity)),
            ],
        ),
        compiler_params=params(),
    )(in_hbm(slot_block), returned, in_hbm(blocks))


def sum_by_key(slot_block, returned, relations, nblocks, chunk=8):
    shards, rows, width = returned.shape
    capacity = slot_block.shape[0]
    bins = relations * nblocks

    def kernel(block_ref, ret_ref, out_ref, acc_ref):
        step = pl.program_id(0)

        @pl.when(step == 0)
        def _():
            acc_ref[...] = jnp.zeros_like(acc_ref)

        for u in range(chunk):
            for c in range(capacity):
                rel = relation_of(ret_ref[u, pl.ds(capacity * BLK, 8), :], c)
                key = rel * nblocks + block_ref[c, step * chunk + u]
                acc_ref[key] += ret_ref[u, pl.ds(c * BLK, BLK), :].astype(F32)

        @pl.when(step == pl.num_programs(0) - 1)
        def _():
            out_ref[...] = acc_ref[...].astype(BF16)

    return pl.pallas_call(
        kernel,
        name="sum_by_key",
        out_shape=pltpu.HBM((bins, BLK, width), BF16),
        grid_spec=pltpu.PrefetchScalarGridSpec(
            num_scalar_prefetch=1,
            grid=(shards // chunk,),
            in_specs=[pl.BlockSpec((chunk, rows, width), lambda i, *_: (i, 0, 0))],
            out_specs=whole((bins, BLK, width)),
            scratch_shapes=[pltpu.VMEM((bins, BLK, width), F32)],
        ),
        compiler_params=params(),
    )(slot_block, returned)


def weight_grads(coef, feats, source_grads, d_out, bases, chunk=128):
    relations, nodes, width = source_grads.shape
    nbase, width_in, _ = bases.shape

    def kernel(coef_ref, feat_ref, src_ref, grad_ref, base_ref, out_ref, dots_ref, acc_ref):
        @pl.when(pl.program_id(0) == 0)
        def _():
            acc_ref[...] = jnp.zeros_like(acc_ref)

        cols = feat_ref[...].T
        for r in range(relations):
            g = jnp.dot(cols, src_ref[r], preferred_element_type=F32)
            for b in range(nbase):
                scaled = coef_ref[r * nbase + b] * g
                if r == 0:
                    out_ref[b] = scaled
                else:
                    out_ref[b] += scaled
                prod = g * base_ref[b].astype(F32)
                acc_ref[r * nbase + b] += jnp.sum(prod.reshape(-1, 8, width), axis=0)
        out_ref[nbase] = jnp.dot(cols, grad_ref[...], preferred_element_type=F32)

        @pl.when(pl.program_id(0) == pl.num_programs(0) - 1)
        def _():
            row = lax.broadcasted_iota(jnp.int32, (8, BLK), 0)
            lane = lax.broadcasted_iota(jnp.int32, (8, BLK), 1)
            tile = jnp.zeros((8, BLK), F32)
            for r in range(relations):
                for b in range(nbase):
                    total = jnp.sum(acc_ref[r * nbase + b])
                    tile = jnp.where((row == b) & (lane == r), total, tile)
            dots_ref[...] = tile

    return pl.pallas_call(
        kernel,
        name="weight_grads",
        cost_estimate=pl.CostEstimate(
            flops=2 * (relations + 1) * nodes * width_in * width,
            transcendentals=0,
            bytes_accessed=2 * nodes * (width_in + (relations + 1) * width)
            + 6 * (nbase + 1) * width_in * width,
        ),
        out_shape=(
            jax.ShapeDtypeStruct((nbase + 1, width_in, width), F32),
            jax.ShapeDtypeStruct((8, BLK), F32),
        ),
        grid_spec=pltpu.PrefetchScalarGridSpec(
            num_scalar_prefetch=1,
            grid=(width_in // chunk,),
            in_specs=[
                pl.BlockSpec((nodes, chunk), lambda i, *_: (0, i)),
                whole(source_grads.shape),
                whole(d_out.shape),
                pl.BlockSpec((nbase, chunk, width), lambda i, *_: (0, i, 0)),
            ],
            out_specs=(
                pl.BlockSpec((nbase + 1, chunk, width), lambda i, *_: (0, i, 0)),
                whole((8, BLK)),
            ),
            scratch_shapes=[pltpu.VMEM((relations * nbase, 8, width), F32)],
        ),
        compiler_params=params(),
    )(coef, feats, source_grads, d_out, bases)


def exchange(x, axis, mask):
    return lax.ppermute(x, axis, [(i, i ^ mask) for i in range(lax.axis_size(axis))])


def chunk_of(x, at, dim):
    return lax.dynamic_index_in_dim(x, at, dim, keepdims=False)


def two_terms(x):
    high = x.astype(BF16)
    low = (x - high.astype(F32)).astype(BF16)
    return high, low


def sum_terms(x):
    return x[:, :BLK].astype(F32) + x[:, BLK:].astype(F32)


def first_stage(place, stacked, got, dots, size):
    parts, _, rest, _, rows, width = stacked.shape
    length = parts * rest * rows

    def kernel(place_ref, own_ref, got_ref, dots_ref, keep_ref, *send_refs):
        core = place_ref[0]
        at = place_ref[1]
        high, low = two_terms(dots_ref[...])
        for k in range(size):
            for p in range(parts):
                for q in range(rest):
                    value = own_ref[p, at ^ k, q, core] + got_ref[p, at ^ k, q].astype(F32)
                    if k == 0:
                        keep_ref[p, q] = value
                    else:
                        send_refs[k - 1][pl.ds((p * rest + q) * rows, rows), :] = value.astype(BF16)
            if k:
                send_refs[k - 1][pl.ds(length, 8), pl.ds(0, BLK)] = high
                send_refs[k - 1][pl.ds(length, 8), pl.ds(BLK, BLK)] = low

    sent = (length + 8, width)
    return pl.pallas_call(
        kernel,
        name="first_stage",
        out_shape=(jax.ShapeDtypeStruct((parts, rest, rows, width), F32),)
        + (jax.ShapeDtypeStruct(sent, BF16),) * (size - 1),
        grid_spec=pltpu.PrefetchScalarGridSpec(
            num_scalar_prefetch=1,
            grid=(1,),
            in_specs=[whole(stacked.shape), whole(got.shape), whole(dots.shape)],
            out_specs=(whole((parts, rest, rows, width)),) + (whole(sent),) * (size - 1),
        ),
        compiler_params=params(),
    )(place, stacked, got, dots)


def second_stage(place, kept, dots, got, size):
    parts, _, rows, width = kept.shape
    length = parts * rows

    def kernel(place_ref, own_ref, dots_ref, *refs):
        gots = refs[: len(got)]
        keep_ref, all_ref = refs[len(got) : len(got) + 2]
        send_refs = refs[len(got) + 2 :]
        at = place_ref[2]
        high, low = two_terms(dots_ref[...])
        sums = [high.astype(F32) + low.astype(F32)]
        sums += [sum_terms(g[pl.ds(length * size, 8), :]) for g in gots]
        while len(sums) > 1:
            sums = [sums[i] + sums[i + 1] for i in range(0, len(sums), 2)]
        all_ref[...] = sums[0]
        high, low = two_terms(sums[0])
        for k in range(size):
            for p in range(parts):
                value = own_ref[p, at ^ k]
                start = pl.multiple_of((p * size + (at ^ k)) * rows, 8)
                for g in gots:
                    value = value + g[pl.ds(start, rows), :].astype(F32)
                if k == 0:
                    keep_ref[p] = value
                else:
                    send_refs[k - 1][pl.ds(p * rows, rows), :] = value.astype(BF16)
            if k:
                send_refs[k - 1][pl.ds(length, 8), pl.ds(0, BLK)] = high
                send_refs[k - 1][pl.ds(length, 8), pl.ds(BLK, BLK)] = low

    sent = (length + 8, width)
    return pl.pallas_call(
        kernel,
        name="second_stage",
        out_shape=(
            jax.ShapeDtypeStruct((parts, rows, width), F32),
            jax.ShapeDtypeStruct((8, BLK), F32),
        )
        + (jax.ShapeDtypeStruct(sent, BF16),) * (size - 1),
        grid_spec=pltpu.PrefetchScalarGridSpec(
            num_scalar_prefetch=1,
            grid=(1,),
            in_specs=[whole(kept.shape), whole(dots.shape)] + [whole(g.shape) for g in got],
            out_specs=(whole((parts, rows, width)), whole((8, BLK))) + (whole(sent),) * (size - 1),
        ),
        compiler_params=params(),
    )(place, kept, dots, *got)


def last_stage(kept, dots, got, relations):
    parts, rows, width = kept.shape
    length = parts * rows
    nbase = parts - 1

    def kernel(own_ref, dots_ref, *refs):
        gots = refs[: len(got)]
        bases_ref, root_ref, coef_ref = refs[len(got) :]
        high, low = two_terms(dots_ref[...])
        sums = [high.astype(F32) + low.astype(F32)]
        sums += [sum_terms(g[pl.ds(length, 8), :]) for g in gots]
        while len(sums) > 1:
            sums = [sums[i] + sums[i + 1] for i in range(0, len(sums), 2)]
        coef_ref[...] = sums[0][:nbase, :relations]
        for p in range(parts):
            value = own_ref[p]
            for g in gots:
                value = value + g[pl.ds(p * rows, rows), :].astype(F32)
            if p < nbase:
                bases_ref[p] = value
            else:
                root_ref[...] = value

    shapes = ((nbase, rows, width), (rows, width), (nbase, relations))
    return pl.pallas_call(
        kernel,
        name="last_stage",
        out_shape=tuple(jax.ShapeDtypeStruct(x, F32) for x in shapes),
        grid=(1,),
        in_specs=[whole(kept.shape), whole(dots.shape)] + [whole(g.shape) for g in got],
        out_specs=tuple(whole(x) for x in shapes),
        compiler_params=params(),
    )(kept, dots, *got)


def body(
    feats, bases, coef, root_weight, slot_block, recv_rel, tile_slot, tile_dst, tile_adj, d_out
):
    shards = lax.axis_size("shard")
    reps = lax.axis_size("rep")
    me = lax.axis_index("shard")
    my_rep = lax.axis_index("rep")
    nblocks = feats.shape[0] // BLK
    width_in = feats.shape[1]
    width = root_weight.shape[1]
    relations, nbase = coef.shape
    capacity = slot_block.shape[2]
    slots = shards * capacity

    slot_grads = tile_grads(
        tile_slot[0],
        tile_dst[0],
        recv_rel[0].T,
        tile_adj[0],
        d_out.reshape(nblocks, BLK, width),
        shards,
    )
    returned = lax.all_to_all(slot_grads, "shard", 0, 0, tiled=True)

    rel_weights = (
        jnp.dot(coef, bases.reshape(nbase, -1), preferred_element_type=F32)
        .astype(BF16)
        .reshape(relations, width_in, width)
    )
    projected = project(feats, rel_weights, nblocks)
    root_term = jnp.dot(feats, root_weight, preferred_element_type=F32)

    requested = slot_block[0].T
    outgoing = select_blocks(requested, returned, projected, nblocks, capacity)
    outgoing, returned = lax.optimization_barrier((outgoing, returned))
    incoming = lax.all_to_all(outgoing, "shard", 0, 0, tiled=True)

    source_grads = sum_by_key(requested, returned, relations, nblocks)
    source_grads = source_grads.reshape(relations, nblocks * BLK, width)
    through = jnp.einsum("rno,rco->nc", source_grads, rel_weights, preferred_element_type=F32)
    through = through + jnp.dot(d_out, root_weight.T, preferred_element_type=F32)
    through = through.reshape(reps, -1, width_in)
    parts = [chunk_of(through, my_rep ^ k, 0).astype(BF16) for k in range(1, reps)]
    stacked, dots = weight_grads(
        coef.astype(F32).reshape(-1), feats, source_grads, d_out, bases
    )
    dots = dots + exchange(dots, "shard", 1)
    for step in (1, 2):
        dots = dots + exchange(dots, "rep", step)

    dots, *parts = lax.optimization_barrier((dots, *parts))
    grad_feats = chunk_of(through, my_rep, 0)
    for k, part in zip(range(1, reps), parts):
        grad_feats = grad_feats + exchange(part, "rep", k).astype(F32)
    grad_feats = grad_feats.astype(BF16)

    rows = width_in // shards
    stacked = stacked.reshape(nbase + 1, 4, 4, 2, rows, width)
    place = jnp.stack([me & 1, (me >> 3) & 3, (me >> 1) & 3]).astype(jnp.int32)
    got = exchange(chunk_of(stacked, (me & 1) ^ 1, 3).astype(BF16), "shard", 1)
    kept, *sends = first_stage(place, stacked, got, dots, 4)
    got = [exchange(x, "shard", k << 3) for k, x in zip((1, 2, 3), sends)]
    output = tile_sums(
        tile_slot[0],
        tile_dst[0],
        tile_adj[0],
        incoming.reshape(slots, BLK, width),
        root_term.reshape(nblocks, BLK, width),
    ).reshape(nblocks * BLK, width)
    output, grad_feats, kept = lax.optimization_barrier((output, grad_feats, kept))
    kept, dots, *sends = second_stage(place, kept, dots, got, 4)
    got = [exchange(x, "shard", k << 1) for k, x in zip((1, 2, 3), sends)]
    grad_bases, grad_root, grad_coef = last_stage(kept, dots, got, relations)
    return (output, grad_feats, grad_bases, grad_root, grad_coef.T)


def solution(mesh):
    placed = (
        P("shard", None),
        P(None, None, "rep"),
        P(),
        P(None, "rep"),
        P("shard", None, None),
        P("shard", None, None),
        P("shard", None),
        P("shard", None),
        P("shard", None, None, None),
        P("shard", "rep"),
    )
    return jax.shard_map(
        body,
        mesh=mesh,
        in_specs=placed,
        out_specs=(
            P("shard", "rep"),
            P(("shard", "rep"), None),
            P(None, "shard", "rep"),
            P("shard", "rep"),
            P(),
        ),
        check_vma=False,
    )
```

```python
import jax
import jax.numpy as jnp
from jax import lax
from jax.experimental import pallas as pl
from jax.experimental.pallas import tpu as pltpu
from jax.sharding import PartitionSpec as P

BLK = 128
F32 = jnp.float32
BF16 = jnp.bfloat16
VMEM_LIMIT = 48 * 1024 * 1024
GROUP = 4
GROUP_CHUNK = 12


def params():
    return pltpu.CompilerParams(vmem_limit_bytes=VMEM_LIMIT)


def in_hbm(x):
    return pltpu.with_memory_space_constraint(x, pltpu.HBM)


def whole(shape):
    return pl.BlockSpec(shape, lambda *_: (0,) * len(shape))


def tile_grads(tile_ids, dest_ids, rels, adjacency, grads, shards, chunk=64):
    tiles = adjacency.shape[0]
    nblocks, _, width = grads.shape
    capacity = rels.shape[0]
    slots = shards * capacity
    rows = capacity * BLK + 8

    def kernel(slot_ref, dst_ref, rel_ref, adj_ref, grad_ref, out_ref, acc_ref):
        step = pl.program_id(0)

        @pl.when(step == 0)
        def _():
            acc_ref[...] = jnp.zeros_like(acc_ref)

        for u in range(chunk):
            t = step * chunk + u
            part = lax.dot_general(
                adj_ref[u],
                grad_ref[dst_ref[t]],
                (((0,), (0,)), ((), ())),
                preferred_element_type=F32,
            )
            acc_ref[slot_ref[t]] += part

        @pl.when(step == pl.num_programs(0) - 1)
        def _():
            lane = lax.broadcasted_iota(jnp.int32, (8, width), 1)
            for o in range(shards):
                tail = jnp.zeros((8, width), F32)
                for c in range(capacity):
                    s = o * capacity + c
                    out_ref[o, pl.ds(c * BLK, BLK), :] = acc_ref[s].astype(BF16)
                    tail = jnp.where(lane // BLK == c, rel_ref[c, o].astype(F32), tail)
                out_ref[o, pl.ds(capacity * BLK, 8), :] = tail.astype(BF16)

    return pl.pallas_call(
        kernel,
        name="tile_grads",
        out_shape=pltpu.HBM((shards, rows, width), BF16),
        grid_spec=pltpu.PrefetchScalarGridSpec(
            num_scalar_prefetch=3,
            grid=(tiles // chunk,),
            in_specs=[
                pl.BlockSpec((chunk, BLK, BLK), lambda i, *_: (i, 0, 0)),
                whole(grads.shape),
            ],
            out_specs=whole((shards, rows, width)),
            scratch_shapes=[pltpu.VMEM((slots, BLK, width), F32)],
        ),
        compiler_params=params(),
    )(in_hbm(tile_ids), in_hbm(dest_ids), in_hbm(rels), adjacency, in_hbm(grads))


def project(feats, rel_weights, nblocks):
    relations, _, width = rel_weights.shape

    def kernel(feat_ref, w_ref, out_ref):
        for b in range(nblocks):
            out_ref[b] = jnp.dot(
                feat_ref[pl.ds(b * BLK, BLK), :], w_ref[0], preferred_element_type=F32
            ).astype(BF16)

    return pl.pallas_call(
        kernel,
        name="project",
        out_shape=pltpu.HBM((relations * nblocks, BLK, width), BF16),
        grid=(relations,),
        in_specs=[
            whole(feats.shape),
            pl.BlockSpec((1,) + rel_weights.shape[1:], lambda r: (r, 0, 0)),
        ],
        out_specs=pl.BlockSpec((nblocks, BLK, width), lambda r: (r, 0, 0)),
        compiler_params=params(),
    )(feats, rel_weights)


def group_tables(tile_ids, dest_ids, nblocks):
    tiles = tile_ids.shape[0]
    groups = -(-(tiles + nblocks * (GROUP - 1)) // GROUP)
    groups = -(-groups // GROUP_CHUNK) * GROUP_CHUNK
    index = jnp.arange(tiles)
    hot = (dest_ids[:, None] == jnp.arange(nblocks)[None, :]).astype(jnp.int32)
    sizes = (jnp.sum(hot, axis=0) + GROUP - 1) // GROUP
    blocks = jnp.arange(nblocks)
    ends = jnp.sum(jnp.where(blocks[:, None] <= blocks[None, :], sizes[:, None], 0), axis=0)
    same = dest_ids[:, None] == dest_ids[None, :]
    rank = jnp.sum((same & (index[None, :] < index[:, None])).astype(jnp.int32), axis=1)
    place = jnp.sum(hot * (ends - sizes)[None, :], axis=1) * GROUP + rank
    here = place[None, :] == jnp.arange(groups * GROUP)[:, None]
    tile_at = jnp.sum(jnp.where(here, index[None, :] + 1, 0), axis=1) - 1
    slot_at = jnp.sum(jnp.where(here, tile_ids[None, :], 0), axis=1)
    passed = (jnp.arange(groups)[:, None] >= ends[None, :]).astype(jnp.int32)
    dest_of = jnp.minimum(jnp.sum(passed, axis=1), nblocks - 1)
    return tile_at.astype(jnp.int32), slot_at.astype(jnp.int32), dest_of.astype(jnp.int32)


def sort_tiles(tile_at, adjacency, chunk=GROUP * GROUP_CHUNK):
    places = tile_at.shape[0]

    def kernel(at_ref, adj_ref, out_ref):
        step = pl.program_id(0)
        for u in range(chunk):
            t = at_ref[step * chunk + u]

            @pl.when(t >= 0)
            def _():
                out_ref[u] = adj_ref[jnp.maximum(t, 0)]

            @pl.when(t < 0)
            def _():
                out_ref[u] = jnp.zeros((BLK, BLK), BF16)

    return pl.pallas_call(
        kernel,
        name="sort_tiles",
        out_shape=pltpu.HBM((places, BLK, BLK), BF16),
        grid_spec=pltpu.PrefetchScalarGridSpec(
            num_scalar_prefetch=1,
            grid=(places // chunk,),
            in_specs=[whole(adjacency.shape)],
            out_specs=pl.BlockSpec((chunk, BLK, BLK), lambda i, *_: (i, 0, 0)),
        ),
        compiler_params=params(),
    )(tile_at, adjacency)


def tile_sums(slot_at, dest_of, sorted_tiles, msgs, root_term, ahead=2):
    places = sorted_tiles.shape[0]
    chunk = GROUP * GROUP_CHUNK
    steps = places // chunk

    def kernel(
        slot_ref, dest_ref, root_hbm, tile_hbm, msg_hbm, out_hbm,
        tile_ref, msg_ref, root_ref, out_ref, acc_ref, tile_sem, sem,
    ):
        load = pltpu.make_async_copy(msg_hbm, msg_ref, sem.at[0])
        load.start()
        copies = [
            pltpu.make_async_copy(
                tile_hbm.at[pl.ds(i * chunk, chunk)],
                tile_ref.at[pl.ds(i * chunk, chunk)],
                tile_sem.at[i],
            )
            for i in range(steps)
        ]
        for i in range(min(ahead, steps)):
            copies[i].start()
        root = pltpu.make_async_copy(root_hbm, root_ref, sem.at[1])
        acc_ref[...] = jnp.zeros_like(acc_ref)
        load.wait()
        for i in range(steps):
            if i + ahead < steps:
                copies[i + ahead].start()
            if i == min(1, steps - 1):
                root.start()
            copies[i].wait()
            for g in range(i * GROUP_CHUNK, (i + 1) * GROUP_CHUNK):
                at = range(g * GROUP, (g + 1) * GROUP)
                left = jnp.concatenate([tile_ref[p] for p in at], axis=1)
                right = jnp.concatenate([msg_ref[slot_ref[p]] for p in at], axis=0)
                acc_ref[dest_ref[g]] += jnp.dot(left, right, preferred_element_type=F32)
        root.wait()
        out_ref[...] = (acc_ref[...] + root_ref[...]).astype(BF16)
        store = pltpu.make_async_copy(out_ref, out_hbm, sem.at[2])
        store.start()
        store.wait()

    anywhere = pl.BlockSpec(memory_space=pl.ANY)
    return pl.pallas_call(
        kernel,
        name="tile_sums",
        out_shape=pltpu.HBM(root_term.shape, BF16),
        grid_spec=pltpu.PrefetchScalarGridSpec(
            num_scalar_prefetch=2,
            grid=(1,),
            in_specs=[anywhere, anywhere, anywhere],
            out_specs=anywhere,
            scratch_shapes=[
                pltpu.VMEM(sorted_tiles.shape, BF16),
                pltpu.VMEM(msgs.shape, BF16),
                pltpu.VMEM(root_term.shape, F32),
                pltpu.VMEM(root_term.shape, BF16),
                pltpu.VMEM(root_term.shape, F32),
                pltpu.SemaphoreType.DMA((steps,)),
                pltpu.SemaphoreType.DMA((3,)),
            ],
        ),
        compiler_params=params(),
    )(in_hbm(slot_at), in_hbm(dest_of), in_hbm(root_term), sorted_tiles, in_hbm(msgs))


def relation_of(ref, c):
    return jnp.max(ref[:, c * BLK : (c + 1) * BLK].astype(F32)).astype(jnp.int32)


def select_blocks(slot_block, returned, blocks, nblocks, capacity):
    shards, _, width = returned.shape

    def kernel(block_ref, ret_ref, in_hbm_ref, out_ref, rel_ref, in_ref, load_ref, sem_ref):
        rows = pltpu.make_async_copy(
            ret_ref.at[:, pl.ds(capacity * BLK, 8), :], rel_ref, load_ref.at[0]
        )
        rows.start()
        load = pltpu.make_async_copy(in_hbm_ref, in_ref, load_ref.at[1])
        load.start()
        rows.wait()
        rels = [[relation_of(rel_ref[o], c) for c in range(capacity)] for o in range(shards)]
        load.wait()
        copies = []
        for o in range(shards):
            for c in range(capacity):
                key = rels[o][c] * nblocks + block_ref[c, o]
                copy = pltpu.make_async_copy(
                    in_ref.at[key], out_ref.at[o, pl.ds(c * BLK, BLK)], sem_ref.at[o, c]
                )
                copy.start()
                copies.append(copy)
        for copy in copies:
            copy.wait()

    return pl.pallas_call(
        kernel,
        name="select_blocks",
        out_shape=pltpu.HBM((shards, capacity * BLK, width), BF16),
        grid_spec=pltpu.PrefetchScalarGridSpec(
            num_scalar_prefetch=1,
            grid=(1,),
            in_specs=[
                pl.BlockSpec(memory_space=pl.ANY),
                pl.BlockSpec(memory_space=pl.ANY),
            ],
            out_specs=pl.BlockSpec(memory_space=pl.ANY),
            scratch_shapes=[
                pltpu.VMEM((shards, 8, width), BF16),
                pltpu.VMEM(blocks.shape, BF16),
                pltpu.SemaphoreType.DMA((2,)),
                pltpu.SemaphoreType.DMA((shards, capacity)),
            ],
        ),
        compiler_params=params(),
    )(in_hbm(slot_block), returned, in_hbm(blocks))


def sum_by_key(slot_block, returned, relations, nblocks, chunk=8):
    shards, rows, width = returned.shape
    capacity = slot_block.shape[0]
    bins = relations * nblocks

    def kernel(block_ref, ret_ref, out_ref, acc_ref):
        step = pl.program_id(0)

        @pl.when(step == 0)
        def _():
            acc_ref[...] = jnp.zeros_like(acc_ref)

        for u in range(chunk):
            for c in range(capacity):
                rel = relation_of(ret_ref[u, pl.ds(capacity * BLK, 8), :], c)
                key = rel * nblocks + block_ref[c, step * chunk + u]
                acc_ref[key] += ret_ref[u, pl.ds(c * BLK, BLK), :].astype(F32)

        @pl.when(step == pl.num_programs(0) - 1)
        def _():
            out_ref[...] = acc_ref[...].astype(BF16)

    return pl.pallas_call(
        kernel,
        name="sum_by_key",
        out_shape=pltpu.HBM((bins, BLK, width), BF16),
        grid_spec=pltpu.PrefetchScalarGridSpec(
            num_scalar_prefetch=1,
            grid=(shards // chunk,),
            in_specs=[pl.BlockSpec((chunk, rows, width), lambda i, *_: (i, 0, 0))],
            out_specs=whole((bins, BLK, width)),
            scratch_shapes=[pltpu.VMEM((bins, BLK, width), F32)],
        ),
        compiler_params=params(),
    )(slot_block, returned)


def weight_grads(coef, feats, source_grads, d_out, bases, chunk=128):
    relations, nodes, width = source_grads.shape
    nbase, width_in, _ = bases.shape

    def kernel(coef_ref, feat_ref, src_ref, grad_ref, base_ref, out_ref, dots_ref, acc_ref):
        @pl.when(pl.program_id(0) == 0)
        def _():
            acc_ref[...] = jnp.zeros_like(acc_ref)

        cols = feat_ref[...].T
        for r in range(relations):
            g = jnp.dot(cols, src_ref[r], preferred_element_type=F32)
            for b in range(nbase):
                scaled = coef_ref[r * nbase + b] * g
                if r == 0:
                    out_ref[b] = scaled
                else:
                    out_ref[b] += scaled
                prod = g * base_ref[b].astype(F32)
                acc_ref[r * nbase + b] += jnp.sum(prod.reshape(-1, 8, width), axis=0)
        out_ref[nbase] = jnp.dot(cols, grad_ref[...], preferred_element_type=F32)

        @pl.when(pl.program_id(0) == pl.num_programs(0) - 1)
        def _():
            row = lax.broadcasted_iota(jnp.int32, (8, BLK), 0)
            lane = lax.broadcasted_iota(jnp.int32, (8, BLK), 1)
            tile = jnp.zeros((8, BLK), F32)
            for r in range(relations):
                for b in range(nbase):
                    total = jnp.sum(acc_ref[r * nbase + b])
                    tile = jnp.where((row == b) & (lane == r), total, tile)
            dots_ref[...] = tile

    return pl.pallas_call(
        kernel,
        name="weight_grads",
        cost_estimate=pl.CostEstimate(
            flops=2 * (relations + 1) * nodes * width_in * width,
            transcendentals=0,
            bytes_accessed=2 * nodes * (width_in + (relations + 1) * width)
            + 6 * (nbase + 1) * width_in * width,
        ),
        out_shape=(
            jax.ShapeDtypeStruct((nbase + 1, width_in, width), F32),
            jax.ShapeDtypeStruct((8, BLK), F32),
        ),
        grid_spec=pltpu.PrefetchScalarGridSpec(
            num_scalar_prefetch=1,
            grid=(width_in // chunk,),
            in_specs=[
                pl.BlockSpec((nodes, chunk), lambda i, *_: (0, i)),
                whole(source_grads.shape),
                whole(d_out.shape),
                pl.BlockSpec((nbase, chunk, width), lambda i, *_: (0, i, 0)),
            ],
            out_specs=(
                pl.BlockSpec((nbase + 1, chunk, width), lambda i, *_: (0, i, 0)),
                whole((8, BLK)),
            ),
            scratch_shapes=[pltpu.VMEM((relations * nbase, 8, width), F32)],
        ),
        compiler_params=params(),
    )(coef, feats, source_grads, d_out, bases)


def exchange(x, axis, mask):
    return lax.ppermute(x, axis, [(i, i ^ mask) for i in range(lax.axis_size(axis))])


def chunk_of(x, at, dim):
    return lax.dynamic_index_in_dim(x, at, dim, keepdims=False)


def two_terms(x):
    high = x.astype(BF16)
    low = (x - high.astype(F32)).astype(BF16)
    return high, low


def sum_terms(x):
    return x[:, :BLK].astype(F32) + x[:, BLK:].astype(F32)


def first_stage(place, stacked, got, dots, size):
    parts, _, rest, _, rows, width = stacked.shape
    length = parts * rest * rows

    def kernel(place_ref, own_ref, got_ref, dots_ref, keep_ref, *send_refs):
        core = place_ref[0]
        at = place_ref[1]
        high, low = two_terms(dots_ref[...])
        for k in range(size):
            for p in range(parts):
                for q in range(rest):
                    value = own_ref[p, at ^ k, q, core] + got_ref[p, at ^ k, q].astype(F32)
                    if k == 0:
                        keep_ref[p, q] = value
                    else:
                        send_refs[k - 1][pl.ds((p * rest + q) * rows, rows), :] = value.astype(BF16)
            if k:
                send_refs[k - 1][pl.ds(length, 8), pl.ds(0, BLK)] = high
                send_refs[k - 1][pl.ds(length, 8), pl.ds(BLK, BLK)] = low

    sent = (length + 8, width)
    return pl.pallas_call(
        kernel,
        name="first_stage",
        out_shape=(jax.ShapeDtypeStruct((parts, rest, rows, width), F32),)
        + (jax.ShapeDtypeStruct(sent, BF16),) * (size - 1),
        grid_spec=pltpu.PrefetchScalarGridSpec(
            num_scalar_prefetch=1,
            grid=(1,),
            in_specs=[whole(stacked.shape), whole(got.shape), whole(dots.shape)],
            out_specs=(whole((parts, rest, rows, width)),) + (whole(sent),) * (size - 1),
        ),
        compiler_params=params(),
    )(place, stacked, got, dots)


def second_stage(place, kept, dots, got, size):
    parts, _, rows, width = kept.shape
    length = parts * rows

    def kernel(place_ref, own_ref, dots_ref, *refs):
        gots = refs[: len(got)]
        keep_ref, all_ref = refs[len(got) : len(got) + 2]
        send_refs = refs[len(got) + 2 :]
        at = place_ref[2]
        high, low = two_terms(dots_ref[...])
        sums = [high.astype(F32) + low.astype(F32)]
        sums += [sum_terms(g[pl.ds(length * size, 8), :]) for g in gots]
        while len(sums) > 1:
            sums = [sums[i] + sums[i + 1] for i in range(0, len(sums), 2)]
        all_ref[...] = sums[0]
        high, low = two_terms(sums[0])
        for k in range(size):
            for p in range(parts):
                value = own_ref[p, at ^ k]
                start = pl.multiple_of((p * size + (at ^ k)) * rows, 8)
                for g in gots:
                    value = value + g[pl.ds(start, rows), :].astype(F32)
                if k == 0:
                    keep_ref[p] = value
                else:
                    send_refs[k - 1][pl.ds(p * rows, rows), :] = value.astype(BF16)
            if k:
                send_refs[k - 1][pl.ds(length, 8), pl.ds(0, BLK)] = high
                send_refs[k - 1][pl.ds(length, 8), pl.ds(BLK, BLK)] = low

    sent = (length + 8, width)
    return pl.pallas_call(
        kernel,
        name="second_stage",
        out_shape=(
            jax.ShapeDtypeStruct((parts, rows, width), F32),
            jax.ShapeDtypeStruct((8, BLK), F32),
        )
        + (jax.ShapeDtypeStruct(sent, BF16),) * (size - 1),
        grid_spec=pltpu.PrefetchScalarGridSpec(
            num_scalar_prefetch=1,
            grid=(1,),
            in_specs=[whole(kept.shape), whole(dots.shape)] + [whole(g.shape) for g in got],
            out_specs=(whole((parts, rows, width)), whole((8, BLK))) + (whole(sent),) * (size - 1),
        ),
        compiler_params=params(),
    )(place, kept, dots, *got)


def last_stage(kept, dots, got, relations):
    parts, rows, width = kept.shape
    length = parts * rows
    nbase = parts - 1

    def kernel(own_ref, dots_ref, *refs):
        gots = refs[: len(got)]
        bases_ref, root_ref, coef_ref = refs[len(got) :]
        high, low = two_terms(dots_ref[...])
        sums = [high.astype(F32) + low.astype(F32)]
        sums += [sum_terms(g[pl.ds(length, 8), :]) for g in gots]
        while len(sums) > 1:
            sums = [sums[i] + sums[i + 1] for i in range(0, len(sums), 2)]
        coef_ref[...] = sums[0][:nbase, :relations]
        for p in range(parts):
            value = own_ref[p]
            for g in gots:
                value = value + g[pl.ds(p * rows, rows), :].astype(F32)
            if p < nbase:
                bases_ref[p] = value
            else:
                root_ref[...] = value

    shapes = ((nbase, rows, width), (rows, width), (nbase, relations))
    return pl.pallas_call(
        kernel,
        name="last_stage",
        out_shape=tuple(jax.ShapeDtypeStruct(x, F32) for x in shapes),
        grid=(1,),
        in_specs=[whole(kept.shape), whole(dots.shape)] + [whole(g.shape) for g in got],
        out_specs=tuple(whole(x) for x in shapes),
        compiler_params=params(),
    )(kept, dots, *got)


def body(
    feats, bases, coef, root_weight, slot_block, recv_rel, tile_slot, tile_dst, tile_adj, d_out
):
    shards = lax.axis_size("shard")
    reps = lax.axis_size("rep")
    me = lax.axis_index("shard")
    my_rep = lax.axis_index("rep")
    nblocks = feats.shape[0] // BLK
    width_in = feats.shape[1]
    width = root_weight.shape[1]
    relations, nbase = coef.shape
    capacity = slot_block.shape[2]
    slots = shards * capacity

    slot_grads = tile_grads(
        tile_slot[0],
        tile_dst[0],
        recv_rel[0].T,
        tile_adj[0],
        d_out.reshape(nblocks, BLK, width),
        shards,
    )
    returned = lax.all_to_all(slot_grads, "shard", 0, 0, tiled=True)

    rel_weights = (
        jnp.dot(coef, bases.reshape(nbase, -1), preferred_element_type=F32)
        .astype(BF16)
        .reshape(relations, width_in, width)
    )
    projected = project(feats, rel_weights, nblocks)
    root_term = jnp.dot(feats, root_weight, preferred_element_type=F32)

    tile_at, slot_at, dest_of = group_tables(tile_slot[0], tile_dst[0], nblocks)
    sorted_tiles = sort_tiles(tile_at, tile_adj[0])
    returned, sorted_tiles, slot_at, dest_of = lax.optimization_barrier(
        (returned, sorted_tiles, slot_at, dest_of)
    )
    requested = slot_block[0].T
    outgoing = select_blocks(requested, returned, projected, nblocks, capacity)
    outgoing, returned = lax.optimization_barrier((outgoing, returned))
    incoming = lax.all_to_all(outgoing, "shard", 0, 0, tiled=True)

    source_grads = sum_by_key(requested, returned, relations, nblocks)
    source_grads = source_grads.reshape(relations, nblocks * BLK, width)
    through = jnp.einsum("rno,rco->nc", source_grads, rel_weights, preferred_element_type=F32)
    through = through + jnp.dot(d_out, root_weight.T, preferred_element_type=F32)
    through = through.reshape(reps, -1, width_in)
    parts = [chunk_of(through, my_rep ^ k, 0).astype(BF16) for k in range(1, reps)]
    stacked, dots = weight_grads(
        coef.astype(F32).reshape(-1), feats, source_grads, d_out, bases
    )
    dots = dots + exchange(dots, "shard", 1)
    for step in (1, 2):
        dots = dots + exchange(dots, "rep", step)

    dots, *parts = lax.optimization_barrier((dots, *parts))
    grad_feats = chunk_of(through, my_rep, 0)
    for k, part in zip(range(1, reps), parts):
        grad_feats = grad_feats + exchange(part, "rep", k).astype(F32)
    grad_feats = grad_feats.astype(BF16)

    rows = width_in // shards
    stacked = stacked.reshape(nbase + 1, 4, 4, 2, rows, width)
    place = jnp.stack([me & 1, (me >> 3) & 3, (me >> 1) & 3]).astype(jnp.int32)
    got = exchange(chunk_of(stacked, (me & 1) ^ 1, 3).astype(BF16), "shard", 1)
    kept, *sends = first_stage(place, stacked, got, dots, 4)
    got = [exchange(x, "shard", k << 3) for k, x in zip((1, 2, 3), sends)]
    output = tile_sums(
        slot_at,
        dest_of,
        sorted_tiles,
        incoming.reshape(slots, BLK, width),
        root_term.reshape(nblocks, BLK, width),
    ).reshape(nblocks * BLK, width)
    output, grad_feats, kept = lax.optimization_barrier((output, grad_feats, kept))
    kept, dots, *sends = second_stage(place, kept, dots, got, 4)
    got = [exchange(x, "shard", k << 1) for k, x in zip((1, 2, 3), sends)]
    grad_bases, grad_root, grad_coef = last_stage(kept, dots, got, relations)
    return (output, grad_feats, grad_bases, grad_root, grad_coef.T)


def solution(mesh):
    placed = (
        P("shard", None),
        P(None, None, "rep"),
        P(),
        P(None, "rep"),
        P("shard", None, None),
        P("shard", None, None),
        P("shard", None),
        P("shard", None),
        P("shard", None, None, None),
        P("shard", "rep"),
    )
    return jax.shard_map(
        body,
        mesh=mesh,
        in_specs=placed,
        out_specs=(
            P("shard", "rep"),
            P(("shard", "rep"), None),
            P(None, "shard", "rep"),
            P("shard", "rep"),
            P(),
        ),
        check_vma=False,
    )
```

```python
import jax
import jax.numpy as jnp
from jax import lax
from jax.experimental import pallas as pl
from jax.experimental.pallas import tpu as pltpu
from jax.sharding import PartitionSpec as P

BLK = 128
F32 = jnp.float32
BF16 = jnp.bfloat16
VMEM_LIMIT = 48 * 1024 * 1024
GROUP = 4
GROUP_CHUNK = 12


def params():
    return pltpu.CompilerParams(vmem_limit_bytes=VMEM_LIMIT)


def in_hbm(x):
    return pltpu.with_memory_space_constraint(x, pltpu.HBM)


def whole(shape):
    return pl.BlockSpec(shape, lambda *_: (0,) * len(shape))


def tile_grads(tile_ids, dest_ids, rels, adjacency, grads, shards, chunk=64):
    tiles = adjacency.shape[0]
    nblocks, _, width = grads.shape
    capacity = rels.shape[0]
    slots = shards * capacity
    rows = capacity * BLK + 8

    def kernel(slot_ref, dst_ref, rel_ref, adj_ref, grad_ref, out_ref, acc_ref):
        step = pl.program_id(0)

        @pl.when(step == 0)
        def _():
            acc_ref[...] = jnp.zeros_like(acc_ref)

        for u in range(chunk):
            t = step * chunk + u
            part = lax.dot_general(
                adj_ref[u],
                grad_ref[dst_ref[t]],
                (((0,), (0,)), ((), ())),
                preferred_element_type=F32,
            )
            acc_ref[slot_ref[t]] += part

        @pl.when(step == pl.num_programs(0) - 1)
        def _():
            lane = lax.broadcasted_iota(jnp.int32, (8, width), 1)
            for o in range(shards):
                tail = jnp.zeros((8, width), F32)
                for c in range(capacity):
                    s = o * capacity + c
                    out_ref[o, pl.ds(c * BLK, BLK), :] = acc_ref[s].astype(BF16)
                    tail = jnp.where(lane // BLK == c, rel_ref[c, o].astype(F32), tail)
                out_ref[o, pl.ds(capacity * BLK, 8), :] = tail.astype(BF16)

    return pl.pallas_call(
        kernel,
        name="tile_grads",
        out_shape=pltpu.HBM((shards, rows, width), BF16),
        grid_spec=pltpu.PrefetchScalarGridSpec(
            num_scalar_prefetch=3,
            grid=(tiles // chunk,),
            in_specs=[
                pl.BlockSpec((chunk, BLK, BLK), lambda i, *_: (i, 0, 0)),
                whole(grads.shape),
            ],
            out_specs=whole((shards, rows, width)),
            scratch_shapes=[pltpu.VMEM((slots, BLK, width), F32)],
        ),
        compiler_params=params(),
    )(in_hbm(tile_ids), in_hbm(dest_ids), in_hbm(rels), adjacency, in_hbm(grads))


def project(feats, rel_weights, nblocks):
    relations, _, width = rel_weights.shape

    def kernel(feat_ref, w_ref, out_ref):
        for b in range(nblocks):
            out_ref[b] = jnp.dot(
                feat_ref[pl.ds(b * BLK, BLK), :], w_ref[0], preferred_element_type=F32
            ).astype(BF16)

    return pl.pallas_call(
        kernel,
        name="project",
        out_shape=pltpu.HBM((relations * nblocks, BLK, width), BF16),
        grid=(relations,),
        in_specs=[
            whole(feats.shape),
            pl.BlockSpec((1,) + rel_weights.shape[1:], lambda r: (r, 0, 0)),
        ],
        out_specs=pl.BlockSpec((nblocks, BLK, width), lambda r: (r, 0, 0)),
        compiler_params=params(),
    )(feats, rel_weights)


def group_tables(tile_ids, dest_ids, nblocks):
    tiles = tile_ids.shape[0]
    groups = -(-(tiles + nblocks * (GROUP - 1)) // GROUP)
    groups = -(-groups // GROUP_CHUNK) * GROUP_CHUNK
    index = jnp.arange(tiles)
    hot = (dest_ids[:, None] == jnp.arange(nblocks)[None, :]).astype(jnp.int32)
    sizes = (jnp.sum(hot, axis=0) + GROUP - 1) // GROUP
    blocks = jnp.arange(nblocks)
    ends = jnp.sum(jnp.where(blocks[:, None] <= blocks[None, :], sizes[:, None], 0), axis=0)
    same = dest_ids[:, None] == dest_ids[None, :]
    rank = jnp.sum((same & (index[None, :] < index[:, None])).astype(jnp.int32), axis=1)
    place = jnp.sum(hot * (ends - sizes)[None, :], axis=1) * GROUP + rank
    here = place[None, :] == jnp.arange(groups * GROUP)[:, None]
    tile_at = jnp.sum(jnp.where(here, index[None, :] + 1, 0), axis=1) - 1
    slot_at = jnp.sum(jnp.where(here, tile_ids[None, :], 0), axis=1)
    passed = (jnp.arange(groups)[:, None] >= ends[None, :]).astype(jnp.int32)
    dest_of = jnp.minimum(jnp.sum(passed, axis=1), nblocks - 1)
    return tile_at.astype(jnp.int32), slot_at.astype(jnp.int32), dest_of.astype(jnp.int32)


def sort_tiles(tile_at, adjacency, chunk=GROUP * GROUP_CHUNK):
    places = tile_at.shape[0]

    def kernel(at_ref, adj_ref, out_ref):
        step = pl.program_id(0)
        for u in range(chunk):
            t = at_ref[step * chunk + u]

            @pl.when(t >= 0)
            def _():
                out_ref[u] = adj_ref[jnp.maximum(t, 0)]

            @pl.when(t < 0)
            def _():
                out_ref[u] = jnp.zeros((BLK, BLK), BF16)

    return pl.pallas_call(
        kernel,
        name="sort_tiles",
        out_shape=pltpu.HBM((places, BLK, BLK), BF16),
        grid_spec=pltpu.PrefetchScalarGridSpec(
            num_scalar_prefetch=1,
            grid=(places // chunk,),
            in_specs=[whole(adjacency.shape)],
            out_specs=pl.BlockSpec((chunk, BLK, BLK), lambda i, *_: (i, 0, 0)),
        ),
        compiler_params=params(),
    )(tile_at, adjacency)


def tile_sums(slot_at, dest_of, sorted_tiles, msgs, root_term, ahead=2):
    places = sorted_tiles.shape[0]
    chunk = GROUP * GROUP_CHUNK
    steps = places // chunk

    def kernel(
        slot_ref, dest_ref, root_hbm, tile_hbm, msg_hbm, out_hbm,
        tile_ref, msg_ref, root_ref, out_ref, acc_ref, tile_sem, sem,
    ):
        load = pltpu.make_async_copy(msg_hbm, msg_ref, sem.at[0])
        load.start()
        copies = [
            pltpu.make_async_copy(
                tile_hbm.at[pl.ds(i * chunk, chunk)],
                tile_ref.at[pl.ds(i * chunk, chunk)],
                tile_sem.at[i],
            )
            for i in range(steps)
        ]
        for i in range(min(ahead, steps)):
            copies[i].start()
        root = pltpu.make_async_copy(root_hbm, root_ref, sem.at[1])
        acc_ref[...] = jnp.zeros_like(acc_ref)
        load.wait()
        for i in range(steps):
            if i + ahead < steps:
                copies[i + ahead].start()
            if i == min(1, steps - 1):
                root.start()
            copies[i].wait()
            for g in range(i * GROUP_CHUNK, (i + 1) * GROUP_CHUNK):
                at = range(g * GROUP, (g + 1) * GROUP)
                left = jnp.concatenate([tile_ref[p] for p in at], axis=1)
                right = jnp.concatenate([msg_ref[slot_ref[p]] for p in at], axis=0)
                acc_ref[dest_ref[g]] += jnp.dot(left, right, preferred_element_type=F32)
        root.wait()
        out_ref[...] = (acc_ref[...] + root_ref[...]).astype(BF16)
        store = pltpu.make_async_copy(out_ref, out_hbm, sem.at[2])
        store.start()
        store.wait()

    anywhere = pl.BlockSpec(memory_space=pl.ANY)
    return pl.pallas_call(
        kernel,
        name="tile_sums",
        out_shape=pltpu.HBM(root_term.shape, BF16),
        grid_spec=pltpu.PrefetchScalarGridSpec(
            num_scalar_prefetch=2,
            grid=(1,),
            in_specs=[anywhere, anywhere, anywhere],
            out_specs=anywhere,
            scratch_shapes=[
                pltpu.VMEM(sorted_tiles.shape, BF16),
                pltpu.VMEM(msgs.shape, BF16),
                pltpu.VMEM(root_term.shape, F32),
                pltpu.VMEM(root_term.shape, BF16),
                pltpu.VMEM(root_term.shape, F32),
                pltpu.SemaphoreType.DMA((steps,)),
                pltpu.SemaphoreType.DMA((3,)),
            ],
        ),
        compiler_params=params(),
    )(in_hbm(slot_at), in_hbm(dest_of), in_hbm(root_term), sorted_tiles, in_hbm(msgs))


def relation_of(ref, c):
    return jnp.max(ref[:, c * BLK : (c + 1) * BLK].astype(F32)).astype(jnp.int32)


def select_blocks(slot_block, returned, blocks, nblocks, capacity):
    shards, _, width = returned.shape

    def kernel(block_ref, ret_ref, in_hbm_ref, out_ref, rel_ref, in_ref, load_ref, sem_ref):
        rows = pltpu.make_async_copy(
            ret_ref.at[:, pl.ds(capacity * BLK, 8), :], rel_ref, load_ref.at[0]
        )
        rows.start()
        load = pltpu.make_async_copy(in_hbm_ref, in_ref, load_ref.at[1])
        load.start()
        rows.wait()
        rels = [[relation_of(rel_ref[o], c) for c in range(capacity)] for o in range(shards)]
        load.wait()
        copies = []
        for o in range(shards):
            for c in range(capacity):
                key = rels[o][c] * nblocks + block_ref[c, o]
                copy = pltpu.make_async_copy(
                    in_ref.at[key], out_ref.at[o, pl.ds(c * BLK, BLK)], sem_ref.at[o, c]
                )
                copy.start()
                copies.append(copy)
        for copy in copies:
            copy.wait()

    return pl.pallas_call(
        kernel,
        name="select_blocks",
        out_shape=pltpu.HBM((shards, capacity * BLK, width), BF16),
        grid_spec=pltpu.PrefetchScalarGridSpec(
            num_scalar_prefetch=1,
            grid=(1,),
            in_specs=[
                pl.BlockSpec(memory_space=pl.ANY),
                pl.BlockSpec(memory_space=pl.ANY),
            ],
            out_specs=pl.BlockSpec(memory_space=pl.ANY),
            scratch_shapes=[
                pltpu.VMEM((shards, 8, width), BF16),
                pltpu.VMEM(blocks.shape, BF16),
                pltpu.SemaphoreType.DMA((2,)),
                pltpu.SemaphoreType.DMA((shards, capacity)),
            ],
        ),
        compiler_params=params(),
    )(in_hbm(slot_block), returned, in_hbm(blocks))


def sum_by_key(slot_block, returned, relations, nblocks, chunk=8):
    shards, rows, width = returned.shape
    capacity = slot_block.shape[0]
    bins = relations * nblocks

    def kernel(block_ref, ret_ref, out_ref, acc_ref):
        step = pl.program_id(0)

        @pl.when(step == 0)
        def _():
            acc_ref[...] = jnp.zeros_like(acc_ref)

        for u in range(chunk):
            for c in range(capacity):
                rel = relation_of(ret_ref[u, pl.ds(capacity * BLK, 8), :], c)
                key = rel * nblocks + block_ref[c, step * chunk + u]
                acc_ref[key] += ret_ref[u, pl.ds(c * BLK, BLK), :].astype(F32)

        @pl.when(step == pl.num_programs(0) - 1)
        def _():
            out_ref[...] = acc_ref[...].astype(BF16)

    return pl.pallas_call(
        kernel,
        name="sum_by_key",
        out_shape=pltpu.HBM((bins, BLK, width), BF16),
        grid_spec=pltpu.PrefetchScalarGridSpec(
            num_scalar_prefetch=1,
            grid=(shards // chunk,),
            in_specs=[pl.BlockSpec((chunk, rows, width), lambda i, *_: (i, 0, 0))],
            out_specs=whole((bins, BLK, width)),
            scratch_shapes=[pltpu.VMEM((bins, BLK, width), F32)],
        ),
        compiler_params=params(),
    )(slot_block, returned)


def weight_grads(coef, feats, source_grads, d_out, bases, chunk=128):
    relations, nodes, width = source_grads.shape
    nbase, width_in, _ = bases.shape

    def kernel(coef_ref, feat_ref, src_ref, grad_ref, base_ref, out_ref, dots_ref, acc_ref):
        @pl.when(pl.program_id(0) == 0)
        def _():
            acc_ref[...] = jnp.zeros_like(acc_ref)

        cols = feat_ref[...].T
        for r in range(relations):
            g = jnp.dot(cols, src_ref[r], preferred_element_type=F32)
            for b in range(nbase):
                scaled = coef_ref[r * nbase + b] * g
                if r == 0:
                    out_ref[b] = scaled
                else:
                    out_ref[b] += scaled
                prod = g * base_ref[b].astype(F32)
                acc_ref[r * nbase + b] += jnp.sum(prod.reshape(-1, 8, width), axis=0)
        out_ref[nbase] = jnp.dot(cols, grad_ref[...], preferred_element_type=F32)

        @pl.when(pl.program_id(0) == pl.num_programs(0) - 1)
        def _():
            row = lax.broadcasted_iota(jnp.int32, (8, BLK), 0)
            lane = lax.broadcasted_iota(jnp.int32, (8, BLK), 1)
            tile = jnp.zeros((8, BLK), F32)
            for r in range(relations):
                for b in range(nbase):
                    total = jnp.sum(acc_ref[r * nbase + b])
                    tile = jnp.where((row == b) & (lane == r), total, tile)
            dots_ref[...] = tile

    return pl.pallas_call(
        kernel,
        name="weight_grads",
        cost_estimate=pl.CostEstimate(
            flops=2 * (relations + 1) * nodes * width_in * width,
            transcendentals=0,
            bytes_accessed=2 * nodes * (width_in + (relations + 1) * width)
            + 6 * (nbase + 1) * width_in * width,
        ),
        out_shape=(
            jax.ShapeDtypeStruct((nbase + 1, width_in, width), F32),
            jax.ShapeDtypeStruct((8, BLK), F32),
        ),
        grid_spec=pltpu.PrefetchScalarGridSpec(
            num_scalar_prefetch=1,
            grid=(width_in // chunk,),
            in_specs=[
                pl.BlockSpec((nodes, chunk), lambda i, *_: (0, i)),
                whole(source_grads.shape),
                whole(d_out.shape),
                pl.BlockSpec((nbase, chunk, width), lambda i, *_: (0, i, 0)),
            ],
            out_specs=(
                pl.BlockSpec((nbase + 1, chunk, width), lambda i, *_: (0, i, 0)),
                whole((8, BLK)),
            ),
            scratch_shapes=[pltpu.VMEM((relations * nbase, 8, width), F32)],
        ),
        compiler_params=params(),
    )(coef, feats, source_grads, d_out, bases)


def exchange(x, axis, mask):
    return lax.ppermute(x, axis, [(i, i ^ mask) for i in range(lax.axis_size(axis))])


def chunk_of(x, at, dim):
    return lax.dynamic_index_in_dim(x, at, dim, keepdims=False)


def two_terms(x):
    high = x.astype(BF16)
    low = (x - high.astype(F32)).astype(BF16)
    return high, low


def sum_terms(x):
    return x[:, :BLK].astype(F32) + x[:, BLK:].astype(F32)


def first_stage(place, stacked, got, dots, size):
    parts, _, rest, _, rows, width = stacked.shape
    length = parts * rest * rows

    def kernel(place_ref, own_ref, got_ref, dots_ref, keep_ref, *send_refs):
        core = place_ref[0]
        high, low = two_terms(dots_ref[...])
        for k in range(size):
            role = (place_ref[1] ^ (k >> 1), place_ref[2] ^ (k & 1))
            for p in range(parts):
                for q in range(rest):
                    first = 3 - role[0] if q >> 1 else role[0]
                    second = 3 - role[1] if q & 1 else role[1]
                    value = own_ref[p, first, second, core]
                    value = value + got_ref[p, first, second].astype(F32)
                    if k == 0:
                        keep_ref[p, q] = value
                    else:
                        send_refs[k - 1][pl.ds((p * rest + q) * rows, rows), :] = value.astype(BF16)
            if k:
                send_refs[k - 1][pl.ds(length, 8), pl.ds(0, BLK)] = high
                send_refs[k - 1][pl.ds(length, 8), pl.ds(BLK, BLK)] = low

    sent = (length + 8, width)
    return pl.pallas_call(
        kernel,
        name="first_stage",
        out_shape=(jax.ShapeDtypeStruct((parts, rest, rows, width), F32),)
        + (jax.ShapeDtypeStruct(sent, BF16),) * (size - 1),
        grid_spec=pltpu.PrefetchScalarGridSpec(
            num_scalar_prefetch=1,
            grid=(1,),
            in_specs=[whole(stacked.shape), whole(got.shape), whole(dots.shape)],
            out_specs=(whole((parts, rest, rows, width)),) + (whole(sent),) * (size - 1),
        ),
        compiler_params=params(),
    )(place, stacked, got, dots)


def second_stage(place, kept, dots, got, size):
    parts, _, rows, width = kept.shape
    length = parts * rows

    def kernel(place_ref, own_ref, dots_ref, *refs):
        gots = refs[: len(got)]
        keep_ref, all_ref = refs[len(got) : len(got) + 2]
        send_refs = refs[len(got) + 2 :]
        at = place_ref[3]
        high, low = two_terms(dots_ref[...])
        sums = [high.astype(F32) + low.astype(F32)]
        sums += [sum_terms(g[pl.ds(length * size, 8), :]) for g in gots]
        while len(sums) > 1:
            sums = [sums[i] + sums[i + 1] for i in range(0, len(sums), 2)]
        all_ref[...] = sums[0]
        high, low = two_terms(sums[0])
        for k in range(size):
            for p in range(parts):
                value = own_ref[p, at ^ k]
                start = pl.multiple_of((p * size + (at ^ k)) * rows, 8)
                for g in gots:
                    value = value + g[pl.ds(start, rows), :].astype(F32)
                if k == 0:
                    keep_ref[p] = value
                else:
                    send_refs[k - 1][pl.ds(p * rows, rows), :] = value.astype(BF16)
            if k:
                send_refs[k - 1][pl.ds(length, 8), pl.ds(0, BLK)] = high
                send_refs[k - 1][pl.ds(length, 8), pl.ds(BLK, BLK)] = low

    sent = (length + 8, width)
    return pl.pallas_call(
        kernel,
        name="second_stage",
        out_shape=(
            jax.ShapeDtypeStruct((parts, rows, width), F32),
            jax.ShapeDtypeStruct((8, BLK), F32),
        )
        + (jax.ShapeDtypeStruct(sent, BF16),) * (size - 1),
        grid_spec=pltpu.PrefetchScalarGridSpec(
            num_scalar_prefetch=1,
            grid=(1,),
            in_specs=[whole(kept.shape), whole(dots.shape)] + [whole(g.shape) for g in got],
            out_specs=(whole((parts, rows, width)), whole((8, BLK))) + (whole(sent),) * (size - 1),
        ),
        compiler_params=params(),
    )(place, kept, dots, *got)


def last_stage(kept, dots, got, relations):
    parts, rows, width = kept.shape
    length = parts * rows
    nbase = parts - 1

    def kernel(own_ref, dots_ref, *refs):
        gots = refs[: len(got)]
        bases_ref, root_ref, coef_ref = refs[len(got) :]
        high, low = two_terms(dots_ref[...])
        sums = [high.astype(F32) + low.astype(F32)]
        sums += [sum_terms(g[pl.ds(length, 8), :]) for g in gots]
        while len(sums) > 1:
            sums = [sums[i] + sums[i + 1] for i in range(0, len(sums), 2)]
        coef_ref[...] = sums[0][:nbase, :relations]
        for p in range(parts):
            value = own_ref[p]
            for g in gots:
                value = value + g[pl.ds(p * rows, rows), :].astype(F32)
            if p < nbase:
                bases_ref[p] = value
            else:
                root_ref[...] = value

    shapes = ((nbase, rows, width), (rows, width), (nbase, relations))
    return pl.pallas_call(
        kernel,
        name="last_stage",
        out_shape=tuple(jax.ShapeDtypeStruct(x, F32) for x in shapes),
        grid=(1,),
        in_specs=[whole(kept.shape), whole(dots.shape)] + [whole(g.shape) for g in got],
        out_specs=tuple(whole(x) for x in shapes),
        compiler_params=params(),
    )(kept, dots, *got)


def body(
    feats, bases, coef, root_weight, slot_block, recv_rel, tile_slot, tile_dst, tile_adj, d_out
):
    shards = lax.axis_size("shard")
    reps = lax.axis_size("rep")
    me = lax.axis_index("shard")
    my_rep = lax.axis_index("rep")
    nblocks = feats.shape[0] // BLK
    width_in = feats.shape[1]
    width = root_weight.shape[1]
    relations, nbase = coef.shape
    capacity = slot_block.shape[2]
    slots = shards * capacity

    slot_grads = tile_grads(
        tile_slot[0],
        tile_dst[0],
        recv_rel[0].T,
        tile_adj[0],
        d_out.reshape(nblocks, BLK, width),
        shards,
    )
    returned = lax.all_to_all(slot_grads, "shard", 0, 0, tiled=True)

    rel_weights = (
        jnp.dot(coef, bases.reshape(nbase, -1), preferred_element_type=F32)
        .astype(BF16)
        .reshape(relations, width_in, width)
    )
    projected = project(feats, rel_weights, nblocks)
    root_term = jnp.dot(feats, root_weight, preferred_element_type=F32)

    tile_at, slot_at, dest_of = group_tables(tile_slot[0], tile_dst[0], nblocks)
    sorted_tiles = sort_tiles(tile_at, tile_adj[0])
    returned, sorted_tiles, slot_at, dest_of = lax.optimization_barrier(
        (returned, sorted_tiles, slot_at, dest_of)
    )
    requested = slot_block[0].T
    outgoing = select_blocks(requested, returned, projected, nblocks, capacity)
    outgoing, returned = lax.optimization_barrier((outgoing, returned))
    incoming = lax.all_to_all(outgoing, "shard", 0, 0, tiled=True)

    source_grads = sum_by_key(requested, returned, relations, nblocks)
    source_grads = source_grads.reshape(relations, nblocks * BLK, width)
    through = jnp.einsum("rno,rco->nc", source_grads, rel_weights, preferred_element_type=F32)
    through = through + jnp.dot(d_out, root_weight.T, preferred_element_type=F32)
    through = through.reshape(reps, -1, width_in)
    parts = [chunk_of(through, my_rep ^ k, 0).astype(BF16) for k in range(1, reps)]
    stacked, dots = weight_grads(
        coef.astype(F32).reshape(-1), feats, source_grads, d_out, bases
    )
    dots = dots + exchange(dots, "shard", 1)
    for step in (1, 2):
        dots = dots + exchange(dots, "rep", step)

    dots, *parts = lax.optimization_barrier((dots, *parts))
    grad_feats = chunk_of(through, my_rep, 0)
    for k, part in zip(range(1, reps), parts):
        grad_feats = grad_feats + exchange(part, "rep", k).astype(F32)
    grad_feats = grad_feats.astype(BF16)

    rows = width_in // shards
    stacked = stacked.reshape(nbase + 1, 4, 4, 2, rows, width)
    along = ((me >> 3) & 3, (me >> 1) & 3)
    role = [(i & 1) ^ (i >> 1) for i in along]
    place = jnp.stack([me & 1, *role, (along[0] >> 1) * 2 + (along[1] >> 1)]).astype(jnp.int32)
    got = exchange(chunk_of(stacked, (me & 1) ^ 1, 3).astype(BF16), "shard", 1)
    kept, *sends = first_stage(place, stacked, got, dots, 4)
    got = [exchange(x, "shard", k) for k, x in zip((2, 8, 10), sends)]
    output = tile_sums(
        slot_at,
        dest_of,
        sorted_tiles,
        incoming.reshape(slots, BLK, width),
        root_term.reshape(nblocks, BLK, width),
    ).reshape(nblocks * BLK, width)
    output, grad_feats, kept = lax.optimization_barrier((output, grad_feats, kept))
    kept, dots, *sends = second_stage(place, kept, dots, got, 4)
    got = [exchange(x, "shard", k) for k, x in zip((6, 24, 30), sends)]
    grad_bases, grad_root, grad_coef = last_stage(kept, dots, got, relations)
    return (output, grad_feats, grad_bases, grad_root, grad_coef.T)


def solution(mesh):
    placed = (
        P("shard", None),
        P(None, None, "rep"),
        P(),
        P(None, "rep"),
        P("shard", None, None),
        P("shard", None, None),
        P("shard", None),
        P("shard", None),
        P("shard", None, None, None),
        P("shard", "rep"),
    )
    return jax.shard_map(
        body,
        mesh=mesh,
        in_specs=placed,
        out_specs=(
            P("shard", "rep"),
            P(("shard", "rep"), None),
            P(None, "shard", "rep"),
            P("shard", "rep"),
            P(),
        ),
        check_vma=False,
    )
```

```python
import jax
import jax.numpy as jnp
from jax import lax
from jax.experimental import pallas as pl
from jax.experimental.pallas import tpu as pltpu
from jax.sharding import PartitionSpec as P

BLK = 128
F32 = jnp.float32
BF16 = jnp.bfloat16
VMEM_LIMIT = 48 * 1024 * 1024
GROUP = 4
GROUP_CHUNK = 12


def params():
    return pltpu.CompilerParams(vmem_limit_bytes=VMEM_LIMIT)


def in_hbm(x):
    return pltpu.with_memory_space_constraint(x, pltpu.HBM)


def whole(shape):
    return pl.BlockSpec(shape, lambda *_: (0,) * len(shape))


def tile_grads(tile_ids, dest_ids, rels, adjacency, grads, shards, chunk=64):
    tiles = adjacency.shape[0]
    nblocks, _, width = grads.shape
    capacity = rels.shape[0]
    slots = shards * capacity
    rows = capacity * BLK + 8

    def kernel(slot_ref, dst_ref, rel_ref, adj_ref, grad_ref, out_ref, acc_ref):
        step = pl.program_id(0)

        @pl.when(step == 0)
        def _():
            acc_ref[...] = jnp.zeros_like(acc_ref)

        for u in range(chunk):
            t = step * chunk + u
            part = lax.dot_general(
                adj_ref[u],
                grad_ref[dst_ref[t]],
                (((0,), (0,)), ((), ())),
                preferred_element_type=F32,
            )
            acc_ref[slot_ref[t]] += part

        @pl.when(step == pl.num_programs(0) - 1)
        def _():
            lane = lax.broadcasted_iota(jnp.int32, (8, width), 1)
            for o in range(shards):
                tail = jnp.zeros((8, width), F32)
                for c in range(capacity):
                    s = o * capacity + c
                    out_ref[o, pl.ds(c * BLK, BLK), :] = acc_ref[s].astype(BF16)
                    tail = jnp.where(lane // BLK == c, rel_ref[c, o].astype(F32), tail)
                out_ref[o, pl.ds(capacity * BLK, 8), :] = tail.astype(BF16)

    return pl.pallas_call(
        kernel,
        name="tile_grads",
        out_shape=pltpu.HBM((shards, rows, width), BF16),
        grid_spec=pltpu.PrefetchScalarGridSpec(
            num_scalar_prefetch=3,
            grid=(tiles // chunk,),
            in_specs=[
                pl.BlockSpec((chunk, BLK, BLK), lambda i, *_: (i, 0, 0)),
                whole(grads.shape),
            ],
            out_specs=whole((shards, rows, width)),
            scratch_shapes=[pltpu.VMEM((slots, BLK, width), F32)],
        ),
        compiler_params=params(),
    )(in_hbm(tile_ids), in_hbm(dest_ids), in_hbm(rels), adjacency, in_hbm(grads))


def project(feats, rel_weights, nblocks):
    relations, _, width = rel_weights.shape

    def kernel(feat_ref, w_ref, out_ref):
        for b in range(nblocks):
            out_ref[b] = jnp.dot(
                feat_ref[pl.ds(b * BLK, BLK), :], w_ref[0], preferred_element_type=F32
            ).astype(BF16)

    return pl.pallas_call(
        kernel,
        name="project",
        out_shape=pltpu.HBM((relations * nblocks, BLK, width), BF16),
        grid=(relations,),
        in_specs=[
            whole(feats.shape),
            pl.BlockSpec((1,) + rel_weights.shape[1:], lambda r: (r, 0, 0)),
        ],
        out_specs=pl.BlockSpec((nblocks, BLK, width), lambda r: (r, 0, 0)),
        compiler_params=params(),
    )(feats, rel_weights)


def group_tables(tile_ids, dest_ids, nblocks):
    tiles = tile_ids.shape[0]
    groups = -(-(tiles + nblocks * (GROUP - 1)) // GROUP)
    groups = -(-groups // GROUP_CHUNK) * GROUP_CHUNK
    index = jnp.arange(tiles)
    hot = (dest_ids[:, None] == jnp.arange(nblocks)[None, :]).astype(jnp.int32)
    sizes = (jnp.sum(hot, axis=0) + GROUP - 1) // GROUP
    blocks = jnp.arange(nblocks)
    ends = jnp.sum(jnp.where(blocks[:, None] <= blocks[None, :], sizes[:, None], 0), axis=0)
    same = dest_ids[:, None] == dest_ids[None, :]
    rank = jnp.sum((same & (index[None, :] < index[:, None])).astype(jnp.int32), axis=1)
    place = jnp.sum(hot * (ends - sizes)[None, :], axis=1) * GROUP + rank
    here = place[None, :] == jnp.arange(groups * GROUP)[:, None]
    tile_at = jnp.sum(jnp.where(here, index[None, :] + 1, 0), axis=1) - 1
    slot_at = jnp.sum(jnp.where(here, tile_ids[None, :], 0), axis=1)
    passed = (jnp.arange(groups)[:, None] >= ends[None, :]).astype(jnp.int32)
    dest_of = jnp.minimum(jnp.sum(passed, axis=1), nblocks - 1)
    return tile_at.astype(jnp.int32), slot_at.astype(jnp.int32), dest_of.astype(jnp.int32)


def sort_tiles(tile_at, adjacency, chunk=GROUP * GROUP_CHUNK):
    places = tile_at.shape[0]

    def kernel(at_ref, adj_ref, out_ref):
        step = pl.program_id(0)
        for u in range(chunk):
            t = at_ref[step * chunk + u]

            @pl.when(t >= 0)
            def _():
                out_ref[u] = adj_ref[jnp.maximum(t, 0)]

            @pl.when(t < 0)
            def _():
                out_ref[u] = jnp.zeros((BLK, BLK), BF16)

    return pl.pallas_call(
        kernel,
        name="sort_tiles",
        out_shape=pltpu.HBM((places, BLK, BLK), BF16),
        grid_spec=pltpu.PrefetchScalarGridSpec(
            num_scalar_prefetch=1,
            grid=(places // chunk,),
            in_specs=[whole(adjacency.shape)],
            out_specs=pl.BlockSpec((chunk, BLK, BLK), lambda i, *_: (i, 0, 0)),
        ),
        compiler_params=params(),
    )(tile_at, adjacency)


def tile_sums(slot_at, dest_of, sorted_tiles, msgs, root_term, ahead=2):
    places = sorted_tiles.shape[0]
    chunk = GROUP * GROUP_CHUNK
    steps = places // chunk

    def kernel(
        slot_ref, dest_ref, root_hbm, tile_hbm, msg_hbm, out_hbm,
        tile_ref, msg_ref, root_ref, out_ref, acc_ref, tile_sem, sem,
    ):
        load = pltpu.make_async_copy(msg_hbm, msg_ref, sem.at[0])
        load.start()
        copies = [
            pltpu.make_async_copy(
                tile_hbm.at[pl.ds(i * chunk, chunk)],
                tile_ref.at[pl.ds(i * chunk, chunk)],
                tile_sem.at[i],
            )
            for i in range(steps)
        ]
        for i in range(min(ahead, steps)):
            copies[i].start()
        root = pltpu.make_async_copy(root_hbm, root_ref, sem.at[1])
        acc_ref[...] = jnp.zeros_like(acc_ref)
        load.wait()
        for i in range(steps):
            if i + ahead < steps:
                copies[i + ahead].start()
            if i == min(1, steps - 1):
                root.start()
            copies[i].wait()
            for g in range(i * GROUP_CHUNK, (i + 1) * GROUP_CHUNK):
                at = range(g * GROUP, (g + 1) * GROUP)
                left = jnp.concatenate([tile_ref[p] for p in at], axis=1)
                right = jnp.concatenate([msg_ref[slot_ref[p]] for p in at], axis=0)
                acc_ref[dest_ref[g]] += jnp.dot(left, right, preferred_element_type=F32)
        root.wait()
        out_ref[...] = (acc_ref[...] + root_ref[...]).astype(BF16)
        store = pltpu.make_async_copy(out_ref, out_hbm, sem.at[2])
        store.start()
        store.wait()

    anywhere = pl.BlockSpec(memory_space=pl.ANY)
    return pl.pallas_call(
        kernel,
        name="tile_sums",
        out_shape=pltpu.HBM(root_term.shape, BF16),
        grid_spec=pltpu.PrefetchScalarGridSpec(
            num_scalar_prefetch=2,
            grid=(1,),
            in_specs=[anywhere, anywhere, anywhere],
            out_specs=anywhere,
            scratch_shapes=[
                pltpu.VMEM(sorted_tiles.shape, BF16),
                pltpu.VMEM(msgs.shape, BF16),
                pltpu.VMEM(root_term.shape, F32),
                pltpu.VMEM(root_term.shape, BF16),
                pltpu.VMEM(root_term.shape, F32),
                pltpu.SemaphoreType.DMA((steps,)),
                pltpu.SemaphoreType.DMA((3,)),
            ],
        ),
        compiler_params=params(),
    )(in_hbm(slot_at), in_hbm(dest_of), in_hbm(root_term), sorted_tiles, in_hbm(msgs))


def relation_of(ref, c):
    return jnp.max(ref[:, c * BLK : (c + 1) * BLK].astype(F32)).astype(jnp.int32)


def select_blocks(slot_block, returned, blocks, nblocks, capacity):
    shards, _, width = returned.shape
    relations = blocks.shape[0] // nblocks

    def kernel(block_ref, ret_ref, in_hbm_ref, out_ref, rel_ref, in_ref, load_ref, sem_ref):
        rows = pltpu.make_async_copy(
            ret_ref.at[:, pl.ds(capacity * BLK, 8), :], rel_ref, load_ref.at[relations]
        )
        rows.start()
        loads = []
        for r in range(relations):
            part = pl.ds(r * nblocks, nblocks)
            load = pltpu.make_async_copy(in_hbm_ref.at[part], in_ref.at[part], load_ref.at[r])
            load.start()
            loads.append(load)
        rows.wait()
        rels = [[relation_of(rel_ref[o], c) for c in range(capacity)] for o in range(shards)]

        def copy(o, c, r):
            return pltpu.make_async_copy(
                in_ref.at[r * nblocks + block_ref[c, o]],
                out_ref.at[o, pl.ds(c * BLK, BLK)],
                sem_ref.at[o, c],
            )

        for r in range(relations):
            loads[r].wait()
            for o in range(shards):
                for c in range(capacity):

                    @pl.when(rels[o][c] == r)
                    def _():
                        copy(o, c, r).start()

        for o in range(shards):
            for c in range(capacity):
                copy(o, c, 0).wait()

    return pl.pallas_call(
        kernel,
        name="select_blocks",
        out_shape=pltpu.HBM((shards, capacity * BLK, width), BF16),
        grid_spec=pltpu.PrefetchScalarGridSpec(
            num_scalar_prefetch=1,
            grid=(1,),
            in_specs=[
                pl.BlockSpec(memory_space=pl.ANY),
                pl.BlockSpec(memory_space=pl.ANY),
            ],
            out_specs=pl.BlockSpec(memory_space=pl.ANY),
            scratch_shapes=[
                pltpu.VMEM((shards, 8, width), BF16),
                pltpu.VMEM(blocks.shape, BF16),
                pltpu.SemaphoreType.DMA((relations + 1,)),
                pltpu.SemaphoreType.DMA((shards, capacity)),
            ],
        ),
        compiler_params=params(),
    )(in_hbm(slot_block), returned, in_hbm(blocks))


def sum_by_key(slot_block, returned, relations, nblocks, chunk=8):
    shards, rows, width = returned.shape
    capacity = slot_block.shape[0]
    bins = relations * nblocks

    def kernel(block_ref, ret_ref, out_ref, acc_ref):
        step = pl.program_id(0)

        @pl.when(step == 0)
        def _():
            acc_ref[...] = jnp.zeros_like(acc_ref)

        for u in range(chunk):
            for c in range(capacity):
                rel = relation_of(ret_ref[u, pl.ds(capacity * BLK, 8), :], c)
                key = rel * nblocks + block_ref[c, step * chunk + u]
                acc_ref[key] += ret_ref[u, pl.ds(c * BLK, BLK), :].astype(F32)

        @pl.when(step == pl.num_programs(0) - 1)
        def _():
            out_ref[...] = acc_ref[...].astype(BF16)

    return pl.pallas_call(
        kernel,
        name="sum_by_key",
        out_shape=pltpu.HBM((bins, BLK, width), BF16),
        grid_spec=pltpu.PrefetchScalarGridSpec(
            num_scalar_prefetch=1,
            grid=(shards // chunk,),
            in_specs=[pl.BlockSpec((chunk, rows, width), lambda i, *_: (i, 0, 0))],
            out_specs=whole((bins, BLK, width)),
            scratch_shapes=[pltpu.VMEM((bins, BLK, width), F32)],
        ),
        compiler_params=params(),
    )(slot_block, returned)


def weight_grads(coef, feats, source_grads, d_out, bases, chunk=128):
    relations, nodes, width = source_grads.shape
    nbase, width_in, _ = bases.shape

    def kernel(coef_ref, feat_ref, src_ref, grad_ref, base_ref, out_ref, dots_ref, acc_ref):
        @pl.when(pl.program_id(0) == 0)
        def _():
            acc_ref[...] = jnp.zeros_like(acc_ref)

        cols = feat_ref[...].T
        for r in range(relations):
            g = jnp.dot(cols, src_ref[r], preferred_element_type=F32)
            for b in range(nbase):
                scaled = coef_ref[r * nbase + b] * g
                if r == 0:
                    out_ref[b] = scaled
                else:
                    out_ref[b] += scaled
                prod = g * base_ref[b].astype(F32)
                acc_ref[r * nbase + b] += jnp.sum(prod.reshape(-1, 8, width), axis=0)
        out_ref[nbase] = jnp.dot(cols, grad_ref[...], preferred_element_type=F32)

        @pl.when(pl.program_id(0) == pl.num_programs(0) - 1)
        def _():
            row = lax.broadcasted_iota(jnp.int32, (8, BLK), 0)
            lane = lax.broadcasted_iota(jnp.int32, (8, BLK), 1)
            tile = jnp.zeros((8, BLK), F32)
            for r in range(relations):
                for b in range(nbase):
                    total = jnp.sum(acc_ref[r * nbase + b])
                    tile = jnp.where((row == b) & (lane == r), total, tile)
            dots_ref[...] = tile

    return pl.pallas_call(
        kernel,
        name="weight_grads",
        cost_estimate=pl.CostEstimate(
            flops=2 * (relations + 1) * nodes * width_in * width,
            transcendentals=0,
            bytes_accessed=2 * nodes * (width_in + (relations + 1) * width)
            + 6 * (nbase + 1) * width_in * width,
        ),
        out_shape=(
            jax.ShapeDtypeStruct((nbase + 1, width_in, width), F32),
            jax.ShapeDtypeStruct((8, BLK), F32),
        ),
        grid_spec=pltpu.PrefetchScalarGridSpec(
            num_scalar_prefetch=1,
            grid=(width_in // chunk,),
            in_specs=[
                pl.BlockSpec((nodes, chunk), lambda i, *_: (0, i)),
                whole(source_grads.shape),
                whole(d_out.shape),
                pl.BlockSpec((nbase, chunk, width), lambda i, *_: (0, i, 0)),
            ],
            out_specs=(
                pl.BlockSpec((nbase + 1, chunk, width), lambda i, *_: (0, i, 0)),
                whole((8, BLK)),
            ),
            scratch_shapes=[pltpu.VMEM((relations * nbase, 8, width), F32)],
        ),
        compiler_params=params(),
    )(coef, feats, source_grads, d_out, bases)


def exchange(x, axis, mask):
    return lax.ppermute(x, axis, [(i, i ^ mask) for i in range(lax.axis_size(axis))])


def chunk_of(x, at, dim):
    return lax.dynamic_index_in_dim(x, at, dim, keepdims=False)


def two_terms(x):
    high = x.astype(BF16)
    low = (x - high.astype(F32)).astype(BF16)
    return high, low


def sum_terms(x):
    return x[:, :BLK].astype(F32) + x[:, BLK:].astype(F32)


def first_stage(place, stacked, got, dots, size):
    parts, _, rest, _, rows, width = stacked.shape
    length = parts * rest * rows

    def kernel(place_ref, own_ref, got_ref, dots_ref, keep_ref, *send_refs):
        core = place_ref[0]
        at = place_ref[1]
        high, low = two_terms(dots_ref[...])
        for k in range(size):
            for p in range(parts):
                for q in range(rest):
                    value = own_ref[p, at ^ k, q, core] + got_ref[p, at ^ k, q].astype(F32)
                    if k == 0:
                        keep_ref[p, q] = value
                    else:
                        send_refs[k - 1][pl.ds((p * rest + q) * rows, rows), :] = value.astype(BF16)
            if k:
                send_refs[k - 1][pl.ds(length, 8), pl.ds(0, BLK)] = high
                send_refs[k - 1][pl.ds(length, 8), pl.ds(BLK, BLK)] = low

    sent = (length + 8, width)
    return pl.pallas_call(
        kernel,
        name="first_stage",
        out_shape=(jax.ShapeDtypeStruct((parts, rest, rows, width), F32),)
        + (jax.ShapeDtypeStruct(sent, BF16),) * (size - 1),
        grid_spec=pltpu.PrefetchScalarGridSpec(
            num_scalar_prefetch=1,
            grid=(1,),
            in_specs=[whole(stacked.shape), whole(got.shape), whole(dots.shape)],
            out_specs=(whole((parts, rest, rows, width)),) + (whole(sent),) * (size - 1),
        ),
        compiler_params=params(),
    )(place, stacked, got, dots)


def second_stage(place, kept, dots, got, size):
    parts, _, rows, width = kept.shape
    length = parts * rows

    def kernel(place_ref, own_ref, dots_ref, *refs):
        gots = refs[: len(got)]
        keep_ref, all_ref = refs[len(got) : len(got) + 2]
        send_refs = refs[len(got) + 2 :]
        at = place_ref[2]
        high, low = two_terms(dots_ref[...])
        sums = [high.astype(F32) + low.astype(F32)]
        sums += [sum_terms(g[pl.ds(length * size, 8), :]) for g in gots]
        while len(sums) > 1:
            sums = [sums[i] + sums[i + 1] for i in range(0, len(sums), 2)]
        all_ref[...] = sums[0]
        high, low = two_terms(sums[0])
        for k in range(size):
            for p in range(parts):
                value = own_ref[p, at ^ k]
                start = pl.multiple_of((p * size + (at ^ k)) * rows, 8)
                for g in gots:
                    value = value + g[pl.ds(start, rows), :].astype(F32)
                if k == 0:
                    keep_ref[p] = value
                else:
                    send_refs[k - 1][pl.ds(p * rows, rows), :] = value.astype(BF16)
            if k:
                send_refs[k - 1][pl.ds(length, 8), pl.ds(0, BLK)] = high
                send_refs[k - 1][pl.ds(length, 8), pl.ds(BLK, BLK)] = low

    sent = (length + 8, width)
    return pl.pallas_call(
        kernel,
        name="second_stage",
        out_shape=(
            jax.ShapeDtypeStruct((parts, rows, width), F32),
            jax.ShapeDtypeStruct((8, BLK), F32),
        )
        + (jax.ShapeDtypeStruct(sent, BF16),) * (size - 1),
        grid_spec=pltpu.PrefetchScalarGridSpec(
            num_scalar_prefetch=1,
            grid=(1,),
            in_specs=[whole(kept.shape), whole(dots.shape)] + [whole(g.shape) for g in got],
            out_specs=(whole((parts, rows, width)), whole((8, BLK))) + (whole(sent),) * (size - 1),
        ),
        compiler_params=params(),
    )(place, kept, dots, *got)


def last_stage(kept, dots, got, relations):
    parts, rows, width = kept.shape
    length = parts * rows
    nbase = parts - 1

    def kernel(own_ref, dots_ref, *refs):
        gots = refs[: len(got)]
        bases_ref, root_ref, coef_ref = refs[len(got) :]
        high, low = two_terms(dots_ref[...])
        sums = [high.astype(F32) + low.astype(F32)]
        sums += [sum_terms(g[pl.ds(length, 8), :]) for g in gots]
        while len(sums) > 1:
            sums = [sums[i] + sums[i + 1] for i in range(0, len(sums), 2)]
        coef_ref[...] = sums[0][:nbase, :relations]
        for p in range(parts):
            value = own_ref[p]
            for g in gots:
                value = value + g[pl.ds(p * rows, rows), :].astype(F32)
            if p < nbase:
                bases_ref[p] = value
            else:
                root_ref[...] = value

    shapes = ((nbase, rows, width), (rows, width), (nbase, relations))
    return pl.pallas_call(
        kernel,
        name="last_stage",
        out_shape=tuple(jax.ShapeDtypeStruct(x, F32) for x in shapes),
        grid=(1,),
        in_specs=[whole(kept.shape), whole(dots.shape)] + [whole(g.shape) for g in got],
        out_specs=tuple(whole(x) for x in shapes),
        compiler_params=params(),
    )(kept, dots, *got)


def body(
    feats, bases, coef, root_weight, slot_block, recv_rel, tile_slot, tile_dst, tile_adj, d_out
):
    shards = lax.axis_size("shard")
    reps = lax.axis_size("rep")
    me = lax.axis_index("shard")
    my_rep = lax.axis_index("rep")
    nblocks = feats.shape[0] // BLK
    width_in = feats.shape[1]
    width = root_weight.shape[1]
    relations, nbase = coef.shape
    capacity = slot_block.shape[2]
    slots = shards * capacity

    slot_grads = tile_grads(
        tile_slot[0],
        tile_dst[0],
        recv_rel[0].T,
        tile_adj[0],
        d_out.reshape(nblocks, BLK, width),
        shards,
    )
    returned = lax.all_to_all(slot_grads, "shard", 0, 0, tiled=True)

    rel_weights = (
        jnp.dot(coef, bases.reshape(nbase, -1), preferred_element_type=F32)
        .astype(BF16)
        .reshape(relations, width_in, width)
    )
    projected = project(feats, rel_weights, nblocks)
    root_term = jnp.dot(feats, root_weight, preferred_element_type=F32)

    tile_at, slot_at, dest_of = group_tables(tile_slot[0], tile_dst[0], nblocks)
    sorted_tiles = sort_tiles(tile_at, tile_adj[0])
    returned, sorted_tiles, slot_at, dest_of = lax.optimization_barrier(
        (returned, sorted_tiles, slot_at, dest_of)
    )
    requested = slot_block[0].T
    outgoing = select_blocks(requested, returned, projected, nblocks, capacity)
    outgoing, returned = lax.optimization_barrier((outgoing, returned))
    incoming = lax.all_to_all(outgoing, "shard", 0, 0, tiled=True)

    source_grads = sum_by_key(requested, returned, relations, nblocks)
    source_grads = source_grads.reshape(relations, nblocks * BLK, width)
    through = jnp.einsum("rno,rco->nc", source_grads, rel_weights, preferred_element_type=F32)
    through = through + jnp.dot(d_out, root_weight.T, preferred_element_type=F32)
    through = through.reshape(reps, -1, width_in)
    parts = [chunk_of(through, my_rep ^ k, 0).astype(BF16) for k in range(1, reps)]
    stacked, dots = weight_grads(
        coef.astype(F32).reshape(-1), feats, source_grads, d_out, bases
    )
    dots = dots + exchange(dots, "shard", 1)
    for step in (1, 2):
        dots = dots + exchange(dots, "rep", step)

    dots, *parts = lax.optimization_barrier((dots, *parts))
    grad_feats = chunk_of(through, my_rep, 0)
    for k, part in zip(range(1, reps), parts):
        grad_feats = grad_feats + exchange(part, "rep", k).astype(F32)
    grad_feats = grad_feats.astype(BF16)

    rows = width_in // shards
    stacked = stacked.reshape(nbase + 1, 4, 4, 2, rows, width)
    place = jnp.stack([me & 1, (me >> 3) & 3, (me >> 1) & 3]).astype(jnp.int32)
    got = exchange(chunk_of(stacked, (me & 1) ^ 1, 3).astype(BF16), "shard", 1)
    kept, *sends = first_stage(place, stacked, got, dots, 4)
    got = [exchange(x, "shard", k << 3) for k, x in zip((1, 2, 3), sends)]
    output = tile_sums(
        slot_at,
        dest_of,
        sorted_tiles,
        incoming.reshape(slots, BLK, width),
        root_term.reshape(nblocks, BLK, width),
    ).reshape(nblocks * BLK, width)
    output, grad_feats, kept = lax.optimization_barrier((output, grad_feats, kept))
    kept, dots, *sends = second_stage(place, kept, dots, got, 4)
    got = [exchange(x, "shard", k << 1) for k, x in zip((1, 2, 3), sends)]
    grad_bases, grad_root, grad_coef = last_stage(kept, dots, got, relations)
    return (output, grad_feats, grad_bases, grad_root, grad_coef.T)


def solution(mesh):
    placed = (
        P("shard", None),
        P(None, None, "rep"),
        P(),
        P(None, "rep"),
        P("shard", None, None),
        P("shard", None, None),
        P("shard", None),
        P("shard", None),
        P("shard", None, None, None),
        P("shard", "rep"),
    )
    return jax.shard_map(
        body,
        mesh=mesh,
        in_specs=placed,
        out_specs=(
            P("shard", "rep"),
            P(("shard", "rep"), None),
            P(None, "shard", "rep"),
            P("shard", "rep"),
            P(),
        ),
        check_vma=False,
    )
```

```python
import jax
import jax.numpy as jnp
from jax import lax
from jax.experimental import pallas as pl
from jax.experimental.pallas import tpu as pltpu
from jax.sharding import PartitionSpec as P

BLK = 128
F32 = jnp.float32
BF16 = jnp.bfloat16
VMEM_LIMIT = 48 * 1024 * 1024
GROUP = 4
GROUP_CHUNK = 12


def params():
    return pltpu.CompilerParams(vmem_limit_bytes=VMEM_LIMIT)


def in_hbm(x):
    return pltpu.with_memory_space_constraint(x, pltpu.HBM)


def whole(shape):
    return pl.BlockSpec(shape, lambda *_: (0,) * len(shape))


def tile_grads(tile_ids, dest_ids, rels, adjacency, grads, shards, chunk=64):
    tiles = adjacency.shape[0]
    nblocks, _, width = grads.shape
    capacity = rels.shape[0]
    slots = shards * capacity
    rows = capacity * BLK + 8

    def kernel(slot_ref, dst_ref, rel_ref, adj_ref, grad_ref, out_ref, acc_ref):
        step = pl.program_id(0)

        @pl.when(step == 0)
        def _():
            acc_ref[...] = jnp.zeros_like(acc_ref)

        for u in range(chunk):
            t = step * chunk + u
            part = lax.dot_general(
                adj_ref[u],
                grad_ref[dst_ref[t]],
                (((0,), (0,)), ((), ())),
                preferred_element_type=F32,
            )
            acc_ref[slot_ref[t]] += part

        @pl.when(step == pl.num_programs(0) - 1)
        def _():
            lane = lax.broadcasted_iota(jnp.int32, (8, width), 1)
            for o in range(shards):
                tail = jnp.zeros((8, width), F32)
                for c in range(capacity):
                    s = o * capacity + c
                    out_ref[o, pl.ds(c * BLK, BLK), :] = acc_ref[s].astype(BF16)
                    tail = jnp.where(lane // BLK == c, rel_ref[c, o].astype(F32), tail)
                out_ref[o, pl.ds(capacity * BLK, 8), :] = tail.astype(BF16)

    return pl.pallas_call(
        kernel,
        name="tile_grads",
        out_shape=pltpu.HBM((shards, rows, width), BF16),
        grid_spec=pltpu.PrefetchScalarGridSpec(
            num_scalar_prefetch=3,
            grid=(tiles // chunk,),
            in_specs=[
                pl.BlockSpec((chunk, BLK, BLK), lambda i, *_: (i, 0, 0)),
                whole(grads.shape),
            ],
            out_specs=whole((shards, rows, width)),
            scratch_shapes=[pltpu.VMEM((slots, BLK, width), F32)],
        ),
        compiler_params=params(),
    )(in_hbm(tile_ids), in_hbm(dest_ids), in_hbm(rels), adjacency, in_hbm(grads))


def project(feats, rel_weights, nblocks):
    relations, _, width = rel_weights.shape

    def kernel(feat_ref, w_ref, out_ref):
        for b in range(nblocks):
            out_ref[b] = jnp.dot(
                feat_ref[pl.ds(b * BLK, BLK), :], w_ref[0], preferred_element_type=F32
            ).astype(BF16)

    return pl.pallas_call(
        kernel,
        name="project",
        out_shape=pltpu.HBM((relations * nblocks, BLK, width), BF16),
        grid=(relations,),
        in_specs=[
            whole(feats.shape),
            pl.BlockSpec((1,) + rel_weights.shape[1:], lambda r: (r, 0, 0)),
        ],
        out_specs=pl.BlockSpec((nblocks, BLK, width), lambda r: (r, 0, 0)),
        compiler_params=params(),
    )(feats, rel_weights)


def group_tables(tile_ids, dest_ids, nblocks):
    tiles = tile_ids.shape[0]
    groups = -(-(tiles + nblocks * (GROUP - 1)) // GROUP)
    groups = -(-groups // GROUP_CHUNK) * GROUP_CHUNK
    index = jnp.arange(tiles)
    hot = (dest_ids[:, None] == jnp.arange(nblocks)[None, :]).astype(jnp.int32)
    sizes = (jnp.sum(hot, axis=0) + GROUP - 1) // GROUP
    blocks = jnp.arange(nblocks)
    ends = jnp.sum(jnp.where(blocks[:, None] <= blocks[None, :], sizes[:, None], 0), axis=0)
    same = dest_ids[:, None] == dest_ids[None, :]
    rank = jnp.sum((same & (index[None, :] < index[:, None])).astype(jnp.int32), axis=1)
    place = jnp.sum(hot * (ends - sizes)[None, :], axis=1) * GROUP + rank
    here = place[None, :] == jnp.arange(groups * GROUP)[:, None]
    tile_at = jnp.sum(jnp.where(here, index[None, :] + 1, 0), axis=1) - 1
    slot_at = jnp.sum(jnp.where(here, tile_ids[None, :], 0), axis=1)
    passed = (jnp.arange(groups)[:, None] >= ends[None, :]).astype(jnp.int32)
    dest_of = jnp.minimum(jnp.sum(passed, axis=1), nblocks - 1)
    return tile_at.astype(jnp.int32), slot_at.astype(jnp.int32), dest_of.astype(jnp.int32)


def sort_tiles(tile_at, adjacency, chunk=GROUP * GROUP_CHUNK):
    places = tile_at.shape[0]

    def kernel(at_ref, adj_ref, out_ref):
        step = pl.program_id(0)
        for u in range(chunk):
            t = at_ref[step * chunk + u]

            @pl.when(t >= 0)
            def _():
                out_ref[u] = adj_ref[jnp.maximum(t, 0)]

            @pl.when(t < 0)
            def _():
                out_ref[u] = jnp.zeros((BLK, BLK), BF16)

    return pl.pallas_call(
        kernel,
        name="sort_tiles",
        out_shape=pltpu.HBM((places, BLK, BLK), BF16),
        grid_spec=pltpu.PrefetchScalarGridSpec(
            num_scalar_prefetch=1,
            grid=(places // chunk,),
            in_specs=[whole(adjacency.shape)],
            out_specs=pl.BlockSpec((chunk, BLK, BLK), lambda i, *_: (i, 0, 0)),
        ),
        compiler_params=params(),
    )(tile_at, adjacency)


def tile_sums(slot_at, dest_of, sorted_tiles, msgs, root_term, ahead=2):
    places = sorted_tiles.shape[0]
    chunk = GROUP * GROUP_CHUNK
    steps = places // chunk

    def kernel(
        slot_ref, dest_ref, root_hbm, tile_hbm, msg_hbm, out_hbm,
        tile_ref, msg_ref, root_ref, out_ref, acc_ref, tile_sem, sem,
    ):
        load = pltpu.make_async_copy(msg_hbm, msg_ref, sem.at[0])
        load.start()
        copies = [
            pltpu.make_async_copy(
                tile_hbm.at[pl.ds(i * chunk, chunk)],
                tile_ref.at[pl.ds(i * chunk, chunk)],
                tile_sem.at[i],
            )
            for i in range(steps)
        ]
        for i in range(min(ahead, steps)):
            copies[i].start()
        root = pltpu.make_async_copy(root_hbm, root_ref, sem.at[1])
        acc_ref[...] = jnp.zeros_like(acc_ref)
        load.wait()
        for i in range(steps):
            if i + ahead < steps:
                copies[i + ahead].start()
            if i == min(1, steps - 1):
                root.start()
            copies[i].wait()
            for g in range(i * GROUP_CHUNK, (i + 1) * GROUP_CHUNK):
                at = range(g * GROUP, (g + 1) * GROUP)
                left = jnp.concatenate([tile_ref[p] for p in at], axis=1)
                right = jnp.concatenate([msg_ref[slot_ref[p]] for p in at], axis=0)
                acc_ref[dest_ref[g]] += jnp.dot(left, right, preferred_element_type=F32)
        root.wait()
        out_ref[...] = (acc_ref[...] + root_ref[...]).astype(BF16)
        store = pltpu.make_async_copy(out_ref, out_hbm, sem.at[2])
        store.start()
        store.wait()

    anywhere = pl.BlockSpec(memory_space=pl.ANY)
    return pl.pallas_call(
        kernel,
        name="tile_sums",
        out_shape=pltpu.HBM(root_term.shape, BF16),
        grid_spec=pltpu.PrefetchScalarGridSpec(
            num_scalar_prefetch=2,
            grid=(1,),
            in_specs=[anywhere, anywhere, anywhere],
            out_specs=anywhere,
            scratch_shapes=[
                pltpu.VMEM(sorted_tiles.shape, BF16),
                pltpu.VMEM(msgs.shape, BF16),
                pltpu.VMEM(root_term.shape, F32),
                pltpu.VMEM(root_term.shape, BF16),
                pltpu.VMEM(root_term.shape, F32),
                pltpu.SemaphoreType.DMA((steps,)),
                pltpu.SemaphoreType.DMA((3,)),
            ],
        ),
        compiler_params=params(),
    )(in_hbm(slot_at), in_hbm(dest_of), in_hbm(root_term), sorted_tiles, in_hbm(msgs))


def relation_of(ref, c):
    return jnp.max(ref[:, c * BLK : (c + 1) * BLK].astype(F32)).astype(jnp.int32)


def select_blocks(slot_block, returned, blocks, nblocks, capacity):
    shards, _, width = returned.shape
    relations = blocks.shape[0] // nblocks

    def kernel(block_ref, ret_ref, in_hbm_ref, out_ref, rel_ref, in_ref, load_ref, sem_ref):
        rows = pltpu.make_async_copy(
            ret_ref.at[:, pl.ds(capacity * BLK, 8), :], rel_ref, load_ref.at[relations]
        )
        rows.start()
        loads = []
        for r in range(relations):
            part = pl.ds(r * nblocks, nblocks)
            load = pltpu.make_async_copy(in_hbm_ref.at[part], in_ref.at[part], load_ref.at[r])
            load.start()
            loads.append(load)
        rows.wait()
        rels = [[relation_of(rel_ref[o], c) for c in range(capacity)] for o in range(shards)]

        def copy(o, c, r):
            return pltpu.make_async_copy(
                in_ref.at[r * nblocks + block_ref[c, o]],
                out_ref.at[o, pl.ds(c * BLK, BLK)],
                sem_ref.at[o, c],
            )

        for r in range(relations):
            loads[r].wait()
            for o in range(shards):
                for c in range(capacity):

                    @pl.when(rels[o][c] == r)
                    def _():
                        copy(o, c, r).start()

        for o in range(shards):
            for c in range(capacity):
                copy(o, c, 0).wait()

    return pl.pallas_call(
        kernel,
        name="select_blocks",
        out_shape=pltpu.HBM((shards, capacity * BLK, width), BF16),
        grid_spec=pltpu.PrefetchScalarGridSpec(
            num_scalar_prefetch=1,
            grid=(1,),
            in_specs=[
                pl.BlockSpec(memory_space=pl.ANY),
                pl.BlockSpec(memory_space=pl.ANY),
            ],
            out_specs=pl.BlockSpec(memory_space=pl.ANY),
            scratch_shapes=[
                pltpu.VMEM((shards, 8, width), BF16),
                pltpu.VMEM(blocks.shape, BF16),
                pltpu.SemaphoreType.DMA((relations + 1,)),
                pltpu.SemaphoreType.DMA((shards, capacity)),
            ],
        ),
        compiler_params=params(),
    )(in_hbm(slot_block), returned, in_hbm(blocks))


def sum_by_key(slot_block, returned, relations, nblocks, chunk=8):
    shards, rows, width = returned.shape
    capacity = slot_block.shape[0]
    bins = relations * nblocks

    def kernel(block_ref, ret_ref, out_ref, acc_ref):
        step = pl.program_id(0)

        @pl.when(step == 0)
        def _():
            acc_ref[...] = jnp.zeros_like(acc_ref)

        for u in range(chunk):
            for c in range(capacity):
                rel = relation_of(ret_ref[u, pl.ds(capacity * BLK, 8), :], c)
                key = rel * nblocks + block_ref[c, step * chunk + u]
                acc_ref[key] += ret_ref[u, pl.ds(c * BLK, BLK), :].astype(F32)

        @pl.when(step == pl.num_programs(0) - 1)
        def _():
            out_ref[...] = acc_ref[...].astype(BF16)

    return pl.pallas_call(
        kernel,
        name="sum_by_key",
        out_shape=pltpu.HBM((bins, BLK, width), BF16),
        grid_spec=pltpu.PrefetchScalarGridSpec(
            num_scalar_prefetch=1,
            grid=(shards // chunk,),
            in_specs=[pl.BlockSpec((chunk, rows, width), lambda i, *_: (i, 0, 0))],
            out_specs=whole((bins, BLK, width)),
            scratch_shapes=[pltpu.VMEM((bins, BLK, width), F32)],
        ),
        compiler_params=params(),
    )(slot_block, returned)


def weight_grads(coef, feats, source_grads, d_out, bases, chunk=128):
    relations, nodes, width = source_grads.shape
    nbase, width_in, _ = bases.shape

    def kernel(coef_ref, feat_ref, src_ref, grad_ref, base_ref, out_ref, dots_ref, acc_ref):
        @pl.when(pl.program_id(0) == 0)
        def _():
            acc_ref[...] = jnp.zeros_like(acc_ref)

        cols = feat_ref[...].T
        for r in range(relations):
            g = jnp.dot(cols, src_ref[r], preferred_element_type=F32)
            for b in range(nbase):
                scaled = coef_ref[r * nbase + b] * g
                if r == 0:
                    out_ref[b] = scaled
                else:
                    out_ref[b] += scaled
                prod = g * base_ref[b].astype(F32)
                acc_ref[r * nbase + b] += jnp.sum(prod.reshape(-1, 8, width), axis=0)
        out_ref[nbase] = jnp.dot(cols, grad_ref[...], preferred_element_type=F32)

        @pl.when(pl.program_id(0) == pl.num_programs(0) - 1)
        def _():
            row = lax.broadcasted_iota(jnp.int32, (8, BLK), 0)
            lane = lax.broadcasted_iota(jnp.int32, (8, BLK), 1)
            tile = jnp.zeros((8, BLK), F32)
            for r in range(relations):
                for b in range(nbase):
                    total = jnp.sum(acc_ref[r * nbase + b])
                    tile = jnp.where((row == b) & (lane == r), total, tile)
            dots_ref[...] = tile

    return pl.pallas_call(
        kernel,
        name="weight_grads",
        cost_estimate=pl.CostEstimate(
            flops=2 * (relations + 1) * nodes * width_in * width,
            transcendentals=0,
            bytes_accessed=2 * nodes * (width_in + (relations + 1) * width)
            + 6 * (nbase + 1) * width_in * width,
        ),
        out_shape=(
            jax.ShapeDtypeStruct((nbase + 1, width_in, width), F32),
            jax.ShapeDtypeStruct((8, BLK), F32),
        ),
        grid_spec=pltpu.PrefetchScalarGridSpec(
            num_scalar_prefetch=1,
            grid=(width_in // chunk,),
            in_specs=[
                pl.BlockSpec((nodes, chunk), lambda i, *_: (0, i)),
                whole(source_grads.shape),
                whole(d_out.shape),
                pl.BlockSpec((nbase, chunk, width), lambda i, *_: (0, i, 0)),
            ],
            out_specs=(
                pl.BlockSpec((nbase + 1, chunk, width), lambda i, *_: (0, i, 0)),
                whole((8, BLK)),
            ),
            scratch_shapes=[pltpu.VMEM((relations * nbase, 8, width), F32)],
        ),
        compiler_params=params(),
    )(coef, feats, source_grads, d_out, bases)


def exchange(x, axis, mask):
    return lax.ppermute(x, axis, [(i, i ^ mask) for i in range(lax.axis_size(axis))])


def chunk_of(x, at, dim):
    return lax.dynamic_index_in_dim(x, at, dim, keepdims=False)


def two_terms(x):
    high = x.astype(BF16)
    low = (x - high.astype(F32)).astype(BF16)
    return high, low


def sum_terms(x):
    return x[:, :BLK].astype(F32) + x[:, BLK:].astype(F32)


def first_stage(place, stacked, got, dots, size):
    parts, rest, _, _, rows, width = stacked.shape
    length = parts * rest * rows

    def kernel(place_ref, own_ref, got_ref, dots_ref, keep_ref, *send_refs):
        core = place_ref[0]
        at = place_ref[1]
        high, low = two_terms(dots_ref[...])
        for k in range(size):
            for p in range(parts):
                for q in range(rest):
                    value = own_ref[p, q, at ^ k, core] + got_ref[p, q, at ^ k].astype(F32)
                    if k == 0:
                        keep_ref[p, q] = value
                    else:
                        send_refs[k - 1][pl.ds((p * rest + q) * rows, rows), :] = value.astype(BF16)
            if k:
                send_refs[k - 1][pl.ds(length, 8), pl.ds(0, BLK)] = high
                send_refs[k - 1][pl.ds(length, 8), pl.ds(BLK, BLK)] = low

    sent = (length + 8, width)
    return pl.pallas_call(
        kernel,
        name="first_stage",
        out_shape=(jax.ShapeDtypeStruct((parts, rest, rows, width), F32),)
        + (jax.ShapeDtypeStruct(sent, BF16),) * (size - 1),
        grid_spec=pltpu.PrefetchScalarGridSpec(
            num_scalar_prefetch=1,
            grid=(1,),
            in_specs=[whole(stacked.shape), whole(got.shape), whole(dots.shape)],
            out_specs=(whole((parts, rest, rows, width)),) + (whole(sent),) * (size - 1),
        ),
        compiler_params=params(),
    )(place, stacked, got, dots)


def second_stage(place, kept, dots, got, size):
    parts, _, rows, width = kept.shape
    length = parts * rows

    def kernel(place_ref, own_ref, dots_ref, *refs):
        gots = refs[: len(got)]
        keep_ref, all_ref = refs[len(got) : len(got) + 2]
        send_refs = refs[len(got) + 2 :]
        at = place_ref[2]
        high, low = two_terms(dots_ref[...])
        sums = [high.astype(F32) + low.astype(F32)]
        sums += [sum_terms(g[pl.ds(length * size, 8), :]) for g in gots]
        while len(sums) > 1:
            sums = [sums[i] + sums[i + 1] for i in range(0, len(sums), 2)]
        all_ref[...] = sums[0]
        high, low = two_terms(sums[0])
        for k in range(size):
            for p in range(parts):
                value = own_ref[p, at ^ k]
                start = pl.multiple_of((p * size + (at ^ k)) * rows, 8)
                for g in gots:
                    value = value + g[pl.ds(start, rows), :].astype(F32)
                if k == 0:
                    keep_ref[p] = value
                else:
                    send_refs[k - 1][pl.ds(p * rows, rows), :] = value.astype(BF16)
            if k:
                send_refs[k - 1][pl.ds(length, 8), pl.ds(0, BLK)] = high
                send_refs[k - 1][pl.ds(length, 8), pl.ds(BLK, BLK)] = low

    sent = (length + 8, width)
    return pl.pallas_call(
        kernel,
        name="second_stage",
        out_shape=(
            jax.ShapeDtypeStruct((parts, rows, width), F32),
            jax.ShapeDtypeStruct((8, BLK), F32),
        )
        + (jax.ShapeDtypeStruct(sent, BF16),) * (size - 1),
        grid_spec=pltpu.PrefetchScalarGridSpec(
            num_scalar_prefetch=1,
            grid=(1,),
            in_specs=[whole(kept.shape), whole(dots.shape)] + [whole(g.shape) for g in got],
            out_specs=(whole((parts, rows, width)), whole((8, BLK))) + (whole(sent),) * (size - 1),
        ),
        compiler_params=params(),
    )(place, kept, dots, *got)


def last_stage(kept, dots, got, relations):
    parts, rows, width = kept.shape
    length = parts * rows
    nbase = parts - 1

    def kernel(own_ref, dots_ref, *refs):
        gots = refs[: len(got)]
        bases_ref, root_ref, coef_ref = refs[len(got) :]
        high, low = two_terms(dots_ref[...])
        sums = [high.astype(F32) + low.astype(F32)]
        sums += [sum_terms(g[pl.ds(length, 8), :]) for g in gots]
        while len(sums) > 1:
            sums = [sums[i] + sums[i + 1] for i in range(0, len(sums), 2)]
        coef_ref[...] = sums[0][:nbase, :relations]
        for p in range(parts):
            value = own_ref[p]
            for g in gots:
                value = value + g[pl.ds(p * rows, rows), :].astype(F32)
            if p < nbase:
                bases_ref[p] = value
            else:
                root_ref[...] = value

    shapes = ((nbase, rows, width), (rows, width), (nbase, relations))
    return pl.pallas_call(
        kernel,
        name="last_stage",
        out_shape=tuple(jax.ShapeDtypeStruct(x, F32) for x in shapes),
        grid=(1,),
        in_specs=[whole(kept.shape), whole(dots.shape)] + [whole(g.shape) for g in got],
        out_specs=tuple(whole(x) for x in shapes),
        compiler_params=params(),
    )(kept, dots, *got)


def body(
    feats, bases, coef, root_weight, slot_block, recv_rel, tile_slot, tile_dst, tile_adj, d_out
):
    shards = lax.axis_size("shard")
    reps = lax.axis_size("rep")
    me = lax.axis_index("shard")
    my_rep = lax.axis_index("rep")
    nblocks = feats.shape[0] // BLK
    width_in = feats.shape[1]
    width = root_weight.shape[1]
    relations, nbase = coef.shape
    capacity = slot_block.shape[2]
    slots = shards * capacity

    slot_grads = tile_grads(
        tile_slot[0],
        tile_dst[0],
        recv_rel[0].T,
        tile_adj[0],
        d_out.reshape(nblocks, BLK, width),
        shards,
    )
    returned = lax.all_to_all(slot_grads, "shard", 0, 0, tiled=True)

    rel_weights = (
        jnp.dot(coef, bases.reshape(nbase, -1), preferred_element_type=F32)
        .astype(BF16)
        .reshape(relations, width_in, width)
    )
    projected = project(feats, rel_weights, nblocks)
    root_term = jnp.dot(feats, root_weight, preferred_element_type=F32)

    tile_at, slot_at, dest_of = group_tables(tile_slot[0], tile_dst[0], nblocks)
    sorted_tiles = sort_tiles(tile_at, tile_adj[0])
    returned, sorted_tiles, slot_at, dest_of = lax.optimization_barrier(
        (returned, sorted_tiles, slot_at, dest_of)
    )
    requested = slot_block[0].T
    outgoing = select_blocks(requested, returned, projected, nblocks, capacity)
    outgoing, returned = lax.optimization_barrier((outgoing, returned))
    incoming = lax.all_to_all(outgoing, "shard", 0, 0, tiled=True)

    source_grads = sum_by_key(requested, returned, relations, nblocks)
    source_grads = source_grads.reshape(relations, nblocks * BLK, width)
    through = jnp.einsum("rno,rco->nc", source_grads, rel_weights, preferred_element_type=F32)
    through = through + jnp.dot(d_out, root_weight.T, preferred_element_type=F32)
    through = through.reshape(reps, -1, width_in)
    parts = [chunk_of(through, my_rep ^ k, 0).astype(BF16) for k in range(1, reps)]
    stacked, dots = weight_grads(
        coef.astype(F32).reshape(-1), feats, source_grads, d_out, bases
    )
    dots = dots + exchange(dots, "shard", 1)
    for step in (1, 2):
        dots = dots + exchange(dots, "rep", step)

    dots, *parts = lax.optimization_barrier((dots, *parts))
    grad_feats = chunk_of(through, my_rep, 0)
    for k, part in zip(range(1, reps), parts):
        grad_feats = grad_feats + exchange(part, "rep", k).astype(F32)
    grad_feats = grad_feats.astype(BF16)

    rows = width_in // shards
    stacked = stacked.reshape(nbase + 1, 4, 4, 2, rows, width)
    place = jnp.stack([me & 1, (me >> 1) & 3, (me >> 3) & 3]).astype(jnp.int32)
    got = exchange(chunk_of(stacked, (me & 1) ^ 1, 3).astype(BF16), "shard", 1)
    kept, *sends = first_stage(place, stacked, got, dots, 4)
    got = [exchange(x, "shard", k << 1) for k, x in zip((1, 2, 3), sends)]
    output = tile_sums(
        slot_at,
        dest_of,
        sorted_tiles,
        incoming.reshape(slots, BLK, width),
        root_term.reshape(nblocks, BLK, width),
    ).reshape(nblocks * BLK, width)
    output, grad_feats, kept = lax.optimization_barrier((output, grad_feats, kept))
    kept, dots, *sends = second_stage(place, kept, dots, got, 4)
    got = [exchange(x, "shard", k << 3) for k, x in zip((1, 2, 3), sends)]
    grad_bases, grad_root, grad_coef = last_stage(kept, dots, got, relations)
    return (output, grad_feats, grad_bases, grad_root, grad_coef.T)


def solution(mesh):
    placed = (
        P("shard", None),
        P(None, None, "rep"),
        P(),
        P(None, "rep"),
        P("shard", None, None),
        P("shard", None, None),
        P("shard", None),
        P("shard", None),
        P("shard", None, None, None),
        P("shard", "rep"),
    )
    return jax.shard_map(
        body,
        mesh=mesh,
        in_specs=placed,
        out_specs=(
            P("shard", "rep"),
            P(("shard", "rep"), None),
            P(None, "shard", "rep"),
            P("shard", "rep"),
            P(),
        ),
        check_vma=False,
    )
```
